32 devices in a mesh: dp: 8 (over z, x), tensor: 4 (over y, core).
Axes of the slice: x: 2, y: 2, z: 4, core: 2. Of those that a mesh axis runs over, the one named last changes fastest.
Arguments:
- inputs: bfloat16 [16, 1024, 1024], P('dp'), may hold values from -6 to 6
- segment_ids: int32 [16, 1024], P('dp'), may hold values from 0 to 7, never falling along the last dimension, each value on 1 to 512 neighbouring positions
- doc_offsets: int32 [16, 8], P('dp'), may hold values from 0 to 3071
- time_index: int32 [16], P('dp'), may hold values from 0 to 999
- w_qkv: bfloat16 [3, 1024, 1024], P(None, 'dp', 'tensor'), may hold values from -0.1875 to 0.1875
- w_out: bfloat16 [1024, 1024], P('tensor', 'dp'), may hold values from -0.75 to 0.75
- w_up: bfloat16 [1024, 4096], P('dp', 'tensor'), may hold values from -0.1875 to 0.1875
- w_down: bfloat16 [4096, 1024], P('tensor', 'dp'), may hold values from -0.09375 to 0.09375
- w_time: bfloat16 [256, 1024], P(None, 'dp'), may hold values from -0.375 to 0.375
- gain_attn: bfloat16 [1024], P('dp'), may hold values from 0.5 to 1.5
- gain_mlp: bfloat16 [1024], P('dp'), may hold values from 0.5 to 1.5
- cotangent: bfloat16 [16, 1024, 1024], P('dp'), may hold values from -6 to 6
Outputs:
- block_out: bfloat16 [16, 1024, 1024], P('dp', None, 'tensor')
- input_grad: float32 [16, 1024, 1024], P('dp', None, 'tensor')
- grad_qkv: float32 [3, 1024, 1024], P(None, 'dp', 'tensor')
- grad_out: float32 [1024, 1024], P('tensor', 'dp')
- grad_up: float32 [1024, 4096], P('dp', 'tensor')
- grad_down: float32 [4096, 1024], P('tensor', 'dp')
- grad_time: float32 [256, 1024], P(None, 'dp')
- grad_gain_attn: float32 [1024], P('dp')
- grad_gain_mlp: float32 [1024], P('dp')
The draws below stay inside these ranges and needn't reach their ends.
Inputs may be any that keep to these rules, and one draw needn't show every extreme that they name: `segment_ids`: in each sequence the ids never fall, every id of 0 to 7 occurs, each document has 1 to 512 tokens and one has exactly 512.
All inputs are finite; a program needn't handle non-finite values.
Results may differ from the reference program's by a relative error of at most 0.022.
Values may be sent and summed in bfloat16 or wider, within the bound.
No kernel may reach another device: no remote copies, remote signals or barrier semaphores. Data moves between devices by JAX's collectives and lax.ppermute only.
A program may use at most 192 MiB of HBM per device.

```python
import math
import jax
import jax.numpy as jnp
import numpy as np
from jax import lax

D = 1024
HEADS = 16
FF = 4096
TEMB = 256
SEQ = 1024
DOCS = 8
OFFSET_TOP = 3072
TIME_STEPS = 1000
SEQS = 16
N_TENSOR = 4


def touch_ends(array, stream_key, smallest, top_value):
    longest = array.shape.index(max(array.shape))
    spots = []
    for shift in (0, 1):
        where = [jax.random.randint(jax.random.fold_in(stream_key, axis), (), 0, length) for axis, length in enumerate(array.shape)]
        where[longest] = (where[longest] + shift) % array.shape[longest]
        spots.append(tuple(where))
    return array.at[spots[0]].set(smallest).at[spots[1]].set(top_value)


def steps_of(stream_key, shape, cuts, smallest, high):
    level = 1.0
    for position, parts in cuts:
        steps = jax.random.uniform(jax.random.fold_in(jax.random.fold_in(stream_key, 6), position), (parts,), jnp.float32, smallest / len(cuts), high / len(cuts))
        level = level * jnp.repeat(jnp.exp(steps), shape[position] // parts).reshape((-1,) + (1,) * (len(shape) - 1 - position))
    return level


def split_up(amount, total, reach, lean):
    loads = [(1 << 20) // math.isqrt(grade ** lean) + 1 for grade in range(2, amount + 1)]
    spare, holding = total - reach - (amount - 1), [1] * (amount - 1)
    while spare > 0:
        movable = [i for i in range(amount - 1) if holding[i] < reach]
        whole, left = sum([loads[i] for i in movable]), spare
        for i in movable:
            addition = min(reach - holding[i], max(1, left * loads[i] // whole), spare)
            holding[i] = holding[i] + addition
            spare = spare - addition
    return np.array([reach] + holding)


def ragged_sizes(rng, count, total, limit, skew):
    if count == 2:
        one = jax.random.randint(rng, (), max(1, total - limit), min(limit, total - 1) + 1)
        return jnp.stack([one, total - one])
    sizes = jnp.asarray(split_up(count, total, limit, skew), jnp.int32)
    pairs = (count - 1) // 2
    donor, receiver = sizes[1:1 + 2 * pairs:2], sizes[2:2 + 2 * pairs:2]
    margin = jnp.minimum(donor - 1, limit - receiver)
    shifted = jax.random.randint(jax.random.fold_in(rng, 1), (pairs,), 0, 1 << 20) % (margin + 1)
    sizes = sizes.at[1:1 + 2 * pairs:2].set(donor - shifted).at[2:2 + 2 * pairs:2].set(receiver + shifted)
    return sizes[jax.random.permutation(jax.random.fold_in(rng, 2), count)]


def gaussian(own_key, dims, scale, reach, pieces=(), held_as=jnp.bfloat16):
    values = scale * jax.random.normal(own_key, dims, jnp.float32)
    if pieces:
        values = values * steps_of(own_key, dims, pieces, -0.22, 0.18)
    return jnp.clip(values, -reach, reach).astype(held_as)


def setup_inputs(seed: int = 0) -> dict:
    splits = jax.random.split(jax.random.key(seed), 13)
    return {
        "inputs": gaussian(splits[0], (SEQS, SEQ, D), 1.0, 6.0, ((0, 8),)),
        "segment_ids": jax.vmap(lambda own: jnp.searchsorted(jnp.cumsum(ragged_sizes(own, DOCS, SEQ, SEQ // 2, 2)), jnp.arange(SEQ), side="right"))(jax.random.split(splits[1], SEQS)).reshape((SEQS, SEQ)).astype(jnp.int32),
        "doc_offsets": touch_ends(jax.random.randint(splits[2], (SEQS, DOCS), 0, OFFSET_TOP), jax.random.fold_in(splits[2], 1), 0, OFFSET_TOP - 1).astype(jnp.int32),
        "time_index": touch_ends(jax.random.randint(splits[3], (SEQS,), 0, TIME_STEPS), jax.random.fold_in(splits[3], 1), 0, TIME_STEPS - 1).astype(jnp.int32),
        "w_qkv": gaussian(splits[4], (3, D, D), D ** -0.5, 0.1875, ((1, 8), (2, 4))),
        "w_out": gaussian(splits[5], (D, D), (D // 16) ** -0.5, 0.75, ((0, 4), (1, 8))),
        "w_up": gaussian(splits[6], (D, FF), D ** -0.5, 0.1875, ((0, 8), (1, 4))),
        "w_down": gaussian(splits[7], (FF, D), FF ** -0.5, 0.09375, ((0, 4), (1, 8))),
        "w_time": gaussian(splits[8], (TEMB, D), TEMB ** -0.5, 0.375, ((1, 8),)),
        "gain_attn": jnp.clip(1.0 + 0.1 * jax.random.normal(splits[9], (D,), jnp.float32), 0.5, 1.5).astype(jnp.bfloat16),
        "gain_mlp": jnp.clip(1.0 + 0.1 * jax.random.normal(splits[10], (D,), jnp.float32), 0.5, 1.5).astype(jnp.bfloat16),
        "cotangent": gaussian(splits[11], (SEQS, SEQ, D), 1.0, 6.0, ((0, 8),)),
    }


@jax.custom_vjp
def low(v):
    return lax.optimization_barrier(v.astype(jnp.bfloat16)).astype(jnp.float32)

@jax.custom_vjp
def low_back(v):
    return v

def low_keep(v):
    return (low(v), None)

def low_pass(kept, grad):
    return (grad,)

def back_keep(v):
    return (v, None)

def back_low(kept, grad):
    return (low(grad),)
low.defvjp(low_keep, low_pass)
low_back.defvjp(back_keep, back_low)
eps = 1e-05
masked = -1000000000.0
highest = lax.Precision.HIGHEST

def sinusoid(values, width):
    half = width // 2
    freqs = jnp.exp(-math.log(10000.0) * jnp.arange(half, dtype=jnp.float32) / half)
    angles = values[..., None] * freqs
    return jnp.concatenate([jnp.sin(angles), jnp.cos(angles)], axis=-1)

def layer_norm(hidden, gain):
    centre = lax.optimization_barrier(jnp.mean(hidden, axis=-1, keepdims=True))
    centred = hidden - centre
    spread = lax.optimization_barrier(jnp.mean(centred * centred, axis=-1, keepdims=True))
    return centred * lax.rsqrt(spread + eps) * gain

def positions(segs, offsets):
    seq_len = segs.shape[0]
    index = jnp.arange(seq_len, dtype=jnp.int32)
    member = segs[:, None] == jnp.arange(offsets.shape[0], dtype=jnp.int32)[None, :]
    starts = lax.optimization_barrier(jnp.min(jnp.where(member, index[:, None], seq_len), axis=0)).astype(jnp.int32)
    start_tok = lax.optimization_barrier(jnp.sum(jnp.where(member, starts[None, :], 0), axis=1)).astype(jnp.int32)
    offset_tok = lax.optimization_barrier(jnp.sum(jnp.where(member, offsets[None, :], 0), axis=1)).astype(jnp.int32)
    return offset_tok + index - start_tok

def block(x, w_qkv, w_out, w_up, w_down, w_time, gain_attn, gain_mlp, embed, temb, same):
    seq_len = x.shape[0]
    head_size = D // HEADS
    h0 = x + embed + jnp.dot(temb, w_time, precision=highest)[None, :]
    n1 = low(layer_norm(h0, gain_attn))
    query = low_back(low(jnp.dot(n1, w_qkv[0], precision=highest))).reshape(seq_len, HEADS, head_size)
    key = low_back(low(jnp.dot(n1, w_qkv[1], precision=highest))).reshape(seq_len, HEADS, head_size)
    value = low_back(low(jnp.dot(n1, w_qkv[2], precision=highest))).reshape(seq_len, HEADS, head_size)
    scores = jnp.einsum('qhe,khe->hqk', query, key, precision=highest) * head_size ** (-0.5)
    scores = low_back(scores)
    scores = jnp.where(same[None], scores, masked)
    top = lax.optimization_barrier(jnp.max(scores, axis=-1, keepdims=True))
    expo = jnp.exp(scores - top)
    probs = expo / lax.optimization_barrier(jnp.sum(expo, axis=-1, keepdims=True))
    mixed = jnp.einsum('hqk,khe->qhe', low(probs), value, precision=highest).reshape(seq_len, D)
    mixed = low_back(low(mixed))
    groups = mixed.reshape(seq_len, N_TENSOR, D // N_TENSOR)
    terms = jnp.einsum('sgc,gcd->gsd', groups, w_out.reshape(N_TENSOR, D // N_TENSOR, D), precision=highest)
    attn = low_back(lax.optimization_barrier(jnp.sum(low(terms), axis=0)))
    h1 = h0 + attn
    n2 = low(layer_norm(h1, gain_mlp))
    hidden = low_back(jnp.dot(n2, w_up, precision=highest))
    active = low(jax.nn.gelu(hidden, approximate=False))
    active_groups = active.reshape(seq_len, N_TENSOR, FF // N_TENSOR)
    down_terms = jnp.einsum('sgf,gfd->gsd', active_groups, w_down.reshape(N_TENSOR, FF // N_TENSOR, D), precision=highest)
    return h1 + lax.optimization_barrier(jnp.sum(low(down_terms), axis=0))

def reference(inputs, segment_ids, doc_offsets, time_index, w_qkv, w_out, w_up, w_down, w_time, gain_attn, gain_mlp, cotangent):
    weights = (w_qkv.astype(jnp.float32), w_out.astype(jnp.float32), w_up.astype(jnp.float32), w_down.astype(jnp.float32), w_time.astype(jnp.float32), gain_attn.astype(jnp.float32), gain_mlp.astype(jnp.float32))

    def step(totals, items):
        x_seq, segs, offsets, time_now, cot = items
        embed = sinusoid(positions(segs, offsets).astype(jnp.float32), D)
        temb = sinusoid(time_now.astype(jnp.float32), TEMB)
        same = segs[:, None] == segs[None, :]

        def inner(x_in, a_w, b_w, c_w, d_w, e_w, f_w, g_w):
            return block(x_in, a_w, b_w, c_w, d_w, e_w, f_w, g_w, embed, temb, same)
        result, back = jax.vjp(inner, x_seq.astype(jnp.float32), weights[0], weights[1], weights[2], weights[3], weights[4], weights[5], weights[6])
        grads = back(cot.astype(jnp.float32))
        totals = tuple((total + grad for total, grad in zip(totals, grads[1:])))
        return (totals, (result.astype(jnp.bfloat16), grads[0]))
    zeros = tuple((jnp.zeros(w.shape, jnp.float32) for w in weights))
    totals, (block_out, input_grad) = lax.scan(step, zeros, (inputs, segment_ids, doc_offsets, time_index, cotangent))
    factor = float(SEQS * SEQ) ** (-0.5)
    return (block_out, input_grad, totals[0] * factor, totals[1] * factor, totals[2] * factor, totals[3] * factor, totals[4] * factor, totals[5] * factor, totals[6] * factor)
```

```python
import math

import jax
import jax.numpy as jnp
from jax import lax
from jax.sharding import PartitionSpec as P

HEADS = 16
TEMB = 256
eps = 1e-05
masked = -1000000000.0
f32 = jnp.float32
bf16 = jnp.bfloat16


def sinusoid(values, width):
    half = width // 2
    freqs = jnp.exp(-math.log(10000.0) * jnp.arange(half, dtype=f32) / half)
    angles = values[..., None] * freqs
    return jnp.concatenate([jnp.sin(angles), jnp.cos(angles)], axis=-1)


def norm_parts(hidden):
    centre = jnp.mean(hidden, axis=-1, keepdims=True)
    centred = hidden - centre
    spread = jnp.mean(centred * centred, axis=-1, keepdims=True)
    inv = lax.rsqrt(spread + eps)
    return centred * inv, inv


def norm_back(unit, inv, gain, grad):
    scaled = grad * gain
    first = jnp.mean(scaled, axis=-1, keepdims=True)
    second = jnp.mean(scaled * unit, axis=-1, keepdims=True)
    return inv * (scaled - first - unit * second)


def positions(segs, offsets):
    seq_len = segs.shape[0]
    index = jnp.arange(seq_len, dtype=jnp.int32)
    member = segs[:, None] == jnp.arange(offsets.shape[0], dtype=jnp.int32)[None, :]
    starts = jnp.min(jnp.where(member, index[:, None], seq_len), axis=0)
    start_tok = jnp.sum(jnp.where(member, starts[None, :], 0), axis=1)
    offset_tok = jnp.sum(jnp.where(member, offsets[None, :], 0), axis=1)
    return offset_tok + index - start_tok


def attend(query, key, value, same, scale):
    scores = jnp.einsum("qhe,khe->hqk", query, key, preferred_element_type=f32) * scale
    scores = jnp.where(same[None], scores, masked)
    top = jnp.max(scores, axis=-1, keepdims=True)
    expo = jnp.exp(scores - top)
    denom = jnp.sum(expo, axis=-1, keepdims=True)
    probs = (expo / denom).astype(bf16)
    out = jnp.einsum("hqk,khe->qhe", probs, value, preferred_element_type=f32)
    return out, top + jnp.log(denom)


def attend_back(query, key, value, same, scale, lse, d_mixed):
    scores = jnp.einsum("qhe,khe->hqk", query, key, preferred_element_type=f32) * scale
    scores = jnp.where(same[None], scores, masked)
    probs = jnp.exp(scores - lse)
    d_probs = jnp.einsum("qhe,khe->hqk", d_mixed, value, preferred_element_type=f32)
    d_value = jnp.einsum("hqk,qhe->khe", probs.astype(bf16), d_mixed, preferred_element_type=f32)
    delta = jnp.sum(probs * d_probs, axis=-1, keepdims=True)
    d_scores = (probs * (d_probs - delta)).astype(bf16)
    d_query = jnp.einsum("hqk,khe->qhe", d_scores, key, preferred_element_type=f32) * scale
    d_key = jnp.einsum("hqk,qhe->khe", d_scores, query, preferred_element_type=f32) * scale
    return d_query, d_key, d_value


def mm(left, right):
    return jnp.dot(left, right, preferred_element_type=f32)


def mm_rt(left, right):
    return jnp.einsum("ik,jk->ij", left, right, preferred_element_type=f32)


def mm_lt(left, right):
    return jnp.einsum("ki,kj->ij", left, right, preferred_element_type=f32)


class Ring:
    def __init__(self, n):
        self.n = n
        self.order = list(range(0, n, 2)) + list(range(n - 1, 0, -2))
        inverse = [self.order.index(i) for i in range(n)]
        self.me = lax.axis_index("dp")
        self.spot = jnp.array(inverse, jnp.int32)[self.me]
        self.table = jnp.array(self.order, jnp.int32)
        self.right = [(self.order[p], self.order[(p + 1) % n]) for p in range(n)]
        self.left = [(b, a) for a, b in self.right]

    def at(self, offset):
        return self.table[(self.spot + offset) % self.n]

    def gather(self, block):
        rows = block.shape[0]
        full = jnp.zeros((self.n * rows,) + block.shape[1:], block.dtype)
        full = lax.dynamic_update_slice_in_dim(full, block, self.me * rows, 0)
        from_left = from_right = block
        for hop in range(1, self.n // 2 + 1):
            from_left = lax.ppermute(from_left, "dp", self.right)
            if hop <= self.n - 1 - self.n // 2:
                from_right = lax.ppermute(from_right, "dp", self.left)
                full = lax.dynamic_update_slice_in_dim(full, from_right, self.at(hop) * rows, 0)
            full = lax.dynamic_update_slice_in_dim(full, from_left, self.at(-hop) * rows, 0)
        return full

    def scatter(self, full):
        rows = full.shape[0] // self.n

        def part(offset):
            return lax.dynamic_slice_in_dim(full, self.at(offset) * rows, rows, 0).astype(f32)

        total = part(0)
        for hops, way, sign in (
            (self.n // 2, self.right, 1),
            (self.n - 1 - self.n // 2, self.left, -1),
        ):
            run = part(sign * hops)
            for hop in range(1, hops + 1):
                run = lax.ppermute(run.astype(bf16), "dp", way).astype(f32)
                if hop < hops:
                    run = run + part(sign * (hops - hop))
            if hops:
                total = total + run
        return total


def swap(value, bit, n):
    return lax.ppermute(value, "tensor", [(i, i ^ bit) for i in range(n)])


def to_features(value, n):
    me = lax.axis_index("tensor")
    tokens, width = value.shape
    value = value.reshape(tokens, n, width // n)
    bit = 1
    while bit < n:
        value = value.reshape(tokens, -1, 2, width // n)
        mine = (me // bit) % 2
        keep = lax.dynamic_index_in_dim(value, mine, 2, keepdims=False)
        send = lax.dynamic_index_in_dim(value, 1 - mine, 2, keepdims=False)
        got = swap(send.astype(bf16), bit, n).astype(f32)
        if bit == 1:
            got = jnp.concatenate([got[tokens // 2 :], got[: tokens // 2]], axis=0)
        value = keep.astype(f32) + got
        bit *= 2
    return value.reshape(tokens, width // n)


def shards(
    inputs,
    segment_ids,
    doc_offsets,
    time_index,
    w_qkv,
    w_out,
    w_up,
    w_down,
    w_time,
    gain_attn,
    gain_mlp,
    cotangent,
):
    n_dp = lax.axis_size("dp")
    n_tensor = lax.axis_size("tensor")
    me_dp = lax.axis_index("dp")
    core = lax.axis_index("tensor") % 2
    chips = n_tensor // 2
    seqs_dev, seq_len, width = inputs.shape
    half = seq_len // 2
    shard = width // n_tensor
    head_size = width // HEADS
    heads_dev = shard // head_size
    scale = head_size ** (-0.5)
    hidden_dev = w_up.shape[1]
    ring = Ring(n_dp)

    w1_part = jnp.concatenate([w_qkv[0], w_qkv[1], w_qkv[2], w_out.T], axis=1)
    w1 = ring.gather(w1_part)
    w2_part = jnp.concatenate([w_up, w_down.T], axis=1)
    w2 = lax.all_gather(w2_part, "dp", axis=0, tiled=True)

    times = lax.all_gather(time_index, "dp", axis=0, tiled=True)
    temb = sinusoid(times.astype(f32), TEMB)
    cond_part = jnp.dot(temb, w_time.astype(f32), precision=lax.Precision.HIGHEST)
    small = jnp.concatenate(
        [cond_part, gain_attn.astype(f32)[None], gain_mlp.astype(f32)[None]], axis=0
    )
    small = lax.all_gather(small, "dp", axis=1, tiled=True)
    n_seqs = n_dp * seqs_dev
    cond = lax.dynamic_slice_in_dim(small, me_dp * seqs_dev, seqs_dev, 0)
    attn_g, mlp_g = small[n_seqs], small[n_seqs + 1]

    def own_first(value):
        return jnp.roll(value, -core * half, axis=0)

    def exchange_core(value):
        return swap(value, 1, n_tensor)

    def sum_chips(value):
        bit = 2
        value = value.astype(f32)
        while bit < n_tensor:
            low = value.astype(bf16)
            value = low.astype(f32) + swap(low, bit, n_tensor).astype(f32)
            bit *= 2
        return value

    seqs = range(seqs_dev)
    cot = [own_first(cotangent[i]) for i in seqs]
    segs = [own_first(segment_ids[i]) for i in seqs]
    same = [s[:, None] == s[None, :] for s in segs]
    h0, unit0, inv0, n1 = [], [], [], []
    for i in seqs:
        place = own_first(positions(segment_ids[i], doc_offsets[i]))
        h = own_first(inputs[i]).astype(f32) + sinusoid(place.astype(f32), width) + cond[i][None]
        unit, inv = norm_parts(h)
        h0.append(h)
        unit0.append(unit)
        inv0.append(inv)
        n1.append((unit * attn_g).astype(bf16))
    query, key, value, mixed, lse = [], [], [], [], []
    h1, unit1, inv1, n2 = [], [], [], []
    for i in seqs:
        qkv = mm(n1[i], w1[:, : 3 * shard]).astype(bf16)
        heads = [
            qkv[:, c * shard : (c + 1) * shard].reshape(seq_len, heads_dev, head_size)
            for c in range(3)
        ]
        out, total = attend(*heads, same[i], scale)
        out = out.reshape(seq_len, shard).astype(bf16)
        send = mm_rt(out[half:], w1[:, 3 * shard :]).astype(bf16)
        keep = mm_rt(out[:half], w1[:, 3 * shard :]).astype(bf16)
        attn = sum_chips(keep.astype(f32) + exchange_core(send).astype(f32))
        h = h0[i][:half] + attn
        unit, inv = norm_parts(h)
        own = (unit * mlp_g).astype(bf16)
        query.append(heads[0])
        key.append(heads[1])
        value.append(heads[2])
        mixed.append(out)
        lse.append(total)
        h1.append(h)
        unit1.append(unit)
        inv1.append(inv)
        n2.append(jnp.concatenate([own, exchange_core(own)], axis=0))
    w_up_full, w_down_t = w2[:, :hidden_dev], w2[:, hidden_dev:]
    active, d_hidden, d_h1, d_h1_low, block_out = [], [], [], [], []
    gain_mlp_sum = jnp.zeros((width,), f32)
    for i in seqs:
        hidden = mm(n2[i], w_up_full)
        d_active = mm(cot[i], w_down_t)
        erf = lax.erf(hidden * (0.5**0.5))
        cdf = 0.5 + 0.5 * erf
        active.append((hidden * cdf).astype(bf16))
        slope = cdf + hidden * jnp.exp(-0.5 * hidden * hidden) * (0.5 / math.pi) ** 0.5
        d_hidden.append((d_active * slope).astype(bf16))
        d_n2_send = mm_rt(d_hidden[i][half:], w_up_full).astype(bf16)
        d_n2_keep = mm_rt(d_hidden[i][:half], w_up_full).astype(bf16)
        d_n2 = sum_chips(d_n2_keep.astype(f32) + exchange_core(d_n2_send).astype(f32))
        gain_mlp_sum = gain_mlp_sum + jnp.sum(d_n2 * unit1[i], axis=0)
        d_h1.append(cot[i][:half].astype(f32) + norm_back(unit1[i], inv1[i], mlp_g, d_n2))
        low = d_h1[i].astype(bf16)
        d_h1_low.append(jnp.concatenate([low, exchange_core(low)], axis=0))
        term = mm_rt(active[i], w_down_t)
        term = jnp.concatenate([term[:half] + h1[i] * (1.0 / chips), term[half:]], axis=0)
        block_out.append(to_features(term.astype(bf16), n_tensor).astype(bf16))
    cot_all = jnp.concatenate(cot, axis=0)
    grad2 = jnp.concatenate(
        [
            mm_lt(jnp.concatenate(n2, axis=0), jnp.concatenate(d_hidden, axis=0)).astype(bf16),
            mm_lt(cot_all, jnp.concatenate(active, axis=0)).astype(bf16),
        ],
        axis=1,
    )
    share2 = lax.psum_scatter(grad2, "dp", scatter_dimension=0, tiled=True).astype(f32)
    d_qkv, input_grad, seq_sums = [], [], []
    gain_attn_sum = jnp.zeros((width,), f32)
    for i in seqs:
        d_mixed = mm(d_h1_low[i], w1[:, 3 * shard :]).astype(bf16)
        parts = attend_back(
            query[i],
            key[i],
            value[i],
            same[i],
            scale,
            lse[i],
            d_mixed.reshape(seq_len, heads_dev, head_size),
        )
        d_qkv.append(
            jnp.concatenate([p.reshape(seq_len, shard).astype(bf16) for p in parts], axis=1)
        )
        d_n1 = mm_rt(d_qkv[i], w1[:, : 3 * shard])
        gain_attn_sum = gain_attn_sum + jnp.sum(d_n1 * unit0[i], axis=0)
        term = norm_back(unit0[i], inv0[i], attn_g, d_n1)
        term = jnp.concatenate([term[:half] + d_h1[i] * (1.0 / chips), term[half:]], axis=0)
        seq_sums.append(jnp.sum(term, axis=0))
        input_grad.append(to_features(term.astype(bf16), n_tensor))
    grad1 = jnp.concatenate(
        [
            mm_lt(jnp.concatenate(n1, axis=0), jnp.concatenate(d_qkv, axis=0)).astype(bf16),
            mm_lt(jnp.concatenate(d_h1_low, axis=0), jnp.concatenate(mixed, axis=0)).astype(bf16),
        ],
        axis=1,
    )
    share1 = ring.scatter(grad1)
    sums = jnp.zeros((n_seqs, width), f32)
    sums = lax.dynamic_update_slice_in_dim(sums, jnp.stack(seq_sums), me_dp * seqs_dev, 0)
    sums = jnp.concatenate(
        [sums, gain_attn_sum[None], gain_mlp_sum[None] * (1.0 / chips)], axis=0
    )
    sums = lax.psum(sums, ("dp", "tensor"))
    rows = width // n_dp
    sums = lax.dynamic_slice_in_dim(sums, me_dp * rows, rows, 1)
    factor = float(n_seqs * seq_len) ** (-0.5)
    grad_time = (
        jnp.einsum("st,sd->td", temb, sums[:n_seqs], precision=lax.Precision.HIGHEST) * factor
    )

    def natural(value):
        return jnp.roll(value, core * half, axis=0)

    share1, share2 = share1 * factor, share2 * factor
    return (
        jnp.stack([natural(b) for b in block_out]),
        jnp.stack([natural(g) for g in input_grad]),
        jnp.stack([share1[:, c * shard : (c + 1) * shard] for c in range(3)]),
        share1[:, 3 * shard :].T,
        share2[:, :hidden_dev],
        share2[:, hidden_dev:].T,
        grad_time,
        sums[n_seqs] * factor,
        sums[n_seqs + 1] * factor,
    )


def solution(mesh):
    in_specs = (
        P("dp", None, None),
        P("dp", None),
        P("dp", None),
        P("dp"),
        P(None, "dp", "tensor"),
        P("tensor", "dp"),
        P("dp", "tensor"),
        P("tensor", "dp"),
        P(None, "dp"),
        P("dp"),
        P("dp"),
        P("dp", None, None),
    )
    out_specs = (
        P("dp", None, "tensor"),
        P("dp", None, "tensor"),
        P(None, "dp", "tensor"),
        P("tensor", "dp"),
        P("dp", "tensor"),
        P("tensor", "dp"),
        P(None, "dp"),
        P("dp"),
        P("dp"),
    )
    return jax.shard_map(shards, mesh=mesh, in_specs=in_specs, out_specs=out_specs, check_vma=False)
```

```python
import functools
import math

import jax
import jax.numpy as jnp
from jax import lax
from jax.experimental import pallas as pl
from jax.experimental.pallas import tpu as pltpu
from jax.sharding import PartitionSpec as P

HEADS = 16
TEMB = 256
BLOCK = 256
LANES = 128
eps = 1e-05
masked = -1000000000.0
f32 = jnp.float32
bf16 = jnp.bfloat16
VMEM = pl.BlockSpec(memory_space=pltpu.VMEM)
SMEM = pl.BlockSpec(memory_space=pltpu.SMEM)
params = pltpu.CompilerParams(vmem_limit_bytes=56 * 1024 * 1024)


def freqs(width):
    half = width // 2
    return jnp.exp(-math.log(10000.0) * jnp.arange(half, dtype=f32) / half)


def sinusoid(values, width):
    angles = values[..., None] * freqs(width)
    return jnp.concatenate([jnp.sin(angles), jnp.cos(angles)], axis=-1)


def norm_parts(hidden):
    centre = jnp.mean(hidden, axis=-1, keepdims=True)
    centred = hidden - centre
    spread = jnp.mean(centred * centred, axis=-1, keepdims=True)
    inv = lax.rsqrt(spread + eps)
    return centred * inv, inv


def norm_back(unit, inv, gain, grad):
    scaled = grad * gain
    first = jnp.mean(scaled, axis=-1, keepdims=True)
    second = jnp.mean(scaled * unit, axis=-1, keepdims=True)
    return inv * (scaled - first - unit * second)


def positions(segs, offsets):
    seq_len = segs.shape[0]
    index = jnp.arange(seq_len, dtype=jnp.int32)
    member = segs[:, None] == jnp.arange(offsets.shape[0], dtype=jnp.int32)[None, :]
    starts = jnp.min(jnp.where(member, index[:, None], seq_len), axis=0)
    start_tok = jnp.sum(jnp.where(member, starts[None, :], 0), axis=1)
    offset_tok = jnp.sum(jnp.where(member, offsets[None, :], 0), axis=1)
    return offset_tok + index - start_tok


def dot(left, right, left_dim, right_dim):
    return lax.dot_general(
        left, right, (((left_dim,), (right_dim,)), ((), ())), preferred_element_type=f32
    )


def like(shape, dtype):
    return jax.ShapeDtypeStruct(shape, dtype)


def rows_at(block):
    return pl.ds(pl.multiple_of(block * BLOCK, BLOCK), BLOCK)


def exchanged(core, block, blocks):
    return lax.rem(block + core * (blocks // 2), blocks)


def embed_kernel(meta, x, place, freq, out):
    half = freq.shape[1]
    angles = place[...].astype(f32) * freq[...]
    out[:, :half] = x[:, :half].astype(f32) + jnp.sin(angles)
    out[:, half:] = x[:, half:].astype(f32) + jnp.cos(angles)


def embedded(meta, x, place):
    seq_len, width = x.shape
    blocks = seq_len // BLOCK

    def source(i, m):
        return (exchanged(m[0], i, blocks), 0)

    return pl.pallas_call(
        embed_kernel,
        out_shape=like((seq_len, width), f32),
        grid_spec=pltpu.PrefetchScalarGridSpec(
            num_scalar_prefetch=1,
            grid=(blocks,),
            in_specs=[
                pl.BlockSpec((BLOCK, width), source),
                pl.BlockSpec((BLOCK, 1), source),
                pl.BlockSpec((1, width // 2), lambda i, m: (0, 0)),
            ],
            out_specs=pl.BlockSpec((BLOCK, width), lambda i, m: (i, 0)),
        ),
        compiler_params=params,
        name="embed",
    )(meta, x, place[:, None], freqs(width)[None])


def first_norm_kernel(x, cond, gain, h0, n1):
    h = x[...] + cond[...]
    unit, inv = norm_parts(h)
    h0[...] = h
    n1[...] = (unit * gain[...]).astype(bf16)


def first_norm(x, cond, gain):
    seq_len, width = x.shape
    row = pl.BlockSpec((BLOCK, width), lambda i: (i, 0))
    one = pl.BlockSpec((1, width), lambda i: (0, 0))
    return pl.pallas_call(
        first_norm_kernel,
        grid=(seq_len // BLOCK,),
        out_shape=(like(x.shape, f32), like(x.shape, bf16)),
        in_specs=[row, one, one],
        out_specs=(row, row),
        compiler_params=params,
        name="first_norm",
    )(x, cond, gain)


def window(meta, block, blocks):
    first, last = meta[1 + block], meta[1 + blocks + block]
    low, high = jnp.int32(blocks), jnp.int32(0)
    for j in range(blocks):
        hit = (meta[1 + blocks + j] >= first) & (meta[1 + j] <= last)
        low = jnp.where(hit & (low == blocks), j, low)
        high = jnp.where(hit, j + 1, high)
    return low, high - low


def set_bias(bias, seg_col, seg_row, block, low, count):
    keys = jnp.concatenate([seg_row[pl.ds(low + j, 1), :] for j in range(count)], axis=1)
    bias[:, : count * BLOCK] = jnp.where(seg_col[rows_at(block), :] == keys, 0.0, masked)


def attend_kernel(shard, scale, meta, n1, w1, seg_col, seg_row, qkv, a, lse, keep, send, bias):
    seq_len = n1.shape[0]
    blocks = seq_len // BLOCK
    half = seq_len // 2

    def project(block, _):
        terms = dot(n1[rows_at(block), :], w1[:, : 3 * shard], 1, 0)
        qkv[rows_at(exchanged(meta[0], block, blocks)), :] = terms.astype(bf16)
        return 0

    lax.fori_loop(0, blocks, project, 0)
    even = lax.broadcasted_iota(jnp.int32, (BLOCK, LANES), 1) < LANES // 2

    def attend(block, _):
        own = rows_at(exchanged(meta[0], block, blocks))
        low, count = window(meta, block, blocks)
        for size in range(1, blocks + 1):

            @pl.when(count == size)
            def _(size=size):
                span = size * BLOCK
                keys = pl.ds(pl.multiple_of(low * BLOCK, BLOCK), span)
                set_bias(bias, seg_col, seg_row, block, low, size)
                for pair in range(shard // LANES):
                    at = pair * LANES
                    query = qkv[rows_at(block), at : at + LANES] * jnp.bfloat16(scale)
                    key = qkv[keys, shard + at : shard + at + LANES]
                    value = qkv[keys, 2 * shard + at : 2 * shard + at + LANES]
                    outs = []
                    for e in range(2):
                        picked = jnp.where(even == (e == 0), query, jnp.bfloat16(0))
                        scores = dot(picked, key, 1, 1) + bias[:, :span]
                        top = jnp.max(scores, axis=1, keepdims=True)
                        expo = jnp.exp(scores - top)
                        denom = jnp.sum(expo, axis=1, keepdims=True)
                        outs.append(dot(expo.astype(bf16), value, 1, 0) * (1.0 / denom))
                        head = 2 * pair + e
                        lse[rows_at(block), head : head + 1] = top + jnp.log(denom)
                    a[own, at : at + LANES] = jnp.where(even, outs[0], outs[1]).astype(bf16)

        return 0

    lax.fori_loop(0, blocks, attend, 0)

    def project_out(block, _):
        w_out_t = w1[:, 3 * shard :]
        send[rows_at(block), :] = dot(a[rows_at(block + blocks // 2), :], w_out_t, 1, 1).astype(bf16)
        keep[rows_at(block), :] = dot(a[rows_at(block), :], w_out_t, 1, 1).astype(bf16)
        return 0

    lax.fori_loop(0, half // BLOCK, project_out, 0)


def attended(meta, n1, w1, seg_col, seg_row, shard, scale):
    seq_len, width = n1.shape
    return pl.pallas_call(
        functools.partial(attend_kernel, shard, scale),
        out_shape=(
            like((seq_len, 3 * shard), bf16),
            like((seq_len, shard), bf16),
            like((seq_len, LANES), f32),
            like((seq_len // 2, width), bf16),
            like((seq_len // 2, width), bf16),
        ),
        in_specs=[SMEM] + [VMEM] * 4,
        out_specs=(VMEM,) * 5,
        scratch_shapes=[pltpu.VMEM((BLOCK, seq_len), f32)],
        compiler_params=params,
        name="attend",
    )(meta, n1, w1, seg_col, seg_row)


def hidden_kernel(share, own, meta, n2, cot, w2, *refs):
    if own:
        h1, act, d_hid, d_n2, keep, send = refs
    else:
        act, d_hid, d_n2, keep, send = refs[-5:]
    hid = act.shape[1]
    chunk = min(512, hid)
    for at in range(0, hid, chunk):
        u = dot(n2[...], w2[:, at : at + chunk], 1, 0)
        d_act = dot(cot[...], w2[:, hid + at : hid + at + chunk], 1, 0)
        cdf = 0.5 + 0.5 * lax.erf(u * (0.5**0.5))
        act[:, at : at + chunk] = (u * cdf).astype(bf16)
        slope = cdf + u * (jnp.exp(-0.5 * u * u) * (0.5 / math.pi) ** 0.5)
        d_hid[:, at : at + chunk] = (d_act * slope).astype(bf16)
    d_n2[...] = dot(d_hid[...], w2[:, :hid], 1, 1).astype(bf16)
    term = dot(act[...], w2[:, hid:], 1, 1)
    if own:
        term = term + h1[...] * share
    split_features(meta[0], term.astype(bf16), keep, send)


def split_features(core, term, keep, send):
    groups, _, part = keep.shape
    for g in range(groups):
        first = term[:, 2 * g * part : (2 * g + 1) * part]
        second = term[:, (2 * g + 1) * part : (2 * g + 2) * part]
        keep[g] = jnp.where(core == 0, first, second)
        send[g] = jnp.where(core == 0, second, first)


def hidden_layer(meta, n2, cot, w2, h1, earlier, seq, seqs, share, groups):
    own = h1 is not None
    half, width = n2.shape
    hid = w2.shape[1] // 2
    per = half // BLOCK
    part = width // (2 * groups)
    base = (0 if own else per) + 2 * per * seq

    def cot_rows(i, m):
        return ((m[0] if own else 1 - m[0]) * per + i, 0)

    row = pl.BlockSpec((BLOCK, width), lambda i, m: (i, 0))
    placed = pl.BlockSpec((BLOCK, hid), lambda i, m: (base + i, 0))
    split = pl.BlockSpec((groups, BLOCK, part), lambda i, m: (0, (0 if own else per) + i, 0))
    ins = [n2, cot, w2]
    specs = [
        row,
        pl.BlockSpec((BLOCK, width), cot_rows),
        pl.BlockSpec(w2.shape, lambda i, m: (0, 0)),
    ]
    if own:
        ins.append(h1)
        specs.append(row)
    outs = {0: 0, 1: 1, 2: 3, 3: 4}
    aliases = {}
    for k, buffer in enumerate(earlier):
        aliases[1 + len(ins)] = outs[k]
        ins.append(buffer)
        specs.append(pl.BlockSpec(memory_space=pl.ANY))
    tokens = 2 * half
    return pl.pallas_call(
        functools.partial(hidden_kernel, share, own)
        if own and not earlier
        else functools.partial(hidden_skip, share, own, len(earlier)),
        out_shape=(
            like((seqs * tokens, hid), bf16),
            like((seqs * tokens, hid), bf16),
            like((half, width), bf16),
            like((groups, tokens, part), bf16),
            like((groups, tokens, part), bf16),
        ),
        grid_spec=pltpu.PrefetchScalarGridSpec(
            num_scalar_prefetch=1,
            grid=(per,),
            in_specs=specs,
            out_specs=(placed, placed, row, split, split),
        ),
        input_output_aliases=aliases,
        compiler_params=params,
        name="hidden_layer",
    )(meta, *ins)


def hidden_skip(share, own, count, meta, n2, cot, w2, *refs):
    if own:
        hidden_kernel(share, own, meta, n2, cot, w2, refs[0], *refs[1 + count :])
    else:
        hidden_kernel(share, own, meta, n2, cot, w2, *refs[count:])


def attend_back_kernel(
    shard,
    scale,
    meta,
    low_own,
    low_other,
    w1,
    qkv,
    a,
    lse,
    seg_col,
    seg_row,
    h0,
    d_h1,
    gain,
    d_qkv,
    keep,
    send,
    sums,
    d_mix,
    total,
    bias,
):
    seq_len = a.shape[0]
    blocks = seq_len // BLOCK
    per = blocks // 2

    def mix(block, _):
        w_out_t = w1[:, 3 * shard :]
        d_mix[rows_at(block), :] = dot(low_own[rows_at(block), :], w_out_t, 1, 0).astype(bf16)
        d_mix[rows_at(block + per), :] = dot(low_other[rows_at(block), :], w_out_t, 1, 0).astype(
            bf16
        )
        return 0

    lax.fori_loop(0, per, mix, 0)
    total[...] = jnp.zeros(total.shape, f32)
    even = lax.broadcasted_iota(jnp.int32, (BLOCK, LANES), 1) < LANES // 2

    def attend(block, _):
        own = rows_at(exchanged(meta[0], block, blocks))
        low, count = window(meta, block, blocks)
        for size in range(1, blocks + 1):

            @pl.when(count == size)
            def _(size=size):
                span = size * BLOCK
                keys = pl.ds(pl.multiple_of(low * BLOCK, BLOCK), span)
                set_bias(bias, seg_col, seg_row, block, low, size)
                for pair in range(shard // LANES):
                    at = pair * LANES
                    query = qkv[rows_at(block), at : at + LANES] * jnp.bfloat16(scale)
                    key = qkv[keys, shard + at : shard + at + LANES]
                    value = qkv[keys, 2 * shard + at : 2 * shard + at + LANES]
                    grad = d_mix[own, at : at + LANES]
                    product = grad.astype(f32) * a[own, at : at + LANES].astype(f32)
                    d_query = []
                    d_key = d_value = 0.0
                    for e in range(2):
                        side = even == (e == 0)
                        picked = jnp.where(side, query, jnp.bfloat16(0))
                        picked_grad = jnp.where(side, grad, jnp.bfloat16(0))
                        delta = jnp.sum(jnp.where(side, product, 0.0), axis=1, keepdims=True)
                        head = 2 * pair + e
                        scores = dot(picked, key, 1, 1) + bias[:, :span]
                        probs = jnp.exp(scores - lse[rows_at(block), head : head + 1])
                        d_probs = dot(picked_grad, value, 1, 1)
                        d_scores = (probs * (d_probs - delta)).astype(bf16)
                        d_query.append(dot(d_scores, key, 1, 0))
                        d_key = d_key + dot(d_scores, picked, 0, 0)
                        d_value = d_value + dot(probs.astype(bf16), picked_grad, 0, 0)
                    total[keys, at : at + LANES] += d_key
                    total[keys, shard + at : shard + at + LANES] += d_value
                    d_qkv[own, at : at + LANES] = (
                        jnp.where(even, d_query[0], d_query[1]) * scale
                    ).astype(bf16)

        return 0

    lax.fori_loop(0, blocks, attend, 0)
    share = 1.0 / keep.shape[0]
    sums[...] = jnp.zeros(sums.shape, f32)

    def back(block, _):
        rows = rows_at(block)
        d_qkv[rows, shard:] = total[rows_at(exchanged(meta[0], block, blocks)), :].astype(bf16)
        d_n1 = dot(d_qkv[rows, :], w1[:, : 3 * shard], 1, 1)
        unit, inv = norm_parts(h0[rows, :])
        sums[0:1, :] += jnp.sum(d_n1 * unit, axis=0, keepdims=True)
        term = norm_back(unit, inv, gain[...], d_n1)
        weight = jnp.where(block < per, share, 0.0)
        term = term + weight * d_h1[rows_at(lax.rem(block, per)), :]
        sums[1:2, :] += jnp.sum(term, axis=0, keepdims=True)
        split_features(meta[0], term.astype(bf16), keep.at[:, rows, :], send.at[:, rows, :])
        return 0

    lax.fori_loop(0, blocks, back, 0)


def attended_back(meta, low_own, low_other, w1, kept, seg_col, seg_row, h0, d_h1, gain, scale, groups):
    qkv, a, lse = kept
    seq_len, shard = a.shape
    width = w1.shape[0]
    part = width // (2 * groups)
    return pl.pallas_call(
        functools.partial(attend_back_kernel, shard, scale),
        out_shape=(
            like((seq_len, 3 * shard), bf16),
            like((groups, seq_len, part), bf16),
            like((groups, seq_len, part), bf16),
            like((8, width), f32),
        ),
        in_specs=[SMEM] + [VMEM] * 11,
        out_specs=(VMEM,) * 4,
        scratch_shapes=[
            pltpu.VMEM((seq_len, shard), bf16),
            pltpu.VMEM((seq_len, 2 * shard), f32),
            pltpu.VMEM((BLOCK, seq_len), f32),
        ],
        compiler_params=params,
        name="attend_back",
    )(meta, low_own, low_other, w1, qkv, a, lse, seg_col, seg_row, h0, d_h1, gain)


def mm_lt(left, right):
    return jnp.einsum("ki,kj->ij", left, right, preferred_element_type=f32)


class Ring:
    def __init__(self, n):
        self.n = n
        self.order = list(range(0, n, 2)) + list(range(n - 1, 0, -2))
        inverse = [self.order.index(i) for i in range(n)]
        self.me = lax.axis_index("dp")
        self.spot = jnp.array(inverse, jnp.int32)[self.me]
        self.table = jnp.array(self.order, jnp.int32)
        self.right = [(self.order[p], self.order[(p + 1) % n]) for p in range(n)]
        self.left = [(b, a) for a, b in self.right]

    def at(self, offset):
        return self.table[(self.spot + offset) % self.n]

    def gather(self, block):
        rows = block.shape[0]
        full = jnp.zeros((self.n * rows,) + block.shape[1:], block.dtype)
        full = lax.dynamic_update_slice_in_dim(full, block, self.me * rows, 0)
        from_left = from_right = block
        for hop in range(1, self.n // 2 + 1):
            from_left = lax.ppermute(from_left, "dp", self.right)
            if hop <= self.n - 1 - self.n // 2:
                from_right = lax.ppermute(from_right, "dp", self.left)
                full = lax.dynamic_update_slice_in_dim(full, from_right, self.at(hop) * rows, 0)
            full = lax.dynamic_update_slice_in_dim(full, from_left, self.at(-hop) * rows, 0)
        return full

    def scatter(self, full):
        rows = full.shape[0] // self.n

        def part(offset):
            return lax.dynamic_slice_in_dim(full, self.at(offset) * rows, rows, 0).astype(f32)

        total = part(0)
        for hops, way, sign in (
            (self.n // 2, self.right, 1),
            (self.n - 1 - self.n // 2, self.left, -1),
        ):
            run = part(sign * hops)
            for hop in range(1, hops + 1):
                run = lax.ppermute(run.astype(bf16), "dp", way).astype(f32)
                if hop < hops:
                    run = run + part(sign * (hops - hop))
            if hops:
                total = total + run
        return total


def swap(value, bit, n):
    return lax.ppermute(value, "tensor", [(i, i ^ bit) for i in range(n)])


def to_features(keep, send, n):
    chip = lax.axis_index("tensor") // 2
    half = keep.shape[1] // 2
    got = swap(send, 1, n)
    got = jnp.concatenate([got[:, half:], got[:, :half]], axis=1)
    value = keep.astype(f32) + got.astype(f32)
    bit = 1
    while 2 * bit < n:
        value = value.reshape((-1, 2) + value.shape[1:])
        mine = (chip // bit) % 2
        kept = lax.dynamic_index_in_dim(value, mine, 1, keepdims=False)
        sent = lax.dynamic_index_in_dim(value, 1 - mine, 1, keepdims=False)
        value = kept + swap(sent.astype(bf16), 2 * bit, n).astype(f32)
        bit *= 2
    return value[0]


def shards(
    inputs,
    segment_ids,
    doc_offsets,
    time_index,
    w_qkv,
    w_out,
    w_up,
    w_down,
    w_time,
    gain_attn,
    gain_mlp,
    cotangent,
):
    n_dp = lax.axis_size("dp")
    n_tensor = lax.axis_size("tensor")
    me_dp = lax.axis_index("dp")
    core = lax.axis_index("tensor") % 2
    chips = n_tensor // 2
    seqs_dev, seq_len, width = inputs.shape
    half = seq_len // 2
    blocks = seq_len // BLOCK
    shard = width // n_tensor
    scale = (width // HEADS) ** (-0.5)
    hidden_dev = w_up.shape[1]
    rows = width // n_dp
    n_seqs = n_dp * seqs_dev
    ring = Ring(n_dp)
    seqs = range(seqs_dev)

    marks = jnp.stack([time_index // 32, time_index % 32]).astype(bf16).reshape(1, -1)
    extra = jnp.concatenate(
        [
            gain_attn[:, None],
            gain_mlp[:, None],
            jnp.broadcast_to(marks, (rows, 2 * seqs_dev)),
            jnp.zeros((rows, LANES - 2 - 2 * seqs_dev), bf16),
        ],
        axis=1,
    )
    small = ring.gather(jnp.concatenate([w_time.T, extra], axis=1))
    w1 = ring.gather(jnp.concatenate([w_qkv[0], w_qkv[1], w_qkv[2], w_out.T], axis=1))
    w2 = lax.all_gather(jnp.concatenate([w_up, w_down.T], axis=1), "dp", axis=0, tiled=True)

    metas, seg_cols, seg_rows, entered = [], [], [], []
    for i in seqs:
        ids = segment_ids[i]
        metas.append(
            jnp.concatenate([core[None].astype(jnp.int32), ids[::BLOCK], ids[BLOCK - 1 :: BLOCK]])
        )
        seg_cols.append(ids[:, None])
        seg_rows.append(ids.reshape(blocks, BLOCK))
        entered.append(embedded(metas[i], inputs[i], positions(ids, doc_offsets[i])))
    temb = sinusoid(time_index.astype(f32), TEMB)
    cond = jnp.sum(temb[:, None, :] * small[None, :, :TEMB].astype(f32), axis=2)
    attn_g = small[:, TEMB].astype(f32)[None]
    mlp_g = small[:, TEMB + 1].astype(f32)[None]
    marks = small[::rows, TEMB + 2 : TEMB + 2 + 2 * seqs_dev].astype(f32)
    times = (marks[:, :seqs_dev] * 32 + marks[:, seqs_dev:]).reshape(n_seqs)

    def exchange_core(value):
        return swap(value, 1, n_tensor)

    def sum_chips(value):
        bit = 2
        while bit < n_tensor:
            low = value.astype(bf16)
            value = low.astype(f32) + swap(low, bit, n_tensor).astype(f32)
            bit *= 2
        return value

    h0, n1, kept, h1, unit1, inv1, n2 = [], [], [], [], [], [], []
    for i in seqs:
        h, n = first_norm(entered[i], cond[i : i + 1], attn_g)
        h0.append(h)
        n1.append(n)
    for i in seqs:
        qkv, a, lse, keep, send = attended(
            metas[i], n1[i], w1, seg_cols[i], seg_rows[i], shard, scale
        )
        kept.append((qkv, a, lse))
        attn = sum_chips(keep.astype(f32) + exchange_core(send).astype(f32))
        h = h0[i][:half] + attn
        unit, inv = norm_parts(h)
        own = (unit * mlp_g).astype(bf16)
        h1.append(h)
        unit1.append(unit)
        inv1.append(inv)
        n2.append((own, exchange_core(own)))
    share = 1.0 / chips
    buffers = ()
    d_h1, d_low, block_out = [], [], []
    gain_mlp_sum = jnp.zeros((1, width), f32)
    for i in seqs:
        act, d_hid, d_keep, keep, send = hidden_layer(
            metas[i], n2[i][0], cotangent[i], w2, h1[i], buffers, i, seqs_dev, share, chips
        )
        act, d_hid, d_send, keep, send = hidden_layer(
            metas[i],
            n2[i][1],
            cotangent[i],
            w2,
            None,
            (act, d_hid, keep, send),
            i,
            seqs_dev,
            share,
            chips,
        )
        buffers = (act, d_hid)
        d_n2 = sum_chips(d_keep.astype(f32) + exchange_core(d_send).astype(f32))
        gain_mlp_sum = gain_mlp_sum + jnp.sum(d_n2 * unit1[i], axis=0, keepdims=True)
        cot_own = lax.dynamic_slice_in_dim(cotangent[i], core * half, half, 0).astype(f32)
        d_h1.append(cot_own + norm_back(unit1[i], inv1[i], mlp_g, d_n2))
        low = d_h1[i].astype(bf16)
        d_low.append((low, exchange_core(low)))
        block_out.append(to_features(keep, send, n_tensor).astype(bf16))
    act, d_hid = buffers
    cot_all = jnp.concatenate([jnp.roll(cotangent[i], -core * half, axis=0) for i in seqs])
    grad2 = jnp.concatenate(
        [
            mm_lt(jnp.concatenate([x for pair in n2 for x in pair]), d_hid).astype(bf16),
            mm_lt(cot_all, act).astype(bf16),
        ],
        axis=1,
    )
    share2 = ring.scatter(grad2)
    d_qkv, input_grad, seq_sums = [], [], []
    gain_attn_sum = jnp.zeros((1, width), f32)
    for i in seqs:
        d, keep, send, sums = attended_back(
            metas[i],
            d_low[i][0],
            d_low[i][1],
            w1,
            kept[i],
            seg_cols[i],
            seg_rows[i],
            h0[i],
            d_h1[i],
            attn_g,
            scale,
            chips,
        )
        d_qkv.append(d)
        gain_attn_sum = gain_attn_sum + sums[0:1]
        seq_sums.append(sums[1:2])
        input_grad.append(to_features(keep, send, n_tensor))
    sums = jnp.zeros((LANES, width), f32)
    sums = lax.dynamic_update_slice_in_dim(sums, jnp.concatenate(seq_sums), me_dp * seqs_dev, 0)
    sums = lax.dynamic_update_slice_in_dim(
        sums, jnp.concatenate([gain_attn_sum, gain_mlp_sum * share]), n_seqs, 0
    )
    grad1 = jnp.concatenate(
        [
            mm_lt(jnp.concatenate(n1), jnp.concatenate(d_qkv)).astype(bf16),
            mm_lt(
                jnp.concatenate([x for pair in d_low for x in pair]),
                jnp.concatenate([k[1] for k in kept]),
            ).astype(bf16),
            sums.T.astype(bf16),
        ],
        axis=1,
    )
    share1 = ring.scatter(grad1)
    sums = share1[:, 4 * shard :]
    bit = 1
    while bit < n_tensor:
        sums = sums + swap(sums, bit, n_tensor)
        bit *= 2
    factor = float(n_seqs * seq_len) ** (-0.5)
    temb_all = sinusoid(times, TEMB)
    grad_time = (
        jnp.einsum("st,ds->td", temb_all, sums[:, :n_seqs], precision=lax.Precision.HIGHEST)
        * factor
    )

    def natural(value):
        return jnp.roll(value, core * half, axis=0)

    cols = 3 * shard
    return (
        jnp.stack([natural(b) for b in block_out]),
        jnp.stack([natural(g) for g in input_grad]),
        jnp.stack([share1[:, c * shard : (c + 1) * shard] for c in range(3)]) * factor,
        share1[:, cols : cols + shard].T * factor,
        share2[:, :hidden_dev] * factor,
        share2[:, hidden_dev:].T * factor,
        grad_time,
        sums[:, n_seqs] * factor,
        sums[:, n_seqs + 1] * factor,
    )


def solution(mesh):
    in_specs = (
        P("dp", None, None),
        P("dp", None),
        P("dp", None),
        P("dp"),
        P(None, "dp", "tensor"),
        P("tensor", "dp"),
        P("dp", "tensor"),
        P("tensor", "dp"),
        P(None, "dp"),
        P("dp"),
        P("dp"),
        P("dp", None, None),
    )
    out_specs = (
        P("dp", None, "tensor"),
        P("dp", None, "tensor"),
        P(None, "dp", "tensor"),
        P("tensor", "dp"),
        P("dp", "tensor"),
        P("tensor", "dp"),
        P(None, "dp"),
        P("dp"),
        P("dp"),
    )
    return jax.shard_map(shards, mesh=mesh, in_specs=in_specs, out_specs=out_specs, check_vma=False)
```

```python
import functools
import math

import jax
import jax.numpy as jnp
from jax import lax
from jax.experimental import pallas as pl
from jax.experimental.pallas import tpu as pltpu
from jax.sharding import PartitionSpec as P

HEADS = 16
TEMB = 256
BLOCK = 256
LANES = 128
FINE = 64
eps = 1e-05
masked = -1000000000.0
f32 = jnp.float32
bf16 = jnp.bfloat16
VMEM = pl.BlockSpec(memory_space=pltpu.VMEM)
SMEM = pl.BlockSpec(memory_space=pltpu.SMEM)
ANY = pl.BlockSpec(memory_space=pl.ANY)
HBM = pl.BlockSpec(memory_space=pltpu.HBM)


def params(mebibytes):
    return pltpu.CompilerParams(vmem_limit_bytes=mebibytes * 1024 * 1024)


def freqs(width):
    half = width // 2
    return jnp.exp(-math.log(10000.0) * jnp.arange(half, dtype=f32) / half)


def sinusoid(values, width):
    angles = values[..., None] * freqs(width)
    return jnp.concatenate([jnp.sin(angles), jnp.cos(angles)], axis=-1)


def norm_parts(hidden):
    centre = jnp.mean(hidden, axis=-1, keepdims=True)
    centred = hidden - centre
    spread = jnp.mean(centred * centred, axis=-1, keepdims=True)
    inv = lax.rsqrt(spread + eps)
    return centred * inv, inv


def norm_back(unit, inv, gain, grad):
    scaled = grad * gain
    first = jnp.mean(scaled, axis=-1, keepdims=True)
    second = jnp.mean(scaled * unit, axis=-1, keepdims=True)
    return inv * (scaled - first - unit * second)


def positions(segs, offsets):
    seq_len = segs.shape[0]
    index = jnp.arange(seq_len, dtype=jnp.int32)
    member = segs[:, None] == jnp.arange(offsets.shape[0], dtype=jnp.int32)[None, :]
    starts = jnp.min(jnp.where(member, index[:, None], seq_len), axis=0)
    start_tok = jnp.sum(jnp.where(member, starts[None, :], 0), axis=1)
    offset_tok = jnp.sum(jnp.where(member, offsets[None, :], 0), axis=1)
    return offset_tok + index - start_tok


def dot(left, right, left_dim, right_dim):
    return lax.dot_general(
        left, right, (((left_dim,), (right_dim,)), ((), ())), preferred_element_type=f32
    )


def like(shape, dtype):
    return jax.ShapeDtypeStruct(shape, dtype)


def rows_at(block):
    return pl.ds(pl.multiple_of(block * BLOCK, BLOCK), BLOCK)


def exchanged(core, block, blocks):
    return lax.rem(block + core * (blocks // 2), blocks)


def call(kernel, name, mebibytes, flops, outs, args, scratch=(), after=(), stored=(), direct=()):
    count, first, total = len(args), len(args) + len(after), len(outs)

    def body(*refs):
        results = list(refs[first : first + total])
        token = refs[first + total]
        rest = refs[first + total + 1 :]
        sems = rest[-1]
        copies = []

        def store(k, rows=slice(None)):
            mine = rest[stored.index(k)]
            copies.append(
                pltpu.make_async_copy(mine.at[rows], refs[first + k].at[rows], sems.at[len(copies)])
            )
            copies[-1].start()

        for at, k in enumerate(stored):
            results[k] = rest[at]
        extra = rest[len(stored) : -1]
        if stored:
            kernel(*refs[:count], *results, *extra, store=store)
        else:
            kernel(*refs[:count], *results, *extra)
        token[...] = jnp.zeros(token.shape, token.dtype)
        for copy in copies:
            copy.wait()

    moved = sum(a.size * a.dtype.itemsize for a in args) + sum(
        math.prod(o.shape) * o.dtype.itemsize for o in outs
    )
    return pl.pallas_call(
        body,
        out_shape=(
            *(
                pltpu.HBM(o.shape, o.dtype) if k in stored else o for k, o in enumerate(outs)
            ),
            like((8, LANES), f32),
        ),
        in_specs=[SMEM]
        + [HBM if k in direct else VMEM for k in range(1, count)]
        + [ANY] * len(after),
        out_specs=tuple(HBM if k in stored else VMEM for k in range(total)) + (VMEM,),
        scratch_shapes=[pltpu.VMEM(outs[k].shape, outs[k].dtype) for k in stored]
        + list(scratch)
        + [pltpu.SemaphoreType.DMA((8,))],
        compiler_params=params(mebibytes),
        cost_estimate=pl.CostEstimate(
            flops=flops // 1024, bytes_accessed=moved // 1024, transcendentals=0
        ),
        name=name,
    )(
        *(
            pltpu.with_memory_space_constraint(a, pltpu.HBM) if k in direct else a
            for k, a in enumerate(args)
        ),
        *after,
    )


def load(given, held, sems):
    copies = [
        pltpu.make_async_copy(ref, mine, sems.at[k])
        for k, (ref, mine) in enumerate(zip(given, held, strict=True))
    ]
    for copy in copies:
        copy.start()
    return lambda: copies.pop(0).wait()


def held_like(arrays):
    return [*(pltpu.VMEM(a.shape, a.dtype) for a in arrays), pltpu.SemaphoreType.DMA((len(arrays),))]


def pieces(table):
    first = table.astype(bf16)
    rest = table - first.astype(f32)
    second = rest.astype(bf16)
    return jnp.concatenate([first, second, (rest - second.astype(f32)).astype(bf16)], axis=0)


def embed_kernel(seqs, meta, inputs, place, freq, *refs, store):
    outs, held, sems = refs[:seqs], refs[seqs], refs[seqs + 1]
    copies = [pltpu.make_async_copy(inputs.at[i], held.at[i], sems.at[i]) for i in range(seqs)]
    for copy in copies:
        copy.start()
    seq_len = inputs.shape[1]
    half = freq.shape[1]
    blocks = seq_len // BLOCK
    step = lax.broadcasted_iota(jnp.int32, (FINE, half), 0).astype(f32)
    angles = (step * (FINE * freq[...]), step * freq[...])
    coarse, fine = (pieces(jnp.concatenate([jnp.sin(t), jnp.cos(t)], axis=1)) for t in angles)
    entry = lax.rem(lax.broadcasted_iota(jnp.int32, (BLOCK, 3 * FINE), 1), FINE)
    for i in range(seqs):

        def add(block, _, i=i):
            source = rows_at(exchanged(meta[0], block, blocks))
            at = place[i, source, :]
            a = dot((entry == at // FINE).astype(bf16), coarse, 1, 0)
            b = dot((entry == lax.rem(at, FINE)).astype(bf16), fine, 1, 0)
            sin_a, cos_a, sin_b, cos_b = a[:, :half], a[:, half:], b[:, :half], b[:, half:]
            x = held[i, source, :].astype(f32)
            outs[i][rows_at(block), :half] = x[:, :half] + (sin_a * cos_b + cos_a * sin_b)
            outs[i][rows_at(block), half:] = x[:, half:] + (cos_a * cos_b - sin_a * sin_b)
            return 0

        copies[i].wait()
        lax.fori_loop(0, blocks, add, 0)
        store(i)


def embedded(meta, inputs, place):
    seqs, seq_len, width = inputs.shape
    return call(
        functools.partial(embed_kernel, seqs),
        "embed",
        18,
        200 * inputs.size,
        (like((seq_len, width), f32),) * seqs,
        (meta, inputs, place[:, :, None], freqs(width)[None]),
        [pltpu.VMEM(inputs.shape, bf16), pltpu.SemaphoreType.DMA((seqs,))],
        stored=tuple(range(seqs)),
        direct=(1,),
    )


def window(meta, block, blocks):
    first, last = meta[2 + block], meta[2 + blocks + block]
    low, high = jnp.int32(blocks), jnp.int32(0)
    for j in range(blocks):
        hit = (meta[2 + blocks + j] >= first) & (meta[2 + j] <= last)
        low = jnp.where(hit & (low == blocks), j, low)
        high = jnp.where(hit, j + 1, high)
    return low, high - low


def set_bias(bias, seg_col, seg_row, block, low, count):
    keys = jnp.concatenate([seg_row[pl.ds(low + j, 1), :] for j in range(count)], axis=1)
    bias[:, : count * BLOCK] = jnp.where(seg_col[rows_at(block), :] == keys, 0.0, masked)


def project_kernel(shard, meta, entered, cond, gain, w1, h0, n1, qkv, inv, store):
    blocks = entered.shape[0] // BLOCK
    for block in range(blocks):
        rows = slice(block * BLOCK, (block + 1) * BLOCK)
        h = entered[rows, :] + cond[...]
        unit, scale = norm_parts(h)
        if block < blocks // 2:
            h0[rows, :] = h
        normed = (unit * gain[...]).astype(bf16)
        n1[rows, :] = normed
        inv[rows, LANES - 1 :] = scale
        terms = dot(normed, w1[:, : 3 * shard], 1, 0)
        qkv[rows_at(exchanged(meta[0], block, blocks)), :] = terms.astype(bf16)
        if block < blocks // 2:
            store(0, rows)
        store(1, rows)


def projected(meta, entered, cond, gain, w1, shard, after):
    seq_len, width = entered.shape
    return call(
        functools.partial(project_kernel, shard),
        "project",
        18,
        6 * seq_len * width * shard,
        (
            like((seq_len // 2, width), f32),
            like((seq_len, width), bf16),
            like((seq_len, 3 * shard), bf16),
            like((seq_len, LANES), f32),
        ),
        (meta, entered, cond, gain, w1),
        after=after,
        stored=(0, 1),
    )


def attend_kernel(shard, scale, meta, qkv, inv, seg_col, seg_row, a, lse, bias):
    seq_len = qkv.shape[0]
    blocks = seq_len // BLOCK
    lse[:, LANES - 1 :] = inv[:, LANES - 1 :]
    even = lax.broadcasted_iota(jnp.int32, (BLOCK, LANES), 1) < LANES // 2

    def attend(block, _):
        own = rows_at(exchanged(meta[0], block, blocks))
        low, count = window(meta, block, blocks)
        for size in range(1, blocks + 1):

            @pl.when(count == size)
            def _(size=size):
                span = size * BLOCK
                keys = pl.ds(pl.multiple_of(low * BLOCK, BLOCK), span)
                set_bias(bias, seg_col, seg_row, block, low, size)
                for pair in range(shard // LANES):
                    at = pair * LANES
                    query = qkv[rows_at(block), at : at + LANES] * jnp.bfloat16(scale)
                    key = qkv[keys, shard + at : shard + at + LANES]
                    value = qkv[keys, 2 * shard + at : 2 * shard + at + LANES]
                    outs = []
                    for e in range(2):
                        picked = jnp.where(even == (e == 0), query, jnp.bfloat16(0))
                        scores = dot(picked, key, 1, 1) + bias[:, :span]
                        top = jnp.max(scores, axis=1, keepdims=True)
                        expo = jnp.exp(scores - top)
                        denom = jnp.sum(expo, axis=1, keepdims=True)
                        outs.append(dot(expo.astype(bf16), value, 1, 0) * (1.0 / denom))
                        head = 2 * pair + e
                        lse[rows_at(block), head : head + 1] = top + jnp.log(denom)
                    a[own, at : at + LANES] = jnp.where(even, outs[0], outs[1]).astype(bf16)

        return 0

    lax.fori_loop(0, blocks, attend, 0)


def attended(meta, qkv, inv, seg_col, seg_row, shard, scale, after):
    seq_len = qkv.shape[0]
    return call(
        functools.partial(attend_kernel, shard, scale),
        "attend",
        10,
        8 * seq_len * seq_len * shard,
        (like((seq_len, shard), bf16), like((seq_len, LANES), f32)),
        (meta, qkv, inv, seg_col, seg_row),
        [pltpu.VMEM((BLOCK, seq_len), f32)],
        after,
    )


def out_kernel(meta, count, *refs):
    mixed, weights, keep, send = refs[:count], refs[count : 2 * count], refs[-2], refs[-1]
    half = keep.shape[0]
    for at in range(0, half, BLOCK):
        for base, out in ((half, send), (0, keep)):
            term = 0.0
            for a, w in zip(mixed, weights, strict=True):
                term = term + dot(a[base + at : base + at + BLOCK, :], w[...], 1, 1)
            out[at : at + BLOCK, :] = term.astype(out.dtype)


def projected_out(meta, mixed, weights, after):
    seq_len, shard = mixed[0].shape
    width = weights[0].shape[0]
    return call(
        lambda m, *refs: out_kernel(m, len(mixed), *refs),
        "project_out",
        7,
        2 * seq_len * width * shard * len(mixed),
        (like((seq_len // 2, width), bf16),) * 2,
        (meta, *mixed, *weights),
        after=after,
    )


def middle_kernel(meta, h0, keep, got, gain, h1, n2, store):
    for at in range(0, keep.shape[0], BLOCK):
        rows = slice(at, at + BLOCK)
        h = h0[rows, :] + (keep[rows, :].astype(f32) + got[rows, :].astype(f32))
        unit, _ = norm_parts(h)
        h1[rows, :] = h
        n2[rows, :] = (unit * gain[...]).astype(bf16)
    store(0)


def middle(meta, h0, keep, got, gain, after):
    return call(
        middle_kernel,
        "middle",
        10,
        20 * keep.size,
        (like(keep.shape, f32), like(keep.shape, bf16)),
        (meta, h0, keep, got, gain),
        after=after,
        stored=(0,),
    )


def split_features(core, term, keep, send):
    groups, _, part = keep.shape
    for g in range(groups):
        first = term[:, 2 * g * part : (2 * g + 1) * part]
        second = term[:, (2 * g + 1) * part : (2 * g + 2) * part]
        keep[g] = jnp.where(core == 0, first, second)
        send[g] = jnp.where(core == 0, second, first)


def hidden_kernel(
    meta, n2_own, n2_other, cot, w2, h1, d_keep, d_send, grad, keep, send, act, d_hid
):
    hid = w2.shape[1] // 2
    half, width = n2_own.shape
    chips = keep.shape[0]
    chunk = min(512, hid)
    own = pl.multiple_of(meta[0] * half, BLOCK)
    other = pl.multiple_of((1 - meta[0]) * half, BLOCK)
    for first, base, n2, d_n2 in ((half, other, n2_other, d_send), (0, own, n2_own, d_keep)):
        for at in range(0, half, BLOCK):
            rows = slice(at, at + BLOCK)
            mine = slice(first + at, first + at + BLOCK)
            d_out = cot[pl.ds(base + at, BLOCK), :]
            for col in range(0, hid, chunk):
                u = dot(n2[rows, :], w2[:, col : col + chunk], 1, 0)
                d_act = dot(d_out, w2[:, hid + col : hid + col + chunk], 1, 0)
                cdf = 0.5 + 0.5 * lax.erf(u * (0.5**0.5))
                act[mine, col : col + chunk] = (u * cdf).astype(bf16)
                slope = cdf + u * (jnp.exp(-0.5 * u * u) * (0.5 / math.pi) ** 0.5)
                d_hid[mine, col : col + chunk] = (d_act * slope).astype(bf16)
            d_n2[rows, :] = dot(d_hid[mine, :], w2[:, :hid], 1, 1).astype(bf16)
            term = dot(act[mine, :], w2[:, hid:], 1, 1)
            if first == 0:
                term = term + h1[rows, :] * (1.0 / chips)
            split_features(
                meta[0], term.astype(bf16), keep.at[:, mine, :], send.at[:, mine, :]
            )
    for at in range(0, width, BLOCK):
        cols = slice(at, at + BLOCK)
        up = dot(n2_own[:, cols], d_hid[:half, :], 0, 0)
        up = up + dot(n2_other[:, cols], d_hid[half:, :], 0, 0)
        grad[cols, :hid] = up.astype(bf16)
        down = dot(cot[pl.ds(own, half), cols], act[:half, :], 0, 0)
        down = down + dot(cot[pl.ds(other, half), cols], act[half:, :], 0, 0)
        grad[cols, hid:] = down.astype(bf16)


def hidden_layer(meta, n2, cot, w2, h1, chips, after):
    half, width = n2[0].shape
    hid = w2.shape[1] // 2
    split = like((chips, 2 * half, width // (2 * chips)), bf16)
    d_n2 = like((half, width), bf16)
    return call(
        hidden_kernel,
        "hidden_layer",
        25,
        24 * half * width * hid,
        (d_n2, d_n2, like((width, 2 * hid), bf16), split, split),
        (meta, *n2, cot, w2, h1),
        [pltpu.VMEM((2 * half, hid), bf16)] * 2,
        after,
    )


def middle_back_kernel(meta, low, got, h1, cot, gain, d_low, sums):
    half = h1.shape[0]
    base = pl.multiple_of(meta[0] * half, BLOCK)
    total = jnp.zeros(sums.shape, f32)
    for at in range(0, half, BLOCK):
        rows = slice(at, at + BLOCK)
        d_n2 = low[rows, :].astype(f32) + got[rows, :].astype(f32)
        unit, inv = norm_parts(h1[rows, :])
        total = total + jnp.sum(d_n2 * unit, axis=0, keepdims=True)
        d_h = cot[pl.ds(base + at, BLOCK), :].astype(f32) + norm_back(unit, inv, gain[...], d_n2)
        d_low[rows, :] = d_h.astype(bf16)
    sums[...] = total


def middle_back(meta, low, got, h1, cot, gain, after):
    return call(
        middle_back_kernel,
        "middle_back",
        10,
        30 * h1.size,
        (like(h1.shape, bf16), like((1, h1.shape[1]), f32)),
        (meta, low, got, h1, cot, gain),
        after=after,
    )


def attend_back_kernel(
    shard,
    scale,
    meta,
    low_own,
    low_other,
    w1,
    qkv,
    a,
    lse,
    seg_col,
    seg_row,
    n1,
    gain,
    grads,
    keep,
    send,
    sums,
    d_mix,
    total,
    bias,
    d_qkv,
):
    seq_len = a.shape[0]
    blocks = seq_len // BLOCK
    per = blocks // 2
    for block in range(per):
        w_out_t = w1[:, 3 * shard : 4 * shard]
        rows = slice(block * BLOCK, (block + 1) * BLOCK)
        d_mix[rows, :] = dot(low_own[rows, :], w_out_t, 1, 0).astype(bf16)
        after = slice((block + per) * BLOCK, (block + per + 1) * BLOCK)
        d_mix[after, :] = dot(low_other[rows, :], w_out_t, 1, 0).astype(bf16)
    total[...] = jnp.zeros(total.shape, f32)
    even = lax.broadcasted_iota(jnp.int32, (BLOCK, LANES), 1) < LANES // 2

    def attend(block, _):
        own = rows_at(exchanged(meta[0], block, blocks))
        low, count = window(meta, block, blocks)
        for size in range(1, blocks + 1):

            @pl.when(count == size)
            def _(size=size):
                span = size * BLOCK
                keys = pl.ds(pl.multiple_of(low * BLOCK, BLOCK), span)
                set_bias(bias, seg_col, seg_row, block, low, size)
                for pair in range(shard // LANES):
                    at = pair * LANES
                    query = qkv[rows_at(block), at : at + LANES] * jnp.bfloat16(scale)
                    key = qkv[keys, shard + at : shard + at + LANES]
                    value = qkv[keys, 2 * shard + at : 2 * shard + at + LANES]
                    grad = d_mix[own, at : at + LANES]
                    product = grad.astype(f32) * a[own, at : at + LANES].astype(f32)
                    d_query = []
                    d_key = d_value = 0.0
                    for e in range(2):
                        side = even == (e == 0)
                        picked = jnp.where(side, query, jnp.bfloat16(0))
                        picked_grad = jnp.where(side, grad, jnp.bfloat16(0))
                        delta = jnp.sum(jnp.where(side, product, 0.0), axis=1, keepdims=True)
                        head = 2 * pair + e
                        scores = dot(picked, key, 1, 1) + bias[:, :span]
                        probs = jnp.exp(scores - lse[rows_at(block), head : head + 1])
                        d_probs = dot(picked_grad, value, 1, 1)
                        d_scores = (probs * (d_probs - delta)).astype(bf16)
                        d_query.append(dot(d_scores, key, 1, 0))
                        d_key = d_key + dot(d_scores, picked, 0, 0)
                        d_value = d_value + dot(probs.astype(bf16), picked_grad, 0, 0)
                    total[keys, at : at + LANES] += d_key
                    total[keys, shard + at : shard + at + LANES] += d_value
                    d_qkv[own, at : at + LANES] = (
                        jnp.where(even, d_query[0], d_query[1]) * scale
                    ).astype(bf16)

        return 0

    lax.fori_loop(0, blocks, attend, 0)
    share = 1.0 / keep.shape[0]
    unit_sum = term_sum = jnp.zeros((1, n1.shape[1]), f32)
    ungain = 1.0 / gain[...]
    for block in range(blocks):
        rows = slice(block * BLOCK, (block + 1) * BLOCK)
        d_qkv[rows, shard:] = total[rows_at(exchanged(meta[0], block, blocks)), :].astype(bf16)
        d_n1 = dot(d_qkv[rows, :], w1[:, : 3 * shard], 1, 1)
        unit = n1[rows, :].astype(f32) * ungain
        inv = lse[rows, LANES - 1 :]
        unit_sum = unit_sum + jnp.sum(d_n1 * unit, axis=0, keepdims=True)
        term = norm_back(unit, inv, gain[...], d_n1)
        if block < per:
            term = term + share * low_own[rows, :].astype(f32)
        term_sum = term_sum + jnp.sum(term, axis=0, keepdims=True)
        split_features(meta[0], term.astype(bf16), keep.at[:, rows, :], send.at[:, rows, :])
    sums[0:1, :] = unit_sum
    sums[1:2, :] = term_sum
    half = low_own.shape[0]
    for at in range(0, n1.shape[1], BLOCK):
        cols = slice(at, at + BLOCK)
        grads[cols, : 3 * shard] = dot(n1[:, cols], d_qkv[...], 0, 0).astype(bf16)
        proj = dot(low_own[:, cols], a[:half, :], 0, 0)
        proj = proj + dot(low_other[:, cols], a[half:, :], 0, 0)
        grads[cols, 3 * shard :] = proj.astype(bf16)


def attended_back(meta, low_own, low_other, w1, kept, seg_col, seg_row, n1, gain, scale, groups, after):
    qkv, a, lse = kept
    seq_len, shard = a.shape
    width = w1.shape[0]
    split = like((groups, seq_len, width // (2 * groups)), bf16)
    return call(
        functools.partial(attend_back_kernel, shard, scale),
        "attend_back",
        24,
        16 * seq_len * width * shard + 20 * seq_len * seq_len * shard,
        (like((width, 4 * shard), bf16), split, split, like((2, width), f32)),
        (meta, low_own, low_other, w1, qkv, a, lse, seg_col, seg_row, n1, gain),
        [
            pltpu.VMEM((seq_len, shard), bf16),
            pltpu.VMEM((seq_len, 2 * shard), f32),
            pltpu.VMEM((BLOCK, seq_len), f32),
            pltpu.VMEM((seq_len, 3 * shard), bf16),
        ],
        after,
    )


def assemble_kernel(spots, *refs):
    come, full, sems = refs[:-2], refs[-2], refs[-1]
    copies = []
    for k, ref in enumerate(come):
        rows = ref.shape[0]
        at = pl.ds(pl.multiple_of(spots[k], rows), rows)
        copies.append(pltpu.make_async_copy(ref, full.at[at, :], sems.at[k]))
    for copy in copies:
        copy.start()
    for copy in copies:
        copy.wait()


def assembled(spots, come):
    rows, cols = sum(c.shape[0] for c in come), come[0].shape[1]
    return pl.pallas_call(
        assemble_kernel,
        out_shape=like((rows, cols), come[0].dtype),
        in_specs=[SMEM] + [HBM] * len(come),
        out_specs=ANY,
        scratch_shapes=[pltpu.SemaphoreType.DMA((len(come),))],
        compiler_params=params(2),
        cost_estimate=pl.CostEstimate(
            flops=0, bytes_accessed=rows * cols // 16, transcendentals=0
        ),
        name="assemble",
    )(spots, *(pltpu.with_memory_space_constraint(c, pltpu.HBM) for c in come))


def pack_kernel(seqs, times, *refs):
    given, first, second, held, sems = refs[:6], refs[6], refs[7], refs[8:-1], refs[-1]
    copies = [
        pltpu.make_async_copy(ref, mine, sems.at[k])
        for k, (ref, mine) in enumerate(zip(given, held, strict=True))
    ]
    for copy in copies:
        copy.start()
    for copy in copies:
        copy.wait()
    w_qkv, w_out, w_time, w_up, w_down, gains = held
    shard = w_qkv.shape[2]
    rows = first.shape[0]
    for c in range(3):
        first[:, c * shard : (c + 1) * shard] = w_qkv[c]
    at = 3 * shard
    for block in (w_out, w_time):
        first[:, at : at + block.shape[0]] = block[...].astype(f32).T.astype(bf16)
        at += block.shape[0]
    row = lax.broadcasted_iota(jnp.int32, (LANES, rows), 0)
    marks = jnp.zeros((LANES, rows), f32)
    for k in range(2):
        marks = jnp.where(row == k, gains[k : k + 1, :].astype(f32), marks)
    for i in range(seqs):
        for k, part in enumerate((times[i] // 32, lax.rem(times[i], 32))):
            marks = jnp.where(row == 2 + 2 * i + k, part.astype(f32), marks)
    first[:, at:] = marks.T.astype(bf16)
    hid = w_up.shape[1]
    second[:, :hid] = w_up[...]
    second[:, hid:] = w_down[...].astype(f32).T.astype(bf16)


def packed(times, *given):
    w_qkv, w_out, w_time, w_up, _, _ = given
    rows = w_up.shape[0]
    cols = 3 * w_qkv.shape[2] + w_out.shape[0] + w_time.shape[0] + LANES
    return call(
        functools.partial(pack_kernel, times.shape[0]),
        "pack",
        8,
        0,
        (like((rows, cols), bf16), like((rows, 2 * w_up.shape[1]), bf16)),
        (times, *given),
        [*(pltpu.VMEM(g.shape, g.dtype) for g in given), pltpu.SemaphoreType.DMA((len(given),))],
        direct=tuple(range(1, 1 + len(given))),
    )


class Ring:
    def __init__(self, n):
        self.n = n
        me = lax.axis_index("dp")
        spot = jnp.where(me & 1 == 0, me >> 1, n - 1 - (me >> 1))
        order = list(range(0, n, 2)) + list(range(n - 1, 0, -2))
        self.right = [(order[p], order[(p + 1) % n]) for p in range(n)]
        self.left = [(b, a) for a, b in self.right]

        def at(offset):
            there = spot + offset
            there = jnp.where(there >= n, there - n, jnp.where(there < 0, there + n, there))
            return jnp.where(there < n // 2, 2 * there, 2 * (n - 1 - there) + 1)

        self.near = tuple(at(k) for k in range(1 - n // 2, n // 2 + 1))

    def at(self, offset):
        return self.near[offset + self.n // 2 - 1]

    def gather(self, block):
        n, rows = self.n, block.shape[0]
        come, spots = [block], [self.at(0) * rows]
        from_left = from_right = block
        waited = yield ()
        for hop in range(1, n // 2):
            from_left = lax.ppermute(from_left, "dp", self.right)
            from_right = lax.ppermute(from_right, "dp", self.left)
            waited = yield (from_left, from_right), waited
            (from_left, from_right), waited = gate((from_left, from_right), waited)
            come += [from_left, from_right]
            spots += [self.at(-hop) * rows, self.at(hop) * rows]
        come.append(lax.ppermute(from_left[: rows // 2], "dp", self.right))
        come.append(lax.ppermute(from_right[rows // 2 :], "dp", self.left))
        farthest = self.at(n // 2) * rows
        spots += [farthest, farthest + rows // 2]
        yield tuple(come[-2:]), waited
        yield assembled(jnp.stack(spots).astype(jnp.int32), come)

    def scatter(self, terms):
        n, rows = self.n, terms[0].shape[0] // self.n

        def whole(offset, at, size):
            parts = [
                lax.dynamic_slice_in_dim(t, self.at(offset) * rows + at, size, 0) for t in terms
            ]
            return sum(p.astype(f32) for p in parts)

        def part(offset, at=0, size=rows):
            return whole(offset, at, size).astype(bf16)

        def plus(run, offset, at=0, size=rows):
            return (run.astype(f32) + whole(offset, at, size)).astype(bf16)

        half = rows // 2
        right, left = part(n // 2, 0, half), part(n // 2, half, half)
        for hop in range(1, n // 2 + 1):
            right = lax.ppermute(right, "dp", self.right)
            left = lax.ppermute(left, "dp", self.left)
            waited = yield (right, left)
            (right, left), _ = gate((right, left), waited)
            if hop == 1:
                rest = n // 2 - 1
                right = jnp.concatenate([plus(right, rest, 0, half), part(rest, half, half)])
                left = jnp.concatenate([part(-rest, 0, half), plus(left, -rest, half, half)])
            elif hop < n // 2:
                right = plus(right, n // 2 - hop)
                left = plus(left, hop - n // 2)
        yield whole(0, 0, rows) + right.astype(f32) + left.astype(f32)


def butterfly(value, axis, bit, n):
    return lax.ppermute(value, axis, [(i, i ^ bit) for i in range(n)])


def gate(values, waited):
    return lax.optimization_barrier((values, tuple(waited)))


def swap(value, bit, n):
    return lax.ppermute(value, "tensor", [(i, i ^ bit) for i in range(n)])


def to_features(keep, got, n, waited):
    chip = lax.axis_index("tensor") // 2
    half = keep.shape[1] // 2
    (keep, got), _ = gate((keep, got), waited)
    got = jnp.concatenate([got[:, half:], got[:, :half]], axis=1)
    shape = keep.shape[1:]
    terms = (keep, got)
    bit = 1
    while 2 * bit < n:
        value = terms[0].astype(f32) + terms[1].astype(f32)
        value = value.reshape((-1, 2) + shape)
        mine = (chip // bit) % 2
        kept = lax.dynamic_index_in_dim(value, mine, 1, keepdims=False)
        sent = lax.dynamic_index_in_dim(value, 1 - mine, 1, keepdims=False)
        terms = (kept, swap(sent.astype(bf16), 2 * bit, n))
        bit *= 2
    return terms


def shards(
    inputs,
    segment_ids,
    doc_offsets,
    time_index,
    w_qkv,
    w_out,
    w_up,
    w_down,
    w_time,
    gain_attn,
    gain_mlp,
    cotangent,
):
    n_dp = lax.axis_size("dp")
    n_tensor = lax.axis_size("tensor")
    me_dp = lax.axis_index("dp")
    core = lax.axis_index("tensor") % 2
    chips = n_tensor // 2
    seqs_dev, seq_len, width = inputs.shape
    half = seq_len // 2
    blocks = seq_len // BLOCK
    shard = width // n_tensor
    scale = (width // HEADS) ** (-0.5)
    hidden_dev = w_up.shape[1]
    rows = width // n_dp
    n_seqs = n_dp * seqs_dev
    ring = Ring(n_dp)
    seqs = range(seqs_dev)

    metas, seg_cols, seg_rows, places = [], [], [], []
    for i in seqs:
        ids = segment_ids[i]
        metas.append(
            jnp.concatenate(
                [
                    jnp.stack([core, me_dp]).astype(jnp.int32),
                    ids[::BLOCK],
                    ids[BLOCK - 1 :: BLOCK],
                ]
            )
        )
        seg_cols.append(ids[:, None])
        seg_rows.append(ids.reshape(blocks, BLOCK))
        places.append(positions(ids, doc_offsets[i]))
    w1_part, w2_part, _ = packed(
        time_index, w_qkv, w_out, w_time, w_up, w_down, jnp.stack([gain_attn, gain_mlp])
    )
    *entered, _ = embedded(metas[0], inputs, jnp.stack(places))
    cot = [cotangent[i] for i in seqs]
    gather1 = ring.gather(w1_part)
    next(gather1)
    brought, passed = [gather1.send(())[0]], []
    beside = [(*seg_cols, *seg_rows, *cot, *ring.near, *metas), tuple(entered)]
    while not isinstance(w1 := gather1.send(beside.pop(0) if beside else ()), jax.Array):
        brought.append(w1[0])
        passed.append(w1[1])
    early, entered = passed[:2]
    seg_cols, seg_rows, cot = (early[k * seqs_dev : (k + 1) * seqs_dev] for k in range(3))
    ring.near = early[3 * seqs_dev : -seqs_dev]
    metas = early[-seqs_dev:]
    w2_part, _ = gate(w2_part, brought[-2][:1])
    gather2 = ring.gather(w2_part)
    next(gather2)
    brought2 = [gather2.send(())[0]]
    small = w1[:, 4 * shard :]
    temb = sinusoid(time_index.astype(f32), TEMB)
    cond = jnp.sum(temb[:, None, :] * small[None, :, :TEMB].astype(f32), axis=2)
    attn_g = small[:, TEMB].astype(f32)[None]
    mlp_g = small[:, TEMB + 1].astype(f32)[None]
    def exchange_core(value):
        return swap(value, 1, n_tensor)

    def gather_chips(value):
        values = [value]
        bit = 2
        while bit < n_tensor:
            values = values + [swap(v, bit, n_tensor) for v in values]
            bit *= 2
        return values

    def sum_chips(value):
        bit = 2
        low, got = value.astype(bf16), jnp.zeros_like(value, bf16)
        while bit < n_tensor:
            low = (low.astype(f32) + got.astype(f32)).astype(bf16)
            got = swap(low, bit, n_tensor)
            bit *= 2
        return low, got

    h0, n1, kept, h1, n2 = [], [], [], [], []
    w_outs = gather_chips(w1[:, 3 * shard : 4 * shard])
    while not isinstance(w2 := gather2.send(()), jax.Array):
        brought2.append(w2[0])
    brought2 = brought2[-4:]
    after = ()
    for i in seqs:
        h, n, qkv, inv, token = projected(
            metas[i], entered[i], cond[i : i + 1], attn_g, w1, shard, after
        )
        a, lse, token = attended(
            metas[i],
            qkv,
            inv,
            seg_cols[i],
            seg_rows[i],
            shard,
            scale,
            (token, *(brought2[i] if i < 2 else ())),
        )
        after = (token, *w_outs[1:])
        h0.append(h)
        n1.append(n)
        kept.append((qkv, a, lse))
    mixes = [gather_chips(k[1]) for k in kept]
    outs, terms, d_n2, grad2, downs = [], [], [], [], []
    share = 1.0 / chips

    def out_of(i, after):
        keep, send, token = projected_out(metas[i], mixes[i], w_outs, after)
        outs.append((keep, exchange_core(send)))
        return token

    def middle_of(i, after):
        h, own, token = middle(metas[i], h0[i], *outs[i], mlp_g, after)
        h1.append(h)
        n2.append((own, exchange_core(own)))
        return token

    def hidden_of(i, after):
        d_keep, d_send, grad, keep, send, token = hidden_layer(
            metas[i], n2[i], cot[i], w2, h1[i], chips, after
        )
        grad2.append(grad)
        terms.append((d_keep, exchange_core(d_send)))
        downs.append((keep, exchange_core(send)))
        return token

    def sum_of(i, after):
        (keep, got), _ = gate(terms[i], after)
        d_n2.append(sum_chips(keep.astype(f32) + got.astype(f32)))
        return d_n2[i][0]

    final = seqs_dev - 1
    for i in seqs:
        token = out_of(i, (token, *(brought2[2] if i == 1 else ())))
        token = middle_of(i, (token,))
    for i in seqs:
        token = hidden_of(i, (token,))
        if i < final:
            token = sum_of(i, (token,))
    grad2, _ = gate(grad2, (got for _, got in d_n2))
    sum2 = ring.scatter(grad2)
    hops2 = next(sum2)
    all_sums, gain_sums, to_inputs, lows = [], [], [], []

    def middle_back_of(i, after):
        low, gain_sum, token = middle_back(metas[i], *d_n2[i], h1[i], cot[i], mlp_g, after)
        lows.append((low, exchange_core(low)))
        gain_sums.append(gain_sum * share)
        return token

    token = middle_back_of(0, (token,))
    if final:
        token = sum_of(final, (token,))
    hops2 = sum2.send((token,))
    grad1, waited, side = [], (), []
    for i in seqs:
        grad, keep, send, s, token = attended_back(
            metas[i],
            *lows[i],
            w1,
            kept[i],
            seg_cols[i],
            seg_rows[i],
            n1[i],
            attn_g,
            scale,
            chips,
            (token, *waited),
        )
        grad1.append(grad)
        all_sums.append(s)
        to_inputs.append((keep, exchange_core(send)))
        if i < final:
            token = middle_back_of(i + 1, (token,))
            hops2 = sum2.send((token,))
            waited = hops2
            block_out = [to_features(*pair, n_tensor, (token,)) for pair in downs]
    table = jnp.zeros((n_seqs, width), f32)
    ours = jnp.concatenate([t[1:2] for t in all_sums])
    table = lax.dynamic_update_slice_in_dim(table, ours, me_dp * seqs_dev, 0)
    table = jnp.concatenate(
        [table, sum(t[0:1] for t in all_sums), sum(gain_sums), jnp.zeros((6, width), f32)]
    )
    side = [to_features(*pair, n_tensor, (token,)) for pair in to_inputs]
    grad1, _ = gate(grad1, (got for _, got in block_out))
    sum1 = ring.scatter(grad1)
    hops1 = next(sum1)
    steps = [("tensor", 1 << k, n_tensor) for k in range(n_tensor.bit_length() - 1)]
    steps += [("dp", 1 << k, n_dp) for k in range(n_dp.bit_length() - 1)]
    moved = butterfly(table, *steps.pop(0))
    sent = list(side)
    while not isinstance(hops1, jax.Array):
        if steps:
            (table, moved), _ = gate((table, moved), hops1)
            table = table + moved
            moved = butterfly(table, *steps.pop(0))
        if not isinstance(hops2, jax.Array):
            hops2 = sum2.send(hops1)
        latest = hops1
        hops1 = sum1.send((moved, sent.pop(0)[1]) if sent else (moved,))
    block_out, _ = gate(block_out, latest)
    side, _ = gate(side, latest)
    for axis, bit, n in steps:
        table = table + moved
        moved = butterfly(table, axis, bit, n)
    table = table + moved
    share1 = hops1
    while not isinstance(hops2, jax.Array):
        hops2 = sum2.send(())
    share2 = hops2
    small, _ = gate(small, (token,))
    marks = small[::rows, TEMB + 2 : TEMB + 2 + 2 * seqs_dev].astype(f32)
    times = (marks[:, 0::2] * 32 + marks[:, 1::2]).reshape(n_seqs)
    sums = lax.dynamic_slice_in_dim(table, me_dp * rows, rows, 1)
    block_out = jnp.concatenate([(k + g.astype(f32)).astype(bf16) for k, g in block_out])
    input_grad = jnp.concatenate([k + g.astype(f32) for k, g in side])
    factor = float(n_seqs * seq_len) ** (-0.5)
    temb_all = sinusoid(times, TEMB)
    grad_time = (
        jnp.einsum("st,sd->td", temb_all, sums[:n_seqs], precision=lax.Precision.HIGHEST)
        * factor
    )

    def natural(value):
        return jnp.roll(value, core * half, axis=1)

    cols = 3 * shard
    return (
        natural(block_out),
        natural(input_grad),
        jnp.stack([share1[:, c * shard : (c + 1) * shard] for c in range(3)]) * factor,
        share1[:, cols : cols + shard].T * factor,
        share2[:, :hidden_dev] * factor,
        share2[:, hidden_dev:].T * factor,
        grad_time,
        sums[n_seqs] * factor,
        sums[n_seqs + 1] * factor,
    )


def solution(mesh):
    in_specs = (
        P("dp", None, None),
        P("dp", None),
        P("dp", None),
        P("dp"),
        P(None, "dp", "tensor"),
        P("tensor", "dp"),
        P("dp", "tensor"),
        P("tensor", "dp"),
        P(None, "dp"),
        P("dp"),
        P("dp"),
        P("dp", None, None),
    )
    out_specs = (
        P("dp", None, "tensor"),
        P("dp", None, "tensor"),
        P(None, "dp", "tensor"),
        P("tensor", "dp"),
        P("dp", "tensor"),
        P("tensor", "dp"),
        P(None, "dp"),
        P("dp"),
        P("dp"),
    )
    return jax.shard_map(shards, mesh=mesh, in_specs=in_specs, out_specs=out_specs, check_vma=False)
```

```python
import functools
import math

import jax
import jax.numpy as jnp
from jax import lax
from jax.experimental import pallas as pl
from jax.experimental.pallas import tpu as pltpu
from jax.sharding import PartitionSpec as P

HEADS = 16
TEMB = 256
BLOCK = 256
LANES = 128
FINE = 64
eps = 1e-05
masked = -1000000000.0
f32 = jnp.float32
bf16 = jnp.bfloat16
VMEM = pl.BlockSpec(memory_space=pltpu.VMEM)
SMEM = pl.BlockSpec(memory_space=pltpu.SMEM)
ANY = pl.BlockSpec(memory_space=pl.ANY)
HBM = pl.BlockSpec(memory_space=pltpu.HBM)


def params(mebibytes):
    return pltpu.CompilerParams(vmem_limit_bytes=mebibytes * 1024 * 1024)


def freqs(width):
    half = width // 2
    return jnp.exp(-math.log(10000.0) * jnp.arange(half, dtype=f32) / half)


def sinusoid(values, width):
    angles = values[..., None] * freqs(width)
    return jnp.concatenate([jnp.sin(angles), jnp.cos(angles)], axis=-1)


def norm_parts(hidden):
    centre = jnp.mean(hidden, axis=-1, keepdims=True)
    centred = hidden - centre
    spread = jnp.mean(centred * centred, axis=-1, keepdims=True)
    inv = lax.rsqrt(spread + eps)
    return centred * inv, inv


def norm_back(unit, inv, gain, grad):
    scaled = grad * gain
    first = jnp.mean(scaled, axis=-1, keepdims=True)
    second = jnp.mean(scaled * unit, axis=-1, keepdims=True)
    return inv * (scaled - first - unit * second)


def positions(segs, offsets):
    seq_len = segs.shape[0]
    index = jnp.arange(seq_len, dtype=jnp.int32)
    member = segs[:, None] == jnp.arange(offsets.shape[0], dtype=jnp.int32)[None, :]
    starts = jnp.min(jnp.where(member, index[:, None], seq_len), axis=0)
    start_tok = jnp.sum(jnp.where(member, starts[None, :], 0), axis=1)
    offset_tok = jnp.sum(jnp.where(member, offsets[None, :], 0), axis=1)
    return offset_tok + index - start_tok


def dot(left, right, left_dim, right_dim):
    return lax.dot_general(
        left, right, (((left_dim,), (right_dim,)), ((), ())), preferred_element_type=f32
    )


def like(shape, dtype):
    return jax.ShapeDtypeStruct(shape, dtype)


def rows_at(block):
    return pl.ds(pl.multiple_of(block * BLOCK, BLOCK), BLOCK)


def exchanged(core, block, blocks):
    return lax.rem(block + core * (blocks // 2), blocks)


def call(kernel, name, mebibytes, flops, outs, args, scratch=(), after=(), stored=(), direct=()):
    count, first, total = len(args), len(args) + len(after), len(outs)

    def body(*refs):
        results = list(refs[first : first + total])
        token = refs[first + total]
        rest = refs[first + total + 1 :]
        sems = rest[-1]
        copies = []

        def store(k, rows=slice(None)):
            mine = rest[stored.index(k)]
            copies.append(
                pltpu.make_async_copy(mine.at[rows], refs[first + k].at[rows], sems.at[len(copies)])
            )
            copies[-1].start()

        for at, k in enumerate(stored):
            results[k] = rest[at]
        extra = rest[len(stored) : -1]
        if stored:
            kernel(*refs[:count], *results, *extra, store=store)
        else:
            kernel(*refs[:count], *results, *extra)
        token[...] = jnp.zeros(token.shape, token.dtype)
        for copy in copies:
            copy.wait()

    moved = sum(a.size * a.dtype.itemsize for a in args) + sum(
        math.prod(o.shape) * o.dtype.itemsize for o in outs
    )
    return pl.pallas_call(
        body,
        out_shape=(
            *(
                pltpu.HBM(o.shape, o.dtype) if k in stored else o for k, o in enumerate(outs)
            ),
            like((8, LANES), f32),
        ),
        in_specs=[SMEM]
        + [HBM if k in direct else VMEM for k in range(1, count)]
        + [ANY] * len(after),
        out_specs=tuple(HBM if k in stored else VMEM for k in range(total)) + (VMEM,),
        scratch_shapes=[pltpu.VMEM(outs[k].shape, outs[k].dtype) for k in stored]
        + list(scratch)
        + [pltpu.SemaphoreType.DMA((8,))],
        compiler_params=params(mebibytes),
        cost_estimate=pl.CostEstimate(
            flops=flops // 1024, bytes_accessed=moved // 1024, transcendentals=0
        ),
        name=name,
    )(
        *(
            pltpu.with_memory_space_constraint(a, pltpu.HBM) if k in direct else a
            for k, a in enumerate(args)
        ),
        *after,
    )


def load(given, held, sems):
    copies = [
        pltpu.make_async_copy(ref, mine, sems.at[k])
        for k, (ref, mine) in enumerate(zip(given, held, strict=True))
    ]
    for copy in copies:
        copy.start()
    return lambda: copies.pop(0).wait()


def held_like(arrays):
    return [*(pltpu.VMEM(a.shape, a.dtype) for a in arrays), pltpu.SemaphoreType.DMA((len(arrays),))]


def pieces(table):
    first = table.astype(bf16)
    rest = table - first.astype(f32)
    second = rest.astype(bf16)
    return jnp.concatenate([first, second, (rest - second.astype(f32)).astype(bf16)], axis=0)


def embed_kernel(seqs, meta, inputs, place, freq, *refs, store):
    outs, held, sems = refs[:seqs], refs[seqs], refs[seqs + 1]
    copies = [pltpu.make_async_copy(inputs.at[i], held.at[i], sems.at[i]) for i in range(seqs)]
    for copy in copies:
        copy.start()
    seq_len = inputs.shape[1]
    half = freq.shape[1]
    blocks = seq_len // BLOCK
    step = lax.broadcasted_iota(jnp.int32, (FINE, half), 0).astype(f32)
    angles = (step * (FINE * freq[...]), step * freq[...])
    coarse, fine = (pieces(jnp.concatenate([jnp.sin(t), jnp.cos(t)], axis=1)) for t in angles)
    entry = lax.rem(lax.broadcasted_iota(jnp.int32, (BLOCK, 3 * FINE), 1), FINE)
    for i in range(seqs):

        def add(block, _, i=i):
            source = rows_at(exchanged(meta[0], block, blocks))
            at = place[i, source, :]
            a = dot((entry == at // FINE).astype(bf16), coarse, 1, 0)
            b = dot((entry == lax.rem(at, FINE)).astype(bf16), fine, 1, 0)
            sin_a, cos_a, sin_b, cos_b = a[:, :half], a[:, half:], b[:, :half], b[:, half:]
            x = held[i, source, :].astype(f32)
            outs[i][rows_at(block), :half] = x[:, :half] + (sin_a * cos_b + cos_a * sin_b)
            outs[i][rows_at(block), half:] = x[:, half:] + (cos_a * cos_b - sin_a * sin_b)
            return 0

        copies[i].wait()
        lax.fori_loop(0, blocks, add, 0)
        store(i)


def embedded(meta, inputs, place):
    seqs, seq_len, width = inputs.shape
    return call(
        functools.partial(embed_kernel, seqs),
        "embed",
        18,
        200 * inputs.size,
        (like((seq_len, width), f32),) * seqs,
        (meta, inputs, place[:, :, None], freqs(width)[None]),
        [pltpu.VMEM(inputs.shape, bf16), pltpu.SemaphoreType.DMA((seqs,))],
        stored=tuple(range(seqs)),
        direct=(1,),
    )


def window(meta, block, blocks):
    first, last = meta[2 + block], meta[2 + blocks + block]
    low, high = jnp.int32(blocks), jnp.int32(0)
    for j in range(blocks):
        hit = (meta[2 + blocks + j] >= first) & (meta[2 + j] <= last)
        low = jnp.where(hit & (low == blocks), j, low)
        high = jnp.where(hit, j + 1, high)
    return low, high - low


def set_bias(bias, seg_col, seg_row, block, low, count):
    keys = jnp.concatenate([seg_row[pl.ds(low + j, 1), :] for j in range(count)], axis=1)
    bias[:, : count * BLOCK] = jnp.where(seg_col[rows_at(block), :] == keys, 0.0, masked)


def project_kernel(shard, meta, entered, cond, gain, w1, h0, n1, qkv, inv, store):
    blocks = entered.shape[0] // BLOCK
    for block in range(blocks):
        rows = slice(block * BLOCK, (block + 1) * BLOCK)
        h = entered[rows, :] + cond[...]
        unit, scale = norm_parts(h)
        if block < blocks // 2:
            h0[rows, :] = h
        normed = (unit * gain[...]).astype(bf16)
        n1[rows, :] = normed
        inv[rows, LANES - 1 :] = scale
        terms = dot(normed, w1[:, : 3 * shard], 1, 0)
        qkv[rows_at(exchanged(meta[0], block, blocks)), :] = terms.astype(bf16)
        if block < blocks // 2:
            store(0, rows)
        store(1, rows)


def projected(meta, entered, cond, gain, w1, shard, after):
    seq_len, width = entered.shape
    return call(
        functools.partial(project_kernel, shard),
        "project",
        18,
        6 * seq_len * width * shard,
        (
            like((seq_len // 2, width), f32),
            like((seq_len, width), bf16),
            like((seq_len, 3 * shard), bf16),
            like((seq_len, LANES), f32),
        ),
        (meta, entered, cond, gain, w1),
        after=after,
        stored=(0, 1),
    )


def attend_kernel(shard, scale, meta, qkv, inv, seg_col, seg_row, a, lse, bias):
    seq_len = qkv.shape[0]
    blocks = seq_len // BLOCK
    lse[:, LANES - 1 :] = inv[:, LANES - 1 :]
    even = lax.broadcasted_iota(jnp.int32, (BLOCK, LANES), 1) < LANES // 2

    def attend(block, _):
        own = rows_at(exchanged(meta[0], block, blocks))
        low, count = window(meta, block, blocks)
        for size in range(1, blocks + 1):

            @pl.when(count == size)
            def _(size=size):
                span = size * BLOCK
                keys = pl.ds(pl.multiple_of(low * BLOCK, BLOCK), span)
                set_bias(bias, seg_col, seg_row, block, low, size)
                for pair in range(shard // LANES):
                    at = pair * LANES
                    query = qkv[rows_at(block), at : at + LANES] * jnp.bfloat16(scale)
                    key = qkv[keys, shard + at : shard + at + LANES]
                    value = qkv[keys, 2 * shard + at : 2 * shard + at + LANES]
                    outs = []
                    for e in range(2):
                        picked = jnp.where(even == (e == 0), query, jnp.bfloat16(0))
                        scores = dot(picked, key, 1, 1) + bias[:, :span]
                        top = jnp.max(scores, axis=1, keepdims=True)
                        expo = jnp.exp(scores - top)
                        denom = jnp.sum(expo, axis=1, keepdims=True)
                        outs.append(dot(expo.astype(bf16), value, 1, 0) * (1.0 / denom))
                        head = 2 * pair + e
                        lse[rows_at(block), head : head + 1] = top + jnp.log(denom)
                    a[own, at : at + LANES] = jnp.where(even, outs[0], outs[1]).astype(bf16)

        return 0

    lax.fori_loop(0, blocks, attend, 0)


def attended(meta, qkv, inv, seg_col, seg_row, shard, scale, after):
    seq_len = qkv.shape[0]
    return call(
        functools.partial(attend_kernel, shard, scale),
        "attend",
        10,
        8 * seq_len * seq_len * shard,
        (like((seq_len, shard), bf16), like((seq_len, LANES), f32)),
        (meta, qkv, inv, seg_col, seg_row),
        [pltpu.VMEM((BLOCK, seq_len), f32)],
        after,
    )


def out_kernel(meta, count, *refs):
    mixed, weights, keep, send = refs[:count], refs[count : 2 * count], refs[-2], refs[-1]
    half = keep.shape[0]
    for at in range(0, half, BLOCK):
        for base, out in ((half, send), (0, keep)):
            term = 0.0
            for a, w in zip(mixed, weights, strict=True):
                term = term + dot(a[base + at : base + at + BLOCK, :], w[...], 1, 1)
            out[at : at + BLOCK, :] = term.astype(out.dtype)


def projected_out(meta, mixed, weights, after):
    seq_len, shard = mixed[0].shape
    width = weights[0].shape[0]
    return call(
        lambda m, *refs: out_kernel(m, len(mixed), *refs),
        "project_out",
        7,
        2 * seq_len * width * shard * len(mixed),
        (like((seq_len // 2, width), bf16),) * 2,
        (meta, *mixed, *weights),
        after=after,
    )


def middle_kernel(meta, h0, keep, got, gain, h1, n2, inv, store):
    for at in range(0, keep.shape[0], BLOCK):
        rows = slice(at, at + BLOCK)
        h = h0[rows, :] + (keep[rows, :].astype(f32) + got[rows, :].astype(f32))
        unit, scale = norm_parts(h)
        inv[rows, :1] = scale
        h1[rows, :] = h
        n2[rows, :] = (unit * gain[...]).astype(bf16)
    store(0)


def middle(meta, h0, keep, got, gain, after):
    return call(
        middle_kernel,
        "middle",
        10,
        20 * keep.size,
        (like(keep.shape, f32), like(keep.shape, bf16), like((keep.shape[0], LANES), f32)),
        (meta, h0, keep, got, gain),
        after=after,
        stored=(0,),
    )


def split_features(core, term, keep, send):
    groups, _, part = keep.shape
    for g in range(groups):
        first = term[:, 2 * g * part : (2 * g + 1) * part]
        second = term[:, (2 * g + 1) * part : (2 * g + 2) * part]
        keep[g] = jnp.where(core == 0, first, second)
        send[g] = jnp.where(core == 0, second, first)


def hidden_kernel(
    meta,
    n2_own,
    n2_other,
    cot,
    w2,
    h1,
    d_keep,
    d_send,
    grad,
    keep,
    send,
    act,
    d_hid,
    held,
    sems,
    store,
):
    ready = load([h1], [held], sems)
    hid = w2.shape[1] // 2
    half, width = n2_own.shape
    chips = keep.shape[0]
    chunk = min(512, hid)
    own = pl.multiple_of(meta[0] * half, BLOCK)
    other = pl.multiple_of((1 - meta[0]) * half, BLOCK)
    for first, base, n2, d_n2 in ((half, other, n2_other, d_send), (0, own, n2_own, d_keep)):
        if first == 0:
            ready()
        for at in range(0, half, BLOCK):
            rows = slice(at, at + BLOCK)
            mine = slice(first + at, first + at + BLOCK)
            d_out = cot[pl.ds(base + at, BLOCK), :]
            for col in range(0, hid, chunk):
                u = dot(n2[rows, :], w2[:, col : col + chunk], 1, 0)
                d_act = dot(d_out, w2[:, hid + col : hid + col + chunk], 1, 0)
                cdf = 0.5 + 0.5 * lax.erf(u * (0.5**0.5))
                act[mine, col : col + chunk] = (u * cdf).astype(bf16)
                slope = cdf + u * (jnp.exp(-0.5 * u * u) * (0.5 / math.pi) ** 0.5)
                d_hid[mine, col : col + chunk] = (d_act * slope).astype(bf16)
            d_n2[rows, :] = dot(d_hid[mine, :], w2[:, :hid], 1, 1).astype(bf16)
            term = dot(act[mine, :], w2[:, hid:], 1, 1)
            if first == 0:
                term = term + held[rows, :] * (1.0 / chips)
            split_features(
                meta[0], term.astype(bf16), keep.at[:, mine, :], send.at[:, mine, :]
            )
    store(3)
    store(4)
    for at in range(0, width, BLOCK):
        cols = slice(at, at + BLOCK)
        up = dot(n2_own[:, cols], d_hid[:half, :], 0, 0)
        up = up + dot(n2_other[:, cols], d_hid[half:, :], 0, 0)
        grad[cols, :hid] = up.astype(bf16)
        down = dot(cot[pl.ds(own, half), cols], act[:half, :], 0, 0)
        down = down + dot(cot[pl.ds(other, half), cols], act[half:, :], 0, 0)
        grad[cols, hid:] = down.astype(bf16)
        store(2, cols)


def hidden_layer(meta, n2, cot, w2, h1, chips, after):
    half, width = n2[0].shape
    hid = w2.shape[1] // 2
    split = like((chips, 2 * half, width // (2 * chips)), bf16)
    d_n2 = like((half, width), bf16)
    return call(
        hidden_kernel,
        "hidden_layer",
        28,
        24 * half * width * hid,
        (d_n2, d_n2, like((width, 2 * hid), bf16), split, split),
        (meta, *n2, cot, w2, h1),
        [*(pltpu.VMEM((2 * half, hid), bf16) for _ in range(2)), *held_like([h1])],
        after,
        (2, 3, 4),
        (5,),
    )


def middle_back_kernel(meta, low, got, n2, inv1, cot, gain, d_low, sums):
    half = n2.shape[0]
    base = pl.multiple_of(meta[0] * half, BLOCK)
    ungain = 1.0 / gain[...]
    total = jnp.zeros(sums.shape, f32)
    for at in range(0, half, BLOCK):
        rows = slice(at, at + BLOCK)
        d_n2 = low[rows, :].astype(f32) + got[rows, :].astype(f32)
        unit = n2[rows, :].astype(f32) * ungain
        total = total + jnp.sum(d_n2 * unit, axis=0, keepdims=True)
        d_h = norm_back(unit, inv1[rows, :1], gain[...], d_n2)
        d_h = d_h + cot[pl.ds(base + at, BLOCK), :].astype(f32)
        d_low[rows, :] = d_h.astype(bf16)
    sums[...] = total


def middle_back(meta, low, got, n2, inv1, cot, gain, after):
    return call(
        middle_back_kernel,
        "middle_back",
        12,
        30 * n2.size,
        (like(n2.shape, bf16), like((1, n2.shape[1]), f32)),
        (meta, low, got, n2, inv1, cot, gain),
        after=after,
    )


def attend_back_kernel(
    shard,
    scale,
    seq,
    seqs,
    n_seqs,
    meta,
    low_own,
    low_other,
    w1,
    qkv,
    a,
    lse,
    seg_col,
    seg_row,
    n1,
    gain,
    gain_sum,
    grads,
    keep,
    send,
    d_mix,
    total,
    bias,
    d_qkv,
    *loads,
    store,
):
    ready = load((qkv, lse, n1), loads[:-1], loads[-1])
    qkv, lse, n1 = loads[:-1]
    seq_len = a.shape[0]
    blocks = seq_len // BLOCK
    per = blocks // 2
    for block in range(per):
        w_out_t = w1[:, 3 * shard : 4 * shard]
        rows = slice(block * BLOCK, (block + 1) * BLOCK)
        d_mix[rows, :] = dot(low_own[rows, :], w_out_t, 1, 0).astype(bf16)
        after = slice((block + per) * BLOCK, (block + per + 1) * BLOCK)
        d_mix[after, :] = dot(low_other[rows, :], w_out_t, 1, 0).astype(bf16)
    ready()
    ready()
    total[...] = jnp.zeros(total.shape, f32)
    even = lax.broadcasted_iota(jnp.int32, (BLOCK, LANES), 1) < LANES // 2

    def attend(block, _):
        own = rows_at(exchanged(meta[0], block, blocks))
        low, count = window(meta, block, blocks)
        for size in range(1, blocks + 1):

            @pl.when(count == size)
            def _(size=size):
                span = size * BLOCK
                keys = pl.ds(pl.multiple_of(low * BLOCK, BLOCK), span)
                set_bias(bias, seg_col, seg_row, block, low, size)
                for pair in range(shard // LANES):
                    at = pair * LANES
                    query = qkv[rows_at(block), at : at + LANES] * jnp.bfloat16(scale)
                    key = qkv[keys, shard + at : shard + at + LANES]
                    value = qkv[keys, 2 * shard + at : 2 * shard + at + LANES]
                    grad = d_mix[own, at : at + LANES]
                    product = grad.astype(f32) * a[own, at : at + LANES].astype(f32)
                    d_query = []
                    d_key = d_value = 0.0
                    for e in range(2):
                        side = even == (e == 0)
                        picked = jnp.where(side, query, jnp.bfloat16(0))
                        picked_grad = jnp.where(side, grad, jnp.bfloat16(0))
                        delta = jnp.sum(jnp.where(side, product, 0.0), axis=1, keepdims=True)
                        head = 2 * pair + e
                        scores = dot(picked, key, 1, 1) + bias[:, :span]
                        probs = jnp.exp(scores - lse[rows_at(block), head : head + 1])
                        d_probs = dot(picked_grad, value, 1, 1)
                        d_scores = (probs * (d_probs - delta)).astype(bf16)
                        d_query.append(dot(d_scores, key, 1, 0))
                        d_key = d_key + dot(d_scores, picked, 0, 0)
                        d_value = d_value + dot(probs.astype(bf16), picked_grad, 0, 0)
                    total[keys, at : at + LANES] += d_key
                    total[keys, shard + at : shard + at + LANES] += d_value
                    d_qkv[own, at : at + LANES] = (
                        jnp.where(even, d_query[0], d_query[1]) * scale
                    ).astype(bf16)

        return 0

    lax.fori_loop(0, blocks, attend, 0)
    share = 1.0 / keep.shape[0]
    unit_sum = term_sum = jnp.zeros((1, n1.shape[1]), f32)
    ungain = 1.0 / gain[...]
    ready()
    for block in range(blocks):
        rows = slice(block * BLOCK, (block + 1) * BLOCK)
        d_qkv[rows, shard:] = total[rows_at(exchanged(meta[0], block, blocks)), :].astype(bf16)
        d_n1 = dot(d_qkv[rows, :], w1[:, : 3 * shard], 1, 1)
        unit = n1[rows, :].astype(f32) * ungain
        inv = lse[rows, LANES - 1 :]
        unit_sum = unit_sum + jnp.sum(d_n1 * unit, axis=0, keepdims=True)
        term = norm_back(unit, inv, gain[...], d_n1)
        if block < per:
            term = term + share * low_own[rows, :].astype(f32)
        term_sum = term_sum + jnp.sum(term, axis=0, keepdims=True)
        split_features(meta[0], term.astype(bf16), keep.at[:, rows, :], send.at[:, rows, :])
    row = lax.broadcasted_iota(jnp.int32, (LANES, n1.shape[1]), 0)
    table = jnp.where(row == meta[1] * seqs + seq, term_sum, 0.0)
    table = jnp.where(row == n_seqs, unit_sum, table)
    table = jnp.where(row == n_seqs + 1, gain_sum[...], table)
    grads[:, 4 * shard :] = table.T.astype(bf16)
    store(1)
    store(2)
    half = low_own.shape[0]
    for at in range(0, n1.shape[1], BLOCK):
        cols = slice(at, at + BLOCK)
        grads[cols, : 3 * shard] = dot(n1[:, cols], d_qkv[...], 0, 0).astype(bf16)
        proj = dot(low_own[:, cols], a[:half, :], 0, 0)
        proj = proj + dot(low_other[:, cols], a[half:, :], 0, 0)
        grads[cols, 3 * shard : 4 * shard] = proj.astype(bf16)
        store(0, cols)


def attended_back(
    meta, low, w1, kept, seg_col, seg_row, n1, gain, gain_sum, scale, groups, place, after
):
    qkv, a, lse = kept
    seq_len, shard = a.shape
    width = w1.shape[0]
    split = like((groups, seq_len, width // (2 * groups)), bf16)
    return call(
        functools.partial(attend_back_kernel, shard, scale, *place),
        "attend_back",
        36,
        16 * seq_len * width * shard + 20 * seq_len * seq_len * shard,
        (like((width, 4 * shard + LANES), bf16), split, split),
        (meta, *low, w1, qkv, a, lse, seg_col, seg_row, n1, gain, gain_sum),
        [
            pltpu.VMEM((seq_len, shard), bf16),
            pltpu.VMEM((seq_len, 2 * shard), f32),
            pltpu.VMEM((BLOCK, seq_len), f32),
            pltpu.VMEM((seq_len, 3 * shard), bf16),
            *held_like((qkv, lse, n1)),
        ],
        after,
        (0, 1, 2),
        (4, 6, 9),
    )


def assemble_kernel(spots, *refs):
    come, full, sems = refs[:-2], refs[-2], refs[-1]
    copies = []
    for k, ref in enumerate(come):
        rows = ref.shape[0]
        at = pl.ds(pl.multiple_of(spots[k], rows), rows)
        copies.append(pltpu.make_async_copy(ref, full.at[at, :], sems.at[k]))
    for copy in copies:
        copy.start()
    for copy in copies:
        copy.wait()


def assembled(spots, come):
    rows, cols = sum(c.shape[0] for c in come), come[0].shape[1]
    return pl.pallas_call(
        assemble_kernel,
        out_shape=like((rows, cols), come[0].dtype),
        in_specs=[SMEM] + [HBM] * len(come),
        out_specs=ANY,
        scratch_shapes=[pltpu.SemaphoreType.DMA((len(come),))],
        compiler_params=params(2),
        cost_estimate=pl.CostEstimate(
            flops=0, bytes_accessed=rows * cols // 16, transcendentals=0
        ),
        name="assemble",
    )(spots, *(pltpu.with_memory_space_constraint(c, pltpu.HBM) for c in come))


def pack_kernel(seqs, times, *refs):
    given, first, second, held, sems = refs[:6], refs[6], refs[7], refs[8:-1], refs[-1]
    copies = [
        pltpu.make_async_copy(ref, mine, sems.at[k])
        for k, (ref, mine) in enumerate(zip(given, held, strict=True))
    ]
    for copy in copies:
        copy.start()
    for copy in copies:
        copy.wait()
    w_qkv, w_out, w_time, w_up, w_down, gains = held
    shard = w_qkv.shape[2]
    rows = first.shape[0]
    for c in range(3):
        first[:, c * shard : (c + 1) * shard] = w_qkv[c]
    at = 3 * shard
    for block in (w_out, w_time):
        first[:, at : at + block.shape[0]] = block[...].astype(f32).T.astype(bf16)
        at += block.shape[0]
    row = lax.broadcasted_iota(jnp.int32, (LANES, rows), 0)
    marks = jnp.zeros((LANES, rows), f32)
    for k in range(2):
        marks = jnp.where(row == k, gains[k : k + 1, :].astype(f32), marks)
    for i in range(seqs):
        for k, part in enumerate((times[i] // 32, lax.rem(times[i], 32))):
            marks = jnp.where(row == 2 + 2 * i + k, part.astype(f32), marks)
    first[:, at:] = marks.T.astype(bf16)
    hid = w_up.shape[1]
    second[:, :hid] = w_up[...]
    second[:, hid:] = w_down[...].astype(f32).T.astype(bf16)


def packed(times, *given):
    w_qkv, w_out, w_time, w_up, _, _ = given
    rows = w_up.shape[0]
    cols = 3 * w_qkv.shape[2] + w_out.shape[0] + w_time.shape[0] + LANES
    return call(
        functools.partial(pack_kernel, times.shape[0]),
        "pack",
        8,
        0,
        (like((rows, cols), bf16), like((rows, 2 * w_up.shape[1]), bf16)),
        (times, *given),
        [*(pltpu.VMEM(g.shape, g.dtype) for g in given), pltpu.SemaphoreType.DMA((len(given),))],
        direct=tuple(range(1, 1 + len(given))),
    )


class Ring:
    def __init__(self, n):
        self.n = n
        me = lax.axis_index("dp")
        spot = jnp.where(me & 1 == 0, me >> 1, n - 1 - (me >> 1))
        order = list(range(0, n, 2)) + list(range(n - 1, 0, -2))
        self.right = [(order[p], order[(p + 1) % n]) for p in range(n)]
        self.left = [(b, a) for a, b in self.right]

        def at(offset):
            there = spot + offset
            there = jnp.where(there >= n, there - n, jnp.where(there < 0, there + n, there))
            return jnp.where(there < n // 2, 2 * there, 2 * (n - 1 - there) + 1)

        self.near = tuple(at(k) for k in range(1 - n // 2, n // 2 + 1))

    def at(self, offset):
        return self.near[offset + self.n // 2 - 1]

    def gather(self, block):
        n, rows = self.n, block.shape[0]
        come, spots = [block], [self.at(0) * rows]
        from_left = from_right = block
        waited = yield ()
        for hop in range(1, n // 2):
            from_left = lax.ppermute(from_left, "dp", self.right)
            from_right = lax.ppermute(from_right, "dp", self.left)
            waited = yield (from_left, from_right), waited
            (from_left, from_right), waited = gate((from_left, from_right), waited)
            come += [from_left, from_right]
            spots += [self.at(-hop) * rows, self.at(hop) * rows]
        come.append(lax.ppermute(from_left[: rows // 2], "dp", self.right))
        come.append(lax.ppermute(from_right[rows // 2 :], "dp", self.left))
        farthest = self.at(n // 2) * rows
        spots += [farthest, farthest + rows // 2]
        yield tuple(come[-2:]), waited
        yield assembled(jnp.stack(spots).astype(jnp.int32), come)

    def scatter(self, terms):
        n, rows = self.n, terms[0].shape[0] // self.n

        def whole(offset, at, size):
            parts = [
                lax.dynamic_slice_in_dim(t, self.at(offset) * rows + at, size, 0) for t in terms
            ]
            return sum(p.astype(f32) for p in parts)

        def part(offset, at=0, size=rows):
            return whole(offset, at, size).astype(bf16)

        def plus(run, offset, at=0, size=rows):
            return (run.astype(f32) + whole(offset, at, size)).astype(bf16)

        half = rows // 2
        right, left = part(n // 2, 0, half), part(n // 2, half, half)
        for hop in range(1, n // 2 + 1):
            right = lax.ppermute(right, "dp", self.right)
            left = lax.ppermute(left, "dp", self.left)
            waited = yield (right, left)
            (right, left), _ = gate((right, left), waited)
            if hop == 1:
                rest = n // 2 - 1
                right = jnp.concatenate([plus(right, rest, 0, half), part(rest, half, half)])
                left = jnp.concatenate([part(-rest, 0, half), plus(left, -rest, half, half)])
            elif hop < n // 2:
                right = plus(right, n // 2 - hop)
                left = plus(left, hop - n // 2)
        yield whole(0, 0, rows) + right.astype(f32) + left.astype(f32)


def butterfly(value, axis, bit, n):
    return lax.ppermute(value, axis, [(i, i ^ bit) for i in range(n)])


def gate(values, waited):
    return lax.optimization_barrier((values, tuple(waited)))


def swap(value, bit, n):
    return lax.ppermute(value, "tensor", [(i, i ^ bit) for i in range(n)])


def to_features(keep, got, n, waited, pieces=1):
    chip = lax.axis_index("tensor") // 2
    half = keep.shape[1] // 2
    (keep, got), _ = gate((keep, got), waited)
    got = jnp.concatenate([got[:, half:], got[:, :half]], axis=1)
    kept, came = keep, [got]
    bit = 1
    while 2 * bit < n:
        value = kept.astype(f32) + jnp.concatenate(came, axis=1).astype(f32)
        value = value.reshape((-1, 2) + keep.shape[1:])
        mine = (chip // bit) % 2
        kept = lax.dynamic_index_in_dim(value, mine, 1, keepdims=False)
        sent = lax.dynamic_index_in_dim(value, 1 - mine, 1, keepdims=False).astype(bf16)
        bit *= 2
        parts = pieces if 2 * bit >= n else 1
        came = [swap(p, bit, n) for p in jnp.split(sent, parts, axis=1)]
    return kept, came


def shards(
    inputs,
    segment_ids,
    doc_offsets,
    time_index,
    w_qkv,
    w_out,
    w_up,
    w_down,
    w_time,
    gain_attn,
    gain_mlp,
    cotangent,
):
    n_dp = lax.axis_size("dp")
    n_tensor = lax.axis_size("tensor")
    me_dp = lax.axis_index("dp")
    core = lax.axis_index("tensor") % 2
    chips = n_tensor // 2
    seqs_dev, seq_len, width = inputs.shape
    half = seq_len // 2
    blocks = seq_len // BLOCK
    shard = width // n_tensor
    scale = (width // HEADS) ** (-0.5)
    hidden_dev = w_up.shape[1]
    rows = width // n_dp
    n_seqs = n_dp * seqs_dev
    ring = Ring(n_dp)
    seqs = range(seqs_dev)

    metas, seg_cols, seg_rows, places = [], [], [], []
    for i in seqs:
        ids = segment_ids[i]
        metas.append(
            jnp.concatenate(
                [
                    jnp.stack([core, me_dp]).astype(jnp.int32),
                    ids[::BLOCK],
                    ids[BLOCK - 1 :: BLOCK],
                ]
            )
        )
        seg_cols.append(ids[:, None])
        seg_rows.append(ids.reshape(blocks, BLOCK))
        places.append(positions(ids, doc_offsets[i]))
    w1_part, w2_part, _ = packed(
        time_index, w_qkv, w_out, w_time, w_up, w_down, jnp.stack([gain_attn, gain_mlp])
    )
    *entered, _ = embedded(metas[0], inputs, jnp.stack(places))
    cot = [cotangent[i] for i in seqs]
    gather1 = ring.gather(w1_part)
    next(gather1)
    brought, passed = [gather1.send(())[0]], []
    beside = [(*seg_cols, *seg_rows, *cot, *ring.near, *metas), tuple(entered)]
    while not isinstance(w1 := gather1.send(beside.pop(0) if beside else ()), jax.Array):
        brought.append(w1[0])
        passed.append(w1[1])
    early, entered = passed[:2]
    seg_cols, seg_rows, cot = (early[k * seqs_dev : (k + 1) * seqs_dev] for k in range(3))
    ring.near = early[3 * seqs_dev : -seqs_dev]
    metas = early[-seqs_dev:]
    w2_part, _ = gate(w2_part, brought[-2][:1])
    gather2 = ring.gather(w2_part)
    next(gather2)
    brought2 = [gather2.send(())[0]]
    small = w1[:, 4 * shard :]
    temb = sinusoid(time_index.astype(f32), TEMB)
    cond = jnp.sum(temb[:, None, :] * small[None, :, :TEMB].astype(f32), axis=2)
    attn_g = small[:, TEMB].astype(f32)[None]
    mlp_g = small[:, TEMB + 1].astype(f32)[None]
    def exchange_core(value):
        return swap(value, 1, n_tensor)

    def gather_chips(value):
        values = [value]
        bit = 2
        while bit < n_tensor:
            values = values + [swap(v, bit, n_tensor) for v in values]
            bit *= 2
        return values

    def sum_chips(value):
        bit = 2
        low, got = value.astype(bf16), jnp.zeros_like(value, bf16)
        while bit < n_tensor:
            low = (low.astype(f32) + got.astype(f32)).astype(bf16)
            got = swap(low, bit, n_tensor)
            bit *= 2
        return low, got

    h0, n1, kept, h1, inv1, n2 = [], [], [], [], [], []
    w_outs = gather_chips(w1[:, 3 * shard : 4 * shard])
    while not isinstance(w2 := gather2.send(()), jax.Array):
        brought2.append(w2[0])
    brought2 = brought2[-4:]
    after = ()
    for i in seqs:
        h, n, qkv, inv, token = projected(
            metas[i], entered[i], cond[i : i + 1], attn_g, w1, shard, after
        )
        a, lse, token = attended(
            metas[i],
            qkv,
            inv,
            seg_cols[i],
            seg_rows[i],
            shard,
            scale,
            (token, *(brought2[i] if i < 2 else ())),
        )
        after = (token, *w_outs[1:])
        h0.append(h)
        n1.append(n)
        kept.append((qkv, a, lse))
    mixes = [gather_chips(k[1]) for k in kept]
    outs, terms, d_n2, grad2, downs = [], [], [], [], []
    share = 1.0 / chips
    final = seqs_dev - 1

    def out_of(i, after):
        keep, send, token = projected_out(metas[i], mixes[i], w_outs, after)
        outs.append((keep, exchange_core(send)))
        return token

    def middle_of(i, after):
        h, own, inv, token = middle(metas[i], h0[i], *outs[i], mlp_g, after)
        inv1.append(inv)
        h1.append(h)
        n2.append((own, exchange_core(own)))
        return token

    def hidden_of(i, after):
        d_keep, d_send, grad, keep, send, token = hidden_layer(
            metas[i], n2[i], cot[i], w2, h1[i], chips, after
        )
        grad2.append(grad)
        terms.append((d_keep, exchange_core(d_send)))
        downs.append((keep, exchange_core(send)))
        return token

    def sum_of(i, after):
        (keep, got), _ = gate(terms[i], after)
        d_n2.append(sum_chips(keep.astype(f32) + got.astype(f32)))
        return d_n2[i][0]

    for i in seqs:
        token = out_of(i, (token, *(brought2[2] if i == 0 else ())))
    for i in seqs:
        token = middle_of(i, (token, *(brought2[3] if i == 0 else ())))
    for i in seqs:
        token = hidden_of(i, (token,))
        if i < final:
            token = sum_of(i, (token,))
    grad2, _ = gate(grad2, (got for _, got in d_n2))
    sum2 = ring.scatter(grad2)
    hops2 = next(sum2)
    gain_sums, to_inputs, lows = [], [], []

    def middle_back_of(i, after):
        low, gain_sum, token = middle_back(
            metas[i], *d_n2[i], n2[i][0], inv1[i], cot[i], mlp_g, after
        )
        lows.append((low, exchange_core(low)))
        gain_sums.append(gain_sum * share)
        return token

    token = middle_back_of(0, (token,))
    if final:
        token = sum_of(final, (token,))
    hops2 = sum2.send((token,))
    grad1 = []
    for i in seqs:
        grad, keep, send, token = attended_back(
            metas[i],
            lows[i],
            w1,
            kept[i],
            seg_cols[i],
            seg_rows[i],
            n1[i],
            attn_g,
            gain_sums[i],
            scale,
            chips,
            (i, seqs_dev, n_seqs),
            (token,),
        )
        grad1.append(grad)
        to_inputs.append((keep, exchange_core(send)))
        hops2 = sum2.send((token,))
        if i < final:
            token = middle_back_of(i + 1, (token,))
            block_out = [to_features(*pair, n_tensor, (token,)) for pair in downs]
    side = [to_features(*pair, n_tensor, (token,), 2) for pair in to_inputs]
    grad1, _ = gate(grad1, (got for _, came in block_out for got in came))
    sum1 = ring.scatter(grad1)
    hops1 = next(sum1)
    came = side[final][1]
    sent = [got for _, came in side for got in came]
    window = 0
    while not isinstance(hops1, jax.Array):
        latest = hops1
        hops1 = sum1.send((sent.pop(0),) if len(sent) > len(came) else ())
        window += 1
        if window == 1:
            block_out, _ = gate(block_out, latest)
        if window == 2:
            hops2 = sum2.send(latest)
        if window == 3:
            side[0], _ = gate(side[0], latest)
    while not isinstance(hops2, jax.Array):
        hops2 = sum2.send(())
    share1, share2 = hops1, hops2
    sums = share1[:, 4 * shard :]
    bit = 1
    while bit < n_tensor:
        sums = sums + butterfly(sums, "tensor", bit, n_tensor)
        bit *= 2
    small, _ = gate(small, (token,))
    marks = small[::rows, TEMB + 2 : TEMB + 2 + 2 * seqs_dev].astype(f32)
    times = (marks[:, 0::2] * 32 + marks[:, 1::2]).reshape(n_seqs)
    block_out, input_grad = (
        [kept + jnp.concatenate(came, axis=1).astype(f32) for kept, came in pairs]
        for pairs in (block_out, side)
    )
    block_out = jnp.concatenate(block_out).astype(bf16)
    input_grad = jnp.concatenate(input_grad)
    factor = float(n_seqs * seq_len) ** (-0.5)
    temb_all = sinusoid(times, TEMB)
    grad_time = (
        jnp.einsum("st,ds->td", temb_all, sums[:, :n_seqs], precision=lax.Precision.HIGHEST)
        * factor
    )

    def natural(value):
        return jnp.roll(value, core * half, axis=1)

    cols = 3 * shard
    return (
        natural(block_out),
        natural(input_grad),
        jnp.stack([share1[:, c * shard : (c + 1) * shard] for c in range(3)]) * factor,
        share1[:, cols : cols + shard].T * factor,
        share2[:, :hidden_dev] * factor,
        share2[:, hidden_dev:].T * factor,
        grad_time,
        sums[:, n_seqs] * factor,
        sums[:, n_seqs + 1] * factor,
    )


def solution(mesh):
    in_specs = (
        P("dp", None, None),
        P("dp", None),
        P("dp", None),
        P("dp"),
        P(None, "dp", "tensor"),
        P("tensor", "dp"),
        P("dp", "tensor"),
        P("tensor", "dp"),
        P(None, "dp"),
        P("dp"),
        P("dp"),
        P("dp", None, None),
    )
    out_specs = (
        P("dp", None, "tensor"),
        P("dp", None, "tensor"),
        P(None, "dp", "tensor"),
        P("tensor", "dp"),
        P("dp", "tensor"),
        P("tensor", "dp"),
        P(None, "dp"),
        P("dp"),
        P("dp"),
    )
    return jax.shard_map(shards, mesh=mesh, in_specs=in_specs, out_specs=out_specs, check_vma=False)
```

```python
import functools
import math

import jax
import jax.numpy as jnp
from jax import lax
from jax.experimental import pallas as pl
from jax.experimental.pallas import tpu as pltpu
from jax.sharding import PartitionSpec as P

HEADS = 16
TEMB = 256
BLOCK = 256
LANES = 128
FINE = 64
eps = 1e-05
masked = -1000000000.0
f32 = jnp.float32
bf16 = jnp.bfloat16
VMEM = pl.BlockSpec(memory_space=pltpu.VMEM)
SMEM = pl.BlockSpec(memory_space=pltpu.SMEM)
ANY = pl.BlockSpec(memory_space=pl.ANY)
HBM = pl.BlockSpec(memory_space=pltpu.HBM)


def params(mebibytes):
    return pltpu.CompilerParams(vmem_limit_bytes=mebibytes * 1024 * 1024)


def freqs(width):
    half = width // 2
    return jnp.exp(-math.log(10000.0) * jnp.arange(half, dtype=f32) / half)


def sinusoid(values, width):
    angles = values[..., None] * freqs(width)
    return jnp.concatenate([jnp.sin(angles), jnp.cos(angles)], axis=-1)


def norm_parts(hidden):
    centre = jnp.mean(hidden, axis=-1, keepdims=True)
    centred = hidden - centre
    spread = jnp.mean(centred * centred, axis=-1, keepdims=True)
    inv = lax.rsqrt(spread + eps)
    return centred * inv, inv


def norm_back(unit, inv, gain, grad):
    scaled = grad * gain
    first = jnp.mean(scaled, axis=-1, keepdims=True)
    second = jnp.mean(scaled * unit, axis=-1, keepdims=True)
    return inv * (scaled - first - unit * second)


def positions(segs, offsets):
    seq_len = segs.shape[0]
    index = jnp.arange(seq_len, dtype=jnp.int32)
    member = segs[:, None] == jnp.arange(offsets.shape[0], dtype=jnp.int32)[None, :]
    starts = jnp.min(jnp.where(member, index[:, None], seq_len), axis=0)
    start_tok = jnp.sum(jnp.where(member, starts[None, :], 0), axis=1)
    offset_tok = jnp.sum(jnp.where(member, offsets[None, :], 0), axis=1)
    return offset_tok + index - start_tok


def dot(left, right, left_dim, right_dim):
    return lax.dot_general(
        left, right, (((left_dim,), (right_dim,)), ((), ())), preferred_element_type=f32
    )


def like(shape, dtype):
    return jax.ShapeDtypeStruct(shape, dtype)


def rows_at(block):
    return pl.ds(pl.multiple_of(block * BLOCK, BLOCK), BLOCK)


def exchanged(core, block, blocks):
    return lax.rem(block + core * (blocks // 2), blocks)


def call(kernel, name, mebibytes, flops, outs, args, scratch=(), after=(), stored=(), direct=()):
    count, first, total = len(args), len(args) + len(after), len(outs)

    def body(*refs):
        results = list(refs[first : first + total])
        token = refs[first + total]
        rest = refs[first + total + 1 :]
        sems = rest[-1]
        copies = []

        def store(k, rows=slice(None)):
            mine = rest[stored.index(k)]
            copies.append(
                pltpu.make_async_copy(mine.at[rows], refs[first + k].at[rows], sems.at[len(copies)])
            )
            copies[-1].start()

        for at, k in enumerate(stored):
            results[k] = rest[at]
        extra = rest[len(stored) : -1]
        if stored:
            kernel(*refs[:count], *results, *extra, store=store)
        else:
            kernel(*refs[:count], *results, *extra)
        token[...] = jnp.zeros(token.shape, token.dtype)
        for copy in copies:
            copy.wait()

    moved = sum(a.size * a.dtype.itemsize for a in args) + sum(
        math.prod(o.shape) * o.dtype.itemsize for o in outs
    )
    return pl.pallas_call(
        body,
        out_shape=(
            *(
                pltpu.HBM(o.shape, o.dtype) if k in stored else o for k, o in enumerate(outs)
            ),
            like((8, LANES), f32),
        ),
        in_specs=[SMEM]
        + [HBM if k in direct else VMEM for k in range(1, count)]
        + [ANY] * len(after),
        out_specs=tuple(HBM if k in stored else VMEM for k in range(total)) + (VMEM,),
        scratch_shapes=[pltpu.VMEM(outs[k].shape, outs[k].dtype) for k in stored]
        + list(scratch)
        + [pltpu.SemaphoreType.DMA((8,))],
        compiler_params=params(mebibytes),
        cost_estimate=pl.CostEstimate(
            flops=flops // 1024, bytes_accessed=moved // 1024, transcendentals=0
        ),
        name=name,
    )(
        *(
            pltpu.with_memory_space_constraint(a, pltpu.HBM) if k in direct else a
            for k, a in enumerate(args)
        ),
        *after,
    )


def load(given, held, sems):
    copies = [
        pltpu.make_async_copy(ref, mine, sems.at[k])
        for k, (ref, mine) in enumerate(zip(given, held, strict=True))
    ]
    for copy in copies:
        copy.start()
    return lambda: copies.pop(0).wait()


def held_like(arrays):
    return [*(pltpu.VMEM(a.shape, a.dtype) for a in arrays), pltpu.SemaphoreType.DMA((len(arrays),))]


def pieces(table):
    first = table.astype(bf16)
    rest = table - first.astype(f32)
    second = rest.astype(bf16)
    return jnp.concatenate([first, second, (rest - second.astype(f32)).astype(bf16)], axis=0)


def embed_kernel(seqs, meta, inputs, place, freq, *refs, store):
    outs, held, sems = refs[:seqs], refs[seqs], refs[seqs + 1]
    copies = [pltpu.make_async_copy(inputs.at[i], held.at[i], sems.at[i]) for i in range(seqs)]
    for copy in copies:
        copy.start()
    seq_len = inputs.shape[1]
    half = freq.shape[1]
    blocks = seq_len // BLOCK
    step = lax.broadcasted_iota(jnp.int32, (FINE, half), 0).astype(f32)
    angles = (step * (FINE * freq[...]), step * freq[...])
    coarse, fine = (pieces(jnp.concatenate([jnp.sin(t), jnp.cos(t)], axis=1)) for t in angles)
    entry = lax.rem(lax.broadcasted_iota(jnp.int32, (BLOCK, 3 * FINE), 1), FINE)
    for i in range(seqs):

        def add(block, _, i=i):
            source = rows_at(exchanged(meta[0], block, blocks))
            at = place[i, source, :]
            a = dot((entry == at // FINE).astype(bf16), coarse, 1, 0)
            b = dot((entry == lax.rem(at, FINE)).astype(bf16), fine, 1, 0)
            sin_a, cos_a, sin_b, cos_b = a[:, :half], a[:, half:], b[:, :half], b[:, half:]
            x = held[i, source, :].astype(f32)
            outs[i][rows_at(block), :half] = x[:, :half] + (sin_a * cos_b + cos_a * sin_b)
            outs[i][rows_at(block), half:] = x[:, half:] + (cos_a * cos_b - sin_a * sin_b)
            return 0

        copies[i].wait()
        lax.fori_loop(0, blocks, add, 0)
        store(i)


def embedded(meta, inputs, place):
    seqs, seq_len, width = inputs.shape
    return call(
        functools.partial(embed_kernel, seqs),
        "embed",
        18,
        200 * inputs.size,
        (like((seq_len, width), f32),) * seqs,
        (meta, inputs, place[:, :, None], freqs(width)[None]),
        [pltpu.VMEM(inputs.shape, bf16), pltpu.SemaphoreType.DMA((seqs,))],
        stored=tuple(range(seqs)),
        direct=(1,),
    )


def window(meta, block, blocks):
    first, last = meta[2 + block], meta[2 + blocks + block]
    low, high = jnp.int32(blocks), jnp.int32(0)
    for j in range(blocks):
        hit = (meta[2 + blocks + j] >= first) & (meta[2 + j] <= last)
        low = jnp.where(hit & (low == blocks), j, low)
        high = jnp.where(hit, j + 1, high)
    return low, high - low


def set_bias(bias, seg_col, seg_row, block, low, count):
    keys = jnp.concatenate([seg_row[pl.ds(low + j, 1), :] for j in range(count)], axis=1)
    bias[:, : count * BLOCK] = jnp.where(seg_col[rows_at(block), :] == keys, 0.0, masked)


def project_kernel(shard, meta, entered, cond, gain, w1, h0, n1, qkv, inv, store):
    blocks = entered.shape[0] // BLOCK
    for block in range(blocks):
        rows = slice(block * BLOCK, (block + 1) * BLOCK)
        h = entered[rows, :] + cond[...]
        unit, scale = norm_parts(h)
        if block < blocks // 2:
            h0[rows, :] = h
        normed = (unit * gain[...]).astype(bf16)
        n1[rows, :] = normed
        inv[rows, LANES - 1 :] = scale
        terms = dot(normed, w1[:, : 3 * shard], 1, 0)
        qkv[rows_at(exchanged(meta[0], block, blocks)), :] = terms.astype(bf16)
        if block < blocks // 2:
            store(0, rows)
        store(1, rows)


def projected(meta, entered, cond, gain, w1, shard, after):
    seq_len, width = entered.shape
    return call(
        functools.partial(project_kernel, shard),
        "project",
        18,
        6 * seq_len * width * shard,
        (
            like((seq_len // 2, width), f32),
            like((seq_len, width), bf16),
            like((seq_len, 3 * shard), bf16),
            like((seq_len, LANES), f32),
        ),
        (meta, entered, cond, gain, w1),
        after=after,
        stored=(0, 1),
    )


def attend_kernel(shard, scale, meta, qkv, inv, seg_col, seg_row, a, lse, bias):
    seq_len = qkv.shape[0]
    blocks = seq_len // BLOCK
    lse[:, LANES - 1 :] = inv[:, LANES - 1 :]
    even = lax.broadcasted_iota(jnp.int32, (BLOCK, LANES), 1) < LANES // 2

    def attend(block, _):
        own = rows_at(exchanged(meta[0], block, blocks))
        low, count = window(meta, block, blocks)
        for size in range(1, blocks + 1):

            @pl.when(count == size)
            def _(size=size):
                span = size * BLOCK
                keys = pl.ds(pl.multiple_of(low * BLOCK, BLOCK), span)
                set_bias(bias, seg_col, seg_row, block, low, size)
                for pair in range(shard // LANES):
                    at = pair * LANES
                    query = qkv[rows_at(block), at : at + LANES] * jnp.bfloat16(scale)
                    key = qkv[keys, shard + at : shard + at + LANES]
                    value = qkv[keys, 2 * shard + at : 2 * shard + at + LANES]
                    outs = []
                    for e in range(2):
                        picked = jnp.where(even == (e == 0), query, jnp.bfloat16(0))
                        scores = dot(picked, key, 1, 1) + bias[:, :span]
                        top = jnp.max(scores, axis=1, keepdims=True)
                        expo = jnp.exp(scores - top)
                        denom = jnp.sum(expo, axis=1, keepdims=True)
                        outs.append(dot(expo.astype(bf16), value, 1, 0) * (1.0 / denom))
                        head = 2 * pair + e
                        lse[rows_at(block), head : head + 1] = top + jnp.log(denom)
                    a[own, at : at + LANES] = jnp.where(even, outs[0], outs[1]).astype(bf16)

        return 0

    lax.fori_loop(0, blocks, attend, 0)


def attended(meta, qkv, inv, seg_col, seg_row, shard, scale, after):
    seq_len = qkv.shape[0]
    return call(
        functools.partial(attend_kernel, shard, scale),
        "attend",
        10,
        8 * seq_len * seq_len * shard,
        (like((seq_len, shard), bf16), like((seq_len, LANES), f32)),
        (meta, qkv, inv, seg_col, seg_row),
        [pltpu.VMEM((BLOCK, seq_len), f32)],
        after,
    )


def out_kernel(meta, count, *refs):
    mixed, weights, keep, send = refs[:count], refs[count : 2 * count], refs[-2], refs[-1]
    half = keep.shape[0]
    for at in range(0, half, BLOCK):
        for base, out in ((half, send), (0, keep)):
            term = 0.0
            for a, w in zip(mixed, weights, strict=True):
                term = term + dot(a[base + at : base + at + BLOCK, :], w[...], 1, 1)
            out[at : at + BLOCK, :] = term.astype(out.dtype)


def projected_out(meta, mixed, weights, after):
    seq_len, shard = mixed[0].shape
    width = weights[0].shape[0]
    return call(
        lambda m, *refs: out_kernel(m, len(mixed), *refs),
        "project_out",
        7,
        2 * seq_len * width * shard * len(mixed),
        (like((seq_len // 2, width), bf16),) * 2,
        (meta, *mixed, *weights),
        after=after,
    )


def middle_kernel(meta, h0, keep, got, gain, h1, n2, inv, store):
    for at in range(0, keep.shape[0], BLOCK):
        rows = slice(at, at + BLOCK)
        h = h0[rows, :] + (keep[rows, :].astype(f32) + got[rows, :].astype(f32))
        unit, scale = norm_parts(h)
        inv[rows, :1] = scale
        h1[rows, :] = h
        n2[rows, :] = (unit * gain[...]).astype(bf16)
    store(0)


def middle(meta, h0, keep, got, gain, after):
    return call(
        middle_kernel,
        "middle",
        10,
        20 * keep.size,
        (like(keep.shape, f32), like(keep.shape, bf16), like((keep.shape[0], LANES), f32)),
        (meta, h0, keep, got, gain),
        after=after,
        stored=(0,),
    )


def split_features(core, term, keep, send):
    groups, _, part = keep.shape
    for g in range(groups):
        first = term[:, 2 * g * part : (2 * g + 1) * part]
        second = term[:, (2 * g + 1) * part : (2 * g + 2) * part]
        keep[g] = jnp.where(core == 0, first, second)
        send[g] = jnp.where(core == 0, second, first)


def halves_of(meta, half):
    own = pl.multiple_of(meta[0] * half, BLOCK)
    other = pl.multiple_of((1 - meta[0]) * half, BLOCK)
    return ((half, other), (0, own))


def hidden_start(meta, n2_own, n2_other, cot, w2, d_keep, d_send, act, d_hid):
    hid = w2.shape[1] // 2
    half = n2_own.shape[0]
    chunk = min(1024, hid)
    for (first, base), n2, d_n2 in zip(
        halves_of(meta, half), (n2_other, n2_own), (d_send, d_keep), strict=True
    ):
        for at in range(0, half, BLOCK):
            rows = slice(at, at + BLOCK)
            mine = slice(first + at, first + at + BLOCK)
            d_out = cot[pl.ds(base + at, BLOCK), :]
            for col in range(0, hid, chunk):
                u = dot(n2[rows, :], w2[:, col : col + chunk], 1, 0)
                d_act = dot(d_out, w2[:, hid + col : hid + col + chunk], 1, 0)
                cdf = 0.5 + 0.5 * lax.erf(u * (0.5**0.5))
                act[mine, col : col + chunk] = (u * cdf).astype(bf16)
                slope = cdf + u * (jnp.exp(-0.5 * u * u) * (0.5 / math.pi) ** 0.5)
                d_hid[mine, col : col + chunk] = (d_act * slope).astype(bf16)
            d_n2[rows, :] = dot(d_hid[mine, :], w2[:, :hid], 1, 1).astype(bf16)


def hidden_end(
    meta, n2_own, n2_other, cot, w2, h1, act, d_hid, grad, keep, send, held, sems, store, outs
):
    ready = load([h1], [held], sems)
    hid = w2.shape[1] // 2
    half, width = n2_own.shape
    chips = keep.shape[0]
    (_, other), (_, own) = halves_of(meta, half)
    for first in (half, 0):
        if first == 0:
            ready()
        for at in range(0, half, BLOCK):
            mine = slice(first + at, first + at + BLOCK)
            term = dot(act[mine, :], w2[:, hid:], 1, 1)
            if first == 0:
                term = term + held[mine, :] * (1.0 / chips)
            split_features(meta[0], term.astype(bf16), keep.at[:, mine, :], send.at[:, mine, :])
    store(outs + 1)
    store(outs + 2)
    for at in range(0, width, BLOCK):
        cols = slice(at, at + BLOCK)
        up = dot(n2_own[:, cols], d_hid[:half, :], 0, 0)
        up = up + dot(n2_other[:, cols], d_hid[half:, :], 0, 0)
        grad[cols, :hid] = up.astype(bf16)
        down = dot(cot[pl.ds(own, half), cols], act[:half, :], 0, 0)
        down = down + dot(cot[pl.ds(other, half), cols], act[half:, :], 0, 0)
        grad[cols, hid:] = down.astype(bf16)
        store(outs, cols)


def hidden_layer(meta, n2, cot, w2, h1, chips, after, part=None):
    half, width = n2[0].shape
    hid = w2.shape[1] // 2
    split = like((chips, 2 * half, width // (2 * chips)), bf16)
    d_n2 = like((half, width), bf16)
    kept = like((2 * half, hid), bf16)
    late = (like((width, 2 * hid), bf16), split, split)
    if part is None:

        def kernel(meta, own, other, cot, w2, h1, *refs, store):
            (d_keep, d_send, *ends), act, d_hid, held, sems = refs[:5], *refs[5:]
            hidden_start(meta, own, other, cot, w2, d_keep, d_send, act, d_hid)
            hidden_end(
                meta, own, other, cot, w2, h1, act, d_hid, *ends, held, sems, store, 2
            )

        scratch = [*(pltpu.VMEM(kept.shape, bf16) for _ in range(2)), *held_like([h1])]
        return call(
            kernel,
            "hidden_layer",
            28,
            24 * half * width * hid,
            (d_n2, d_n2, *late),
            (meta, *n2, cot, w2, h1),
            scratch,
            after,
            (2, 3, 4),
            (5,),
        )
    if part == ():
        return call(
            hidden_start,
            "hidden_start",
            20,
            12 * half * width * hid,
            (d_n2, d_n2, kept, kept),
            (meta, *n2, cot, w2),
            after=after,
        )
    return call(
        lambda *refs, store: hidden_end(*refs, store, 0),
        "hidden_end",
        28,
        12 * half * width * hid,
        late,
        (meta, *n2, cot, w2, h1, *part),
        held_like([h1]),
        after,
        (0, 1, 2),
        (5,),
    )


def middle_back_kernel(meta, low, got, n2, inv1, cot, gain, d_low, sums):
    half = n2.shape[0]
    base = pl.multiple_of(meta[0] * half, BLOCK)
    ungain = 1.0 / gain[...]
    total = jnp.zeros(sums.shape, f32)
    for at in range(0, half, BLOCK):
        rows = slice(at, at + BLOCK)
        d_n2 = low[rows, :].astype(f32) + got[rows, :].astype(f32)
        unit = n2[rows, :].astype(f32) * ungain
        total = total + jnp.sum(d_n2 * unit, axis=0, keepdims=True)
        d_h = norm_back(unit, inv1[rows, :1], gain[...], d_n2)
        d_h = d_h + cot[pl.ds(base + at, BLOCK), :].astype(f32)
        d_low[rows, :] = d_h.astype(bf16)
    sums[...] = total


def middle_back(meta, low, got, n2, inv1, cot, gain, after):
    return call(
        middle_back_kernel,
        "middle_back",
        12,
        30 * n2.size,
        (like(n2.shape, bf16), like((1, n2.shape[1]), f32)),
        (meta, low, got, n2, inv1, cot, gain),
        after=after,
    )


def attend_back_kernel(
    shard,
    scale,
    seq,
    seqs,
    n_seqs,
    meta,
    low_own,
    low_other,
    w1,
    qkv,
    a,
    lse,
    seg_col,
    seg_row,
    n1,
    gain,
    gain_sum,
    grads,
    keep,
    send,
    d_mix,
    total,
    bias,
    d_qkv,
    *loads,
    store,
):
    ready = load((qkv, lse, n1), loads[:-1], loads[-1])
    qkv, lse, n1 = loads[:-1]
    seq_len = a.shape[0]
    blocks = seq_len // BLOCK
    per = blocks // 2
    for block in range(per):
        w_out_t = w1[:, 3 * shard : 4 * shard]
        rows = slice(block * BLOCK, (block + 1) * BLOCK)
        d_mix[rows, :] = dot(low_own[rows, :], w_out_t, 1, 0).astype(bf16)
        after = slice((block + per) * BLOCK, (block + per + 1) * BLOCK)
        d_mix[after, :] = dot(low_other[rows, :], w_out_t, 1, 0).astype(bf16)
    ready()
    ready()
    total[...] = jnp.zeros(total.shape, f32)
    even = lax.broadcasted_iota(jnp.int32, (BLOCK, LANES), 1) < LANES // 2

    def attend(block, _):
        own = rows_at(exchanged(meta[0], block, blocks))
        low, count = window(meta, block, blocks)
        for size in range(1, blocks + 1):

            @pl.when(count == size)
            def _(size=size):
                span = size * BLOCK
                keys = pl.ds(pl.multiple_of(low * BLOCK, BLOCK), span)
                set_bias(bias, seg_col, seg_row, block, low, size)
                for pair in range(shard // LANES):
                    at = pair * LANES
                    query = qkv[rows_at(block), at : at + LANES] * jnp.bfloat16(scale)
                    key = qkv[keys, shard + at : shard + at + LANES]
                    value = qkv[keys, 2 * shard + at : 2 * shard + at + LANES]
                    grad = d_mix[own, at : at + LANES]
                    product = grad.astype(f32) * a[own, at : at + LANES].astype(f32)
                    d_query = []
                    d_key = d_value = 0.0
                    for e in range(2):
                        side = even == (e == 0)
                        picked = jnp.where(side, query, jnp.bfloat16(0))
                        picked_grad = jnp.where(side, grad, jnp.bfloat16(0))
                        delta = jnp.sum(jnp.where(side, product, 0.0), axis=1, keepdims=True)
                        head = 2 * pair + e
                        scores = dot(picked, key, 1, 1) + bias[:, :span]
                        probs = jnp.exp(scores - lse[rows_at(block), head : head + 1])
                        d_probs = dot(picked_grad, value, 1, 1)
                        d_scores = (probs * (d_probs - delta)).astype(bf16)
                        d_query.append(dot(d_scores, key, 1, 0))
                        d_key = d_key + dot(d_scores, picked, 0, 0)
                        d_value = d_value + dot(probs.astype(bf16), picked_grad, 0, 0)
                    total[keys, at : at + LANES] += d_key
                    total[keys, shard + at : shard + at + LANES] += d_value
                    d_qkv[own, at : at + LANES] = (
                        jnp.where(even, d_query[0], d_query[1]) * scale
                    ).astype(bf16)

        return 0

    lax.fori_loop(0, blocks, attend, 0)
    share = 1.0 / keep.shape[0]
    unit_sum = term_sum = jnp.zeros((1, n1.shape[1]), f32)
    ungain = 1.0 / gain[...]
    ready()
    for block in range(blocks):
        rows = slice(block * BLOCK, (block + 1) * BLOCK)
        d_qkv[rows, shard:] = total[rows_at(exchanged(meta[0], block, blocks)), :].astype(bf16)
        d_n1 = dot(d_qkv[rows, :], w1[:, : 3 * shard], 1, 1)
        unit = n1[rows, :].astype(f32) * ungain
        inv = lse[rows, LANES - 1 :]
        unit_sum = unit_sum + jnp.sum(d_n1 * unit, axis=0, keepdims=True)
        term = norm_back(unit, inv, gain[...], d_n1)
        if block < per:
            term = term + share * low_own[rows, :].astype(f32)
        term_sum = term_sum + jnp.sum(term, axis=0, keepdims=True)
        split_features(meta[0], term.astype(bf16), keep.at[:, rows, :], send.at[:, rows, :])
    row = lax.broadcasted_iota(jnp.int32, (LANES, n1.shape[1]), 0)
    table = jnp.where(row == meta[1] * seqs + seq, term_sum, 0.0)
    table = jnp.where(row == n_seqs, unit_sum, table)
    table = jnp.where(row == n_seqs + 1, gain_sum[...], table)
    grads[:, 4 * shard :] = table.T.astype(bf16)
    store(1)
    store(2)
    half = low_own.shape[0]
    for at in range(0, n1.shape[1], BLOCK):
        cols = slice(at, at + BLOCK)
        grads[cols, : 3 * shard] = dot(n1[:, cols], d_qkv[...], 0, 0).astype(bf16)
        proj = dot(low_own[:, cols], a[:half, :], 0, 0)
        proj = proj + dot(low_other[:, cols], a[half:, :], 0, 0)
        grads[cols, 3 * shard : 4 * shard] = proj.astype(bf16)
        store(0, cols)


def attended_back(
    meta, low, w1, kept, seg_col, seg_row, n1, gain, gain_sum, scale, groups, place, after
):
    qkv, a, lse = kept
    seq_len, shard = a.shape
    width = w1.shape[0]
    split = like((groups, seq_len, width // (2 * groups)), bf16)
    return call(
        functools.partial(attend_back_kernel, shard, scale, *place),
        "attend_back",
        36,
        16 * seq_len * width * shard + 20 * seq_len * seq_len * shard,
        (like((width, 4 * shard + LANES), bf16), split, split),
        (meta, *low, w1, qkv, a, lse, seg_col, seg_row, n1, gain, gain_sum),
        [
            pltpu.VMEM((seq_len, shard), bf16),
            pltpu.VMEM((seq_len, 2 * shard), f32),
            pltpu.VMEM((BLOCK, seq_len), f32),
            pltpu.VMEM((seq_len, 3 * shard), bf16),
            *held_like((qkv, lse, n1)),
        ],
        after,
        (0, 1, 2),
        (4, 6, 9),
    )


def assemble_kernel(spots, *refs):
    come, full, sems = refs[:-2], refs[-2], refs[-1]
    copies = []
    for k, ref in enumerate(come):
        rows = ref.shape[0]
        at = pl.ds(pl.multiple_of(spots[k], rows), rows)
        copies.append(pltpu.make_async_copy(ref, full.at[at, :], sems.at[k]))
    for copy in copies:
        copy.start()
    for copy in copies:
        copy.wait()


def assembled(spots, come):
    rows, cols = sum(c.shape[0] for c in come), come[0].shape[1]
    return pl.pallas_call(
        assemble_kernel,
        out_shape=like((rows, cols), come[0].dtype),
        in_specs=[SMEM] + [HBM] * len(come),
        out_specs=ANY,
        scratch_shapes=[pltpu.SemaphoreType.DMA((len(come),))],
        compiler_params=params(2),
        cost_estimate=pl.CostEstimate(
            flops=0, bytes_accessed=rows * cols // 16, transcendentals=0
        ),
        name="assemble",
    )(spots, *(pltpu.with_memory_space_constraint(c, pltpu.HBM) for c in come))


def pack_kernel(seqs, times, *refs):
    given, first, second, held, sems = refs[:6], refs[6], refs[7], refs[8:-1], refs[-1]
    copies = [
        pltpu.make_async_copy(ref, mine, sems.at[k])
        for k, (ref, mine) in enumerate(zip(given, held, strict=True))
    ]
    for copy in copies:
        copy.start()
    for copy in copies:
        copy.wait()
    w_qkv, w_out, w_time, w_up, w_down, gains = held
    shard = w_qkv.shape[2]
    rows = first.shape[0]
    for c in range(3):
        first[:, c * shard : (c + 1) * shard] = w_qkv[c]
    at = 3 * shard
    for block in (w_out, w_time):
        first[:, at : at + block.shape[0]] = block[...].astype(f32).T.astype(bf16)
        at += block.shape[0]
    row = lax.broadcasted_iota(jnp.int32, (LANES, rows), 0)
    marks = jnp.zeros((LANES, rows), f32)
    for k in range(2):
        marks = jnp.where(row == k, gains[k : k + 1, :].astype(f32), marks)
    for i in range(seqs):
        for k, part in enumerate((times[i] // 32, lax.rem(times[i], 32))):
            marks = jnp.where(row == 2 + 2 * i + k, part.astype(f32), marks)
    first[:, at:] = marks.T.astype(bf16)
    hid = w_up.shape[1]
    second[:, :hid] = w_up[...]
    second[:, hid:] = w_down[...].astype(f32).T.astype(bf16)


def packed(times, *given):
    w_qkv, w_out, w_time, w_up, _, _ = given
    rows = w_up.shape[0]
    cols = 3 * w_qkv.shape[2] + w_out.shape[0] + w_time.shape[0] + LANES
    return call(
        functools.partial(pack_kernel, times.shape[0]),
        "pack",
        8,
        0,
        (like((rows, cols), bf16), like((rows, 2 * w_up.shape[1]), bf16)),
        (times, *given),
        [*(pltpu.VMEM(g.shape, g.dtype) for g in given), pltpu.SemaphoreType.DMA((len(given),))],
        direct=tuple(range(1, 1 + len(given))),
    )


class Ring:
    def __init__(self, n):
        self.n = n
        me = lax.axis_index("dp")
        spot = jnp.where(me & 1 == 0, me >> 1, n - 1 - (me >> 1))
        order = list(range(0, n, 2)) + list(range(n - 1, 0, -2))
        self.right = [(order[p], order[(p + 1) % n]) for p in range(n)]
        self.left = [(b, a) for a, b in self.right]

        def at(offset):
            there = spot + offset
            there = jnp.where(there >= n, there - n, jnp.where(there < 0, there + n, there))
            return jnp.where(there < n // 2, 2 * there, 2 * (n - 1 - there) + 1)

        self.near = tuple(at(k) for k in range(1 - n // 2, n // 2 + 1))

    def at(self, offset):
        return self.near[offset + self.n // 2 - 1]

    def gather(self, block):
        n, rows = self.n, block.shape[0]
        come, spots = [block], [self.at(0) * rows]
        from_left = from_right = block
        waited = yield ()
        for hop in range(1, n // 2):
            from_left = lax.ppermute(from_left, "dp", self.right)
            from_right = lax.ppermute(from_right, "dp", self.left)
            waited = yield (from_left, from_right), waited
            (from_left, from_right), waited = gate((from_left, from_right), waited)
            come += [from_left, from_right]
            spots += [self.at(-hop) * rows, self.at(hop) * rows]
        come.append(lax.ppermute(from_left[: rows // 2], "dp", self.right))
        come.append(lax.ppermute(from_right[rows // 2 :], "dp", self.left))
        farthest = self.at(n // 2) * rows
        spots += [farthest, farthest + rows // 2]
        yield tuple(come[-2:]), waited
        yield assembled(jnp.stack(spots).astype(jnp.int32), come)

    def scatter(self, terms):
        n, rows = self.n, terms[0].shape[0] // self.n

        def whole(offset, at, size):
            parts = [
                lax.dynamic_slice_in_dim(t, self.at(offset) * rows + at, size, 0) for t in terms
            ]
            return sum(p.astype(f32) for p in parts)

        def part(offset, at=0, size=rows):
            return whole(offset, at, size).astype(bf16)

        def plus(run, offset, at=0, size=rows):
            return (run.astype(f32) + whole(offset, at, size)).astype(bf16)

        half = rows // 2
        right, left = part(n // 2, 0, half), part(n // 2, half, half)
        for hop in range(1, n // 2 + 1):
            right = lax.ppermute(right, "dp", self.right)
            left = lax.ppermute(left, "dp", self.left)
            waited = yield (right, left)
            (right, left), _ = gate((right, left), waited)
            if hop == 1:
                rest = n // 2 - 1
                right = jnp.concatenate([plus(right, rest, 0, half), part(rest, half, half)])
                left = jnp.concatenate([part(-rest, 0, half), plus(left, -rest, half, half)])
            elif hop < n // 2:
                right = plus(right, n // 2 - hop)
                left = plus(left, hop - n // 2)
        yield whole(0, 0, rows) + right.astype(f32) + left.astype(f32)


def butterfly(value, axis, bit, n):
    return lax.ppermute(value, axis, [(i, i ^ bit) for i in range(n)])


def gate(values, waited):
    return lax.optimization_barrier((values, tuple(waited)))


def swap(value, bit, n):
    return lax.ppermute(value, "tensor", [(i, i ^ bit) for i in range(n)])


def to_features(keep, got, n, waited, pieces=1):
    chip = lax.axis_index("tensor") // 2
    half = keep.shape[1] // 2
    (keep, got), _ = gate((keep, got), waited)
    got = jnp.concatenate([got[:, half:], got[:, :half]], axis=1)
    kept, came = keep, [got]
    bit = 1
    while 2 * bit < n:
        value = kept.astype(f32) + jnp.concatenate(came, axis=1).astype(f32)
        value = value.reshape((-1, 2) + keep.shape[1:])
        mine = (chip // bit) % 2
        kept = lax.dynamic_index_in_dim(value, mine, 1, keepdims=False)
        sent = lax.dynamic_index_in_dim(value, 1 - mine, 1, keepdims=False).astype(bf16)
        bit *= 2
        parts = pieces if 2 * bit >= n else 1
        came = [swap(p, bit, n) for p in jnp.split(sent, parts, axis=1)]
    return kept, came


def shards(
    inputs,
    segment_ids,
    doc_offsets,
    time_index,
    w_qkv,
    w_out,
    w_up,
    w_down,
    w_time,
    gain_attn,
    gain_mlp,
    cotangent,
):
    n_dp = lax.axis_size("dp")
    n_tensor = lax.axis_size("tensor")
    me_dp = lax.axis_index("dp")
    core = lax.axis_index("tensor") % 2
    chips = n_tensor // 2
    seqs_dev, seq_len, width = inputs.shape
    half = seq_len // 2
    blocks = seq_len // BLOCK
    shard = width // n_tensor
    scale = (width // HEADS) ** (-0.5)
    hidden_dev = w_up.shape[1]
    rows = width // n_dp
    n_seqs = n_dp * seqs_dev
    ring = Ring(n_dp)
    seqs = range(seqs_dev)

    metas, seg_cols, seg_rows, places = [], [], [], []
    for i in seqs:
        ids = segment_ids[i]
        metas.append(
            jnp.concatenate(
                [
                    jnp.stack([core, me_dp]).astype(jnp.int32),
                    ids[::BLOCK],
                    ids[BLOCK - 1 :: BLOCK],
                ]
            )
        )
        seg_cols.append(ids[:, None])
        seg_rows.append(ids.reshape(blocks, BLOCK))
        places.append(positions(ids, doc_offsets[i]))
    w1_part, w2_part, _ = packed(
        time_index, w_qkv, w_out, w_time, w_up, w_down, jnp.stack([gain_attn, gain_mlp])
    )
    *entered, _ = embedded(metas[0], inputs, jnp.stack(places))
    cot = [cotangent[i] for i in seqs]
    gather1 = ring.gather(w1_part)
    next(gather1)
    brought, passed = [gather1.send(())[0]], []
    beside = [(*seg_cols, *seg_rows, *cot, *ring.near, *metas), tuple(entered)]
    while not isinstance(w1 := gather1.send(beside.pop(0) if beside else ()), jax.Array):
        brought.append(w1[0])
        passed.append(w1[1])
    early, entered = passed[:2]
    seg_cols, seg_rows, cot = (early[k * seqs_dev : (k + 1) * seqs_dev] for k in range(3))
    ring.near = early[3 * seqs_dev : -seqs_dev]
    metas = early[-seqs_dev:]
    w2_part, _ = gate(w2_part, brought[-2][:1])
    gather2 = ring.gather(w2_part)
    next(gather2)
    brought2 = [gather2.send(())[0]]
    small = w1[:, 4 * shard :]
    temb = sinusoid(time_index.astype(f32), TEMB)
    cond = jnp.sum(temb[:, None, :] * small[None, :, :TEMB].astype(f32), axis=2)
    attn_g = small[:, TEMB].astype(f32)[None]
    mlp_g = small[:, TEMB + 1].astype(f32)[None]
    def exchange_core(value):
        return swap(value, 1, n_tensor)

    def gather_chips(value):
        values = [value]
        bit = 2
        while bit < n_tensor:
            values = values + [swap(v, bit, n_tensor) for v in values]
            bit *= 2
        return values

    def sum_chips(value):
        bit = 2
        low, got = value.astype(bf16), jnp.zeros_like(value, bf16)
        while bit < n_tensor:
            low = (low.astype(f32) + got.astype(f32)).astype(bf16)
            got = swap(low, bit, n_tensor)
            bit *= 2
        return low, got

    h0, n1, kept, h1, inv1, n2 = [], [], [], [], [], []
    w_outs = gather_chips(w1[:, 3 * shard : 4 * shard])
    while not isinstance(w2 := gather2.send(()), jax.Array):
        brought2.append(w2[0])
    brought2 = brought2[-4:]
    after = ()
    for i in seqs:
        h, n, qkv, inv, token = projected(
            metas[i], entered[i], cond[i : i + 1], attn_g, w1, shard, after
        )
        a, lse, token = attended(
            metas[i],
            qkv,
            inv,
            seg_cols[i],
            seg_rows[i],
            shard,
            scale,
            (token, *(brought2[i] if i < 2 else ())),
        )
        after = (token, *w_outs[1:])
        h0.append(h)
        n1.append(n)
        kept.append((qkv, a, lse))
    mixes = [gather_chips(k[1]) for k in kept]
    outs, terms, d_n2, grad2, downs = [], [], [], [], []
    share = 1.0 / chips
    final = seqs_dev - 1

    def out_of(i, after):
        keep, send, token = projected_out(metas[i], mixes[i], w_outs, after)
        outs.append((keep, exchange_core(send)))
        return token

    def middle_of(i, after):
        h, own, inv, token = middle(metas[i], h0[i], *outs[i], mlp_g, after)
        inv1.append(inv)
        h1.append(h)
        n2.append((own, exchange_core(own)))
        return token

    def hidden_of(i, after):
        given = (metas[i], n2[i], cot[i], w2, h1[i], chips)
        if i < final:
            d_keep, d_send, *rest, token = hidden_layer(*given, after, ())
        else:
            d_keep, d_send, *rest, token = hidden_layer(*given, after)
        terms.append((d_keep, exchange_core(d_send)))
        return token, rest

    def rest_of(i, rest, after):
        token = after[0]
        if i < final:
            *rest, token = hidden_layer(
                metas[i], n2[i], cot[i], w2, h1[i], chips, after, tuple(rest)
            )
        grad, keep, send = rest
        grad2.append(grad)
        downs.append((keep, exchange_core(send)))
        return token

    def sum_of(i, after):
        (keep, got), _ = gate(terms[i], after)
        d_n2.append(sum_chips(keep.astype(f32) + got.astype(f32)))
        return d_n2[i][0]

    for i in seqs:
        token = out_of(i, (token, *(brought2[2] if i == 0 else ())))
    for i in seqs:
        token = middle_of(i, (token, *(brought2[3] if i == 0 else ())))
    for i in seqs:
        token, rest = hidden_of(i, (token,))
        if i < final:
            token = sum_of(i, (token,))
        token = rest_of(i, rest, (token,))
    grad2, _ = gate(grad2, (got for _, got in d_n2))
    sum2 = ring.scatter(grad2)
    hops2 = next(sum2)
    gain_sums, to_inputs, lows = [], [], []

    def middle_back_of(i, after):
        low, gain_sum, token = middle_back(
            metas[i], *d_n2[i], n2[i][0], inv1[i], cot[i], mlp_g, after
        )
        lows.append((low, exchange_core(low)))
        gain_sums.append(gain_sum * share)
        return token

    token = middle_back_of(0, (token,))
    if final:
        token = sum_of(final, (token,))
    hops2 = sum2.send((token,))
    grad1 = []
    for i in seqs:
        grad, keep, send, token = attended_back(
            metas[i],
            lows[i],
            w1,
            kept[i],
            seg_cols[i],
            seg_rows[i],
            n1[i],
            attn_g,
            gain_sums[i],
            scale,
            chips,
            (i, seqs_dev, n_seqs),
            (token,),
        )
        grad1.append(grad)
        to_inputs.append((keep, exchange_core(send)))
        hops2 = sum2.send((token,))
        if i < final:
            token = middle_back_of(i + 1, (token,))
            block_out = [to_features(*pair, n_tensor, (token,)) for pair in downs]
    side = [to_features(*pair, n_tensor, (token,), 2) for pair in to_inputs]
    grad1, _ = gate(grad1, (got for _, came in block_out for got in came))
    sum1 = ring.scatter(grad1)
    hops1 = next(sum1)
    came = side[final][1]
    sent = [got for _, came in side for got in came]
    window = 0
    while not isinstance(hops1, jax.Array):
        latest = hops1
        hops1 = sum1.send((sent.pop(0),) if len(sent) > len(came) else ())
        window += 1
        if window == 1:
            block_out, _ = gate(block_out, latest)
        if window == 2:
            hops2 = sum2.send(latest)
        if window == 3:
            side[0], _ = gate(side[0], latest)
    while not isinstance(hops2, jax.Array):
        hops2 = sum2.send(())
    share1, share2 = hops1, hops2
    sums = share1[:, 4 * shard :]
    bit = 1
    while bit < n_tensor:
        sums = sums + butterfly(sums, "tensor", bit, n_tensor)
        bit *= 2
    small, _ = gate(small, (token,))
    marks = small[::rows, TEMB + 2 : TEMB + 2 + 2 * seqs_dev].astype(f32)
    times = (marks[:, 0::2] * 32 + marks[:, 1::2]).reshape(n_seqs)
    block_out, input_grad = (
        [kept + jnp.concatenate(came, axis=1).astype(f32) for kept, came in pairs]
        for pairs in (block_out, side)
    )
    block_out = jnp.concatenate(block_out).astype(bf16)
    input_grad = jnp.concatenate(input_grad)
    factor = float(n_seqs * seq_len) ** (-0.5)
    temb_all = sinusoid(times, TEMB)
    grad_time = (
        jnp.einsum("st,ds->td", temb_all, sums[:, :n_seqs], precision=lax.Precision.HIGHEST)
        * factor
    )

    def natural(value):
        return jnp.roll(value, core * half, axis=1)

    cols = 3 * shard
    return (
        natural(block_out),
        natural(input_grad),
        jnp.stack([share1[:, c * shard : (c + 1) * shard] for c in range(3)]) * factor,
        share1[:, cols : cols + shard].T * factor,
        share2[:, :hidden_dev] * factor,
        share2[:, hidden_dev:].T * factor,
        grad_time,
        sums[:, n_seqs] * factor,
        sums[:, n_seqs + 1] * factor,
    )


def solution(mesh):
    in_specs = (
        P("dp", None, None),
        P("dp", None),
        P("dp", None),
        P("dp"),
        P(None, "dp", "tensor"),
        P("tensor", "dp"),
        P("dp", "tensor"),
        P("tensor", "dp"),
        P(None, "dp"),
        P("dp"),
        P("dp"),
        P("dp", None, None),
    )
    out_specs = (
        P("dp", None, "tensor"),
        P("dp", None, "tensor"),
        P(None, "dp", "tensor"),
        P("tensor", "dp"),
        P("dp", "tensor"),
        P("tensor", "dp"),
        P(None, "dp"),
        P("dp"),
        P("dp"),
    )
    return jax.shard_map(shards, mesh=mesh, in_specs=in_specs, out_specs=out_specs, check_vma=False)
```

```python
import functools
import math

import jax
import jax.numpy as jnp
from jax import lax
from jax.experimental import pallas as pl
from jax.experimental.pallas import tpu as pltpu
from jax.sharding import PartitionSpec as P

HEADS = 16
TEMB = 256
BLOCK = 256
LANES = 128
FINE = 64
eps = 1e-05
masked = -1000000000.0
f32 = jnp.float32
bf16 = jnp.bfloat16
VMEM = pl.BlockSpec(memory_space=pltpu.VMEM)
SMEM = pl.BlockSpec(memory_space=pltpu.SMEM)
ANY = pl.BlockSpec(memory_space=pl.ANY)
HBM = pl.BlockSpec(memory_space=pltpu.HBM)


def params(mebibytes):
    return pltpu.CompilerParams(vmem_limit_bytes=mebibytes * 1024 * 1024)


def freqs(width):
    half = width // 2
    return jnp.exp(-math.log(10000.0) * jnp.arange(half, dtype=f32) / half)


def sinusoid(values, width):
    angles = values[..., None] * freqs(width)
    return jnp.concatenate([jnp.sin(angles), jnp.cos(angles)], axis=-1)


def norm_parts(hidden):
    centre = jnp.mean(hidden, axis=-1, keepdims=True)
    centred = hidden - centre
    spread = jnp.mean(centred * centred, axis=-1, keepdims=True)
    inv = lax.rsqrt(spread + eps)
    return centred * inv, inv


def norm_back(unit, inv, gain, grad):
    scaled = grad * gain
    first = jnp.mean(scaled, axis=-1, keepdims=True)
    second = jnp.mean(scaled * unit, axis=-1, keepdims=True)
    return inv * (scaled - first - unit * second)


def positions(segs, offsets):
    seq_len = segs.shape[0]
    index = jnp.arange(seq_len, dtype=jnp.int32)
    member = segs[:, None] == jnp.arange(offsets.shape[0], dtype=jnp.int32)[None, :]
    starts = jnp.min(jnp.where(member, index[:, None], seq_len), axis=0)
    start_tok = jnp.sum(jnp.where(member, starts[None, :], 0), axis=1)
    offset_tok = jnp.sum(jnp.where(member, offsets[None, :], 0), axis=1)
    return offset_tok + index - start_tok


def dot(left, right, left_dim, right_dim):
    return lax.dot_general(
        left, right, (((left_dim,), (right_dim,)), ((), ())), preferred_element_type=f32
    )


def like(shape, dtype):
    return jax.ShapeDtypeStruct(shape, dtype)


def rows_at(block):
    return pl.ds(pl.multiple_of(block * BLOCK, BLOCK), BLOCK)


def exchanged(core, block, blocks):
    return lax.rem(block + core * (blocks // 2), blocks)


def call(kernel, name, mebibytes, flops, outs, args, scratch=(), after=(), stored=(), direct=()):
    count, first, total = len(args), len(args) + len(after), len(outs)

    def body(*refs):
        results = list(refs[first : first + total])
        token = refs[first + total]
        rest = refs[first + total + 1 :]
        sems = rest[-1]
        copies = []

        def store(k, rows=slice(None)):
            mine = rest[stored.index(k)]
            copies.append(
                pltpu.make_async_copy(mine.at[rows], refs[first + k].at[rows], sems.at[len(copies)])
            )
            copies[-1].start()

        for at, k in enumerate(stored):
            results[k] = rest[at]
        extra = rest[len(stored) : -1]
        if stored:
            kernel(*refs[:count], *results, *extra, store=store)
        else:
            kernel(*refs[:count], *results, *extra)
        token[...] = jnp.zeros(token.shape, token.dtype)
        for copy in copies:
            copy.wait()

    moved = sum(a.size * a.dtype.itemsize for a in args) + sum(
        math.prod(o.shape) * o.dtype.itemsize for o in outs
    )
    return pl.pallas_call(
        body,
        out_shape=(
            *(
                pltpu.HBM(o.shape, o.dtype) if k in stored else o for k, o in enumerate(outs)
            ),
            like((8, LANES), f32),
        ),
        in_specs=[SMEM]
        + [HBM if k in direct else VMEM for k in range(1, count)]
        + [ANY] * len(after),
        out_specs=tuple(HBM if k in stored else VMEM for k in range(total)) + (VMEM,),
        scratch_shapes=[pltpu.VMEM(outs[k].shape, outs[k].dtype) for k in stored]
        + list(scratch)
        + [pltpu.SemaphoreType.DMA((8,))],
        compiler_params=params(mebibytes),
        cost_estimate=pl.CostEstimate(
            flops=flops // 1024, bytes_accessed=moved // 1024, transcendentals=0
        ),
        name=name,
    )(
        *(
            pltpu.with_memory_space_constraint(a, pltpu.HBM) if k in direct else a
            for k, a in enumerate(args)
        ),
        *after,
    )


def load(given, held, sems):
    copies = [
        pltpu.make_async_copy(ref, mine, sems.at[k])
        for k, (ref, mine) in enumerate(zip(given, held, strict=True))
    ]
    for copy in copies:
        copy.start()
    return lambda: copies.pop(0).wait()


def held_like(arrays):
    return [*(pltpu.VMEM(a.shape, a.dtype) for a in arrays), pltpu.SemaphoreType.DMA((len(arrays),))]


def pieces(table):
    first = table.astype(bf16)
    rest = table - first.astype(f32)
    second = rest.astype(bf16)
    return jnp.concatenate([first, second, (rest - second.astype(f32)).astype(bf16)], axis=0)


def embed_kernel(seqs, meta, inputs, place, freq, *refs, store):
    outs, held, sems = refs[:seqs], refs[seqs], refs[seqs + 1]
    copies = [pltpu.make_async_copy(inputs.at[i], held.at[i], sems.at[i]) for i in range(seqs)]
    for copy in copies:
        copy.start()
    seq_len = inputs.shape[1]
    half = freq.shape[1]
    blocks = seq_len // BLOCK
    step = lax.broadcasted_iota(jnp.int32, (FINE, half), 0).astype(f32)
    angles = (step * (FINE * freq[...]), step * freq[...])
    coarse, fine = (pieces(jnp.concatenate([jnp.sin(t), jnp.cos(t)], axis=1)) for t in angles)
    entry = lax.rem(lax.broadcasted_iota(jnp.int32, (BLOCK, 3 * FINE), 1), FINE)
    for i in range(seqs):

        def add(block, _, i=i):
            source = rows_at(exchanged(meta[0], block, blocks))
            at = place[i, source, :]
            a = dot((entry == at // FINE).astype(bf16), coarse, 1, 0)
            b = dot((entry == lax.rem(at, FINE)).astype(bf16), fine, 1, 0)
            sin_a, cos_a, sin_b, cos_b = a[:, :half], a[:, half:], b[:, :half], b[:, half:]
            x = held[i, source, :].astype(f32)
            outs[i][rows_at(block), :half] = x[:, :half] + (sin_a * cos_b + cos_a * sin_b)
            outs[i][rows_at(block), half:] = x[:, half:] + (cos_a * cos_b - sin_a * sin_b)
            return 0

        copies[i].wait()
        lax.fori_loop(0, blocks, add, 0)
        store(i)


def embedded(meta, inputs, place):
    seqs, seq_len, width = inputs.shape
    return call(
        functools.partial(embed_kernel, seqs),
        "embed",
        18,
        200 * inputs.size,
        (like((seq_len, width), f32),) * seqs,
        (meta, inputs, place[:, :, None], freqs(width)[None]),
        [pltpu.VMEM(inputs.shape, bf16), pltpu.SemaphoreType.DMA((seqs,))],
        stored=tuple(range(seqs)),
        direct=(1,),
    )


def window(meta, block, blocks):
    first, last = meta[2 + block], meta[2 + blocks + block]
    low, high = jnp.int32(blocks), jnp.int32(0)
    for j in range(blocks):
        hit = (meta[2 + blocks + j] >= first) & (meta[2 + j] <= last)
        low = jnp.where(hit & (low == blocks), j, low)
        high = jnp.where(hit, j + 1, high)
    return low, high - low


def set_bias(bias, seg_col, seg_row, block, low, count):
    keys = jnp.concatenate([seg_row[pl.ds(low + j, 1), :] for j in range(count)], axis=1)
    bias[:, : count * BLOCK] = jnp.where(seg_col[rows_at(block), :] == keys, 0.0, masked)


def project_kernel(shard, meta, entered, cond, gain, w1, h0, n1, qkv, inv, store):
    blocks = entered.shape[0] // BLOCK
    for block in range(blocks):
        rows = slice(block * BLOCK, (block + 1) * BLOCK)
        h = entered[rows, :] + cond[...]
        unit, scale = norm_parts(h)
        if block < blocks // 2:
            h0[rows, :] = h
        normed = (unit * gain[...]).astype(bf16)
        n1[rows, :] = normed
        inv[rows, LANES - 1 :] = scale
        terms = dot(normed, w1[:, : 3 * shard], 1, 0)
        qkv[rows_at(exchanged(meta[0], block, blocks)), :] = terms.astype(bf16)
        if block < blocks // 2:
            store(0, rows)
        store(1, rows)


def projected(meta, entered, cond, gain, w1, shard, after):
    seq_len, width = entered.shape
    return call(
        functools.partial(project_kernel, shard),
        "project",
        18,
        6 * seq_len * width * shard,
        (
            like((seq_len // 2, width), f32),
            like((seq_len, width), bf16),
            like((seq_len, 3 * shard), bf16),
            like((seq_len, LANES), f32),
        ),
        (meta, entered, cond, gain, w1),
        after=after,
        stored=(0, 1),
    )


def attend_kernel(shard, scale, meta, qkv, inv, seg_col, seg_row, a, lse, bias):
    seq_len = qkv.shape[0]
    blocks = seq_len // BLOCK
    lse[:, LANES - 1 :] = inv[:, LANES - 1 :]
    even = lax.broadcasted_iota(jnp.int32, (BLOCK, LANES), 1) < LANES // 2

    def attend(block, _):
        own = rows_at(exchanged(meta[0], block, blocks))
        low, count = window(meta, block, blocks)
        for size in range(1, blocks + 1):

            @pl.when(count == size)
            def _(size=size):
                span = size * BLOCK
                keys = pl.ds(pl.multiple_of(low * BLOCK, BLOCK), span)
                set_bias(bias, seg_col, seg_row, block, low, size)
                for pair in range(shard // LANES):
                    at = pair * LANES
                    query = qkv[rows_at(block), at : at + LANES] * jnp.bfloat16(scale)
                    key = qkv[keys, shard + at : shard + at + LANES]
                    value = qkv[keys, 2 * shard + at : 2 * shard + at + LANES]
                    outs = []
                    for e in range(2):
                        picked = jnp.where(even == (e == 0), query, jnp.bfloat16(0))
                        scores = dot(picked, key, 1, 1) + bias[:, :span]
                        top = jnp.max(scores, axis=1, keepdims=True)
                        expo = jnp.exp(scores - top)
                        denom = jnp.sum(expo, axis=1, keepdims=True)
                        outs.append(dot(expo.astype(bf16), value, 1, 0) * (1.0 / denom))
                        head = 2 * pair + e
                        lse[rows_at(block), head : head + 1] = top + jnp.log(denom)
                    a[own, at : at + LANES] = jnp.where(even, outs[0], outs[1]).astype(bf16)

        return 0

    lax.fori_loop(0, blocks, attend, 0)


def attended(meta, qkv, inv, seg_col, seg_row, shard, scale, after):
    seq_len = qkv.shape[0]
    return call(
        functools.partial(attend_kernel, shard, scale),
        "attend",
        10,
        8 * seq_len * seq_len * shard,
        (like((seq_len, shard), bf16), like((seq_len, LANES), f32)),
        (meta, qkv, inv, seg_col, seg_row),
        [pltpu.VMEM((BLOCK, seq_len), f32)],
        after,
    )


def out_kernel(meta, count, *refs):
    mixed, weights, keep, send = refs[:count], refs[count : 2 * count], refs[-2], refs[-1]
    half = keep.shape[0]
    for at in range(0, half, BLOCK):
        for base, out in ((half, send), (0, keep)):
            term = 0.0
            for a, w in zip(mixed, weights, strict=True):
                term = term + dot(a[base + at : base + at + BLOCK, :], w[...], 1, 1)
            out[at : at + BLOCK, :] = term.astype(out.dtype)


def projected_out(meta, mixed, weights, after):
    seq_len, shard = mixed[0].shape
    width = weights[0].shape[0]
    return call(
        lambda m, *refs: out_kernel(m, len(mixed), *refs),
        "project_out",
        7,
        2 * seq_len * width * shard * len(mixed),
        (like((seq_len // 2, width), bf16),) * 2,
        (meta, *mixed, *weights),
        after=after,
    )


def middle_kernel(meta, h0, keep, got, gain, h1, n2, inv, store):
    for at in range(0, keep.shape[0], BLOCK):
        rows = slice(at, at + BLOCK)
        h = h0[rows, :] + (keep[rows, :].astype(f32) + got[rows, :].astype(f32))
        unit, scale = norm_parts(h)
        inv[rows, :1] = scale
        h1[rows, :] = h
        n2[rows, :] = (unit * gain[...]).astype(bf16)
    store(0)


def middle(meta, h0, keep, got, gain, after):
    return call(
        middle_kernel,
        "middle",
        10,
        20 * keep.size,
        (like(keep.shape, f32), like(keep.shape, bf16), like((keep.shape[0], LANES), f32)),
        (meta, h0, keep, got, gain),
        after=after,
        stored=(0,),
    )


def split_features(core, term, keep, send):
    groups, _, part = keep.shape
    for g in range(groups):
        first = term[:, 2 * g * part : (2 * g + 1) * part]
        second = term[:, (2 * g + 1) * part : (2 * g + 2) * part]
        keep[g] = jnp.where(core == 0, first, second)
        send[g] = jnp.where(core == 0, second, first)


def halves_of(meta, half):
    own = pl.multiple_of(meta[0] * half, BLOCK)
    other = pl.multiple_of((1 - meta[0]) * half, BLOCK)
    return ((half, other), (0, own))


def hidden_start(meta, n2_own, n2_other, cot, w2, d_keep, d_send, act, d_hid):
    hid = w2.shape[1] // 2
    half = n2_own.shape[0]
    chunk = min(1024, hid)
    for (first, base), n2, d_n2 in zip(
        halves_of(meta, half), (n2_other, n2_own), (d_send, d_keep), strict=True
    ):
        for at in range(0, half, BLOCK):
            rows = slice(at, at + BLOCK)
            mine = slice(first + at, first + at + BLOCK)
            d_out = cot[pl.ds(base + at, BLOCK), :]
            for col in range(0, hid, chunk):
                u = dot(n2[rows, :], w2[:, col : col + chunk], 1, 0)
                d_act = dot(d_out, w2[:, hid + col : hid + col + chunk], 1, 0)
                cdf = 0.5 + 0.5 * lax.erf(u * (0.5**0.5))
                act[mine, col : col + chunk] = (u * cdf).astype(bf16)
                slope = cdf + u * (jnp.exp(-0.5 * u * u) * (0.5 / math.pi) ** 0.5)
                d_hid[mine, col : col + chunk] = (d_act * slope).astype(bf16)
            d_n2[rows, :] = dot(d_hid[mine, :], w2[:, :hid], 1, 1).astype(bf16)


def hidden_end(
    meta, n2_own, n2_other, cot, w2, h1, act, d_hid, grad, keep, send, held, sems, store, outs
):
    ready = load([h1], [held], sems)
    hid = w2.shape[1] // 2
    half, width = n2_own.shape
    chips = keep.shape[0]
    (_, other), (_, own) = halves_of(meta, half)
    for first in (half, 0):
        if first == 0:
            ready()
        for at in range(0, half, BLOCK):
            mine = slice(first + at, first + at + BLOCK)
            term = dot(act[mine, :], w2[:, hid:], 1, 1)
            if first == 0:
                term = term + held[mine, :] * (1.0 / chips)
            split_features(meta[0], term.astype(bf16), keep.at[:, mine, :], send.at[:, mine, :])
    store(outs + 1)
    store(outs + 2)
    for at in range(0, width, BLOCK):
        cols = slice(at, at + BLOCK)
        up = dot(n2_own[:, cols], d_hid[:half, :], 0, 0)
        up = up + dot(n2_other[:, cols], d_hid[half:, :], 0, 0)
        grad[cols, :hid] = up.astype(bf16)
        down = dot(cot[pl.ds(own, half), cols], act[:half, :], 0, 0)
        down = down + dot(cot[pl.ds(other, half), cols], act[half:, :], 0, 0)
        grad[cols, hid:] = down.astype(bf16)
        store(outs, cols)


def hidden_layer(meta, n2, cot, w2, h1, chips, after, part=None):
    half, width = n2[0].shape
    hid = w2.shape[1] // 2
    split = like((chips, 2 * half, width // (2 * chips)), bf16)
    d_n2 = like((half, width), bf16)
    kept = like((2 * half, hid), bf16)
    late = (like((width, 2 * hid), bf16), split, split)
    if part is None:

        def kernel(meta, own, other, cot, w2, h1, *refs, store):
            (d_keep, d_send, *ends), act, d_hid, held, sems = refs[:5], *refs[5:]
            hidden_start(meta, own, other, cot, w2, d_keep, d_send, act, d_hid)
            hidden_end(
                meta, own, other, cot, w2, h1, act, d_hid, *ends, held, sems, store, 2
            )

        scratch = [*(pltpu.VMEM(kept.shape, bf16) for _ in range(2)), *held_like([h1])]
        return call(
            kernel,
            "hidden_layer",
            28,
            24 * half * width * hid,
            (d_n2, d_n2, *late),
            (meta, *n2, cot, w2, h1),
            scratch,
            after,
            (2, 3, 4),
            (5,),
        )
    if part == ():
        return call(
            hidden_start,
            "hidden_start",
            20,
            12 * half * width * hid,
            (d_n2, d_n2, kept, kept),
            (meta, *n2, cot, w2),
            after=after,
        )
    return call(
        lambda *refs, store: hidden_end(*refs, store, 0),
        "hidden_end",
        28,
        12 * half * width * hid,
        late,
        (meta, *n2, cot, w2, h1, *part),
        held_like([h1]),
        after,
        (0, 1, 2),
        (5,),
    )


def middle_back_kernel(meta, low, got, n2, inv1, cot, gain, d_low, sums):
    half = n2.shape[0]
    base = pl.multiple_of(meta[0] * half, BLOCK)
    ungain = 1.0 / gain[...]
    total = jnp.zeros(sums.shape, f32)
    for at in range(0, half, BLOCK):
        rows = slice(at, at + BLOCK)
        d_n2 = low[rows, :].astype(f32) + got[rows, :].astype(f32)
        unit = n2[rows, :].astype(f32) * ungain
        total = total + jnp.sum(d_n2 * unit, axis=0, keepdims=True)
        d_h = norm_back(unit, inv1[rows, :1], gain[...], d_n2)
        d_h = d_h + cot[pl.ds(base + at, BLOCK), :].astype(f32)
        d_low[rows, :] = d_h.astype(bf16)
    sums[...] = total


def middle_back(meta, low, got, n2, inv1, cot, gain, after):
    return call(
        middle_back_kernel,
        "middle_back",
        12,
        30 * n2.size,
        (like(n2.shape, bf16), like((1, n2.shape[1]), f32)),
        (meta, low, got, n2, inv1, cot, gain),
        after=after,
    )


def attend_back_kernel(
    shard,
    scale,
    seq,
    seqs,
    n_seqs,
    meta,
    low_own,
    low_other,
    w1,
    qkv,
    a,
    lse,
    seg_col,
    seg_row,
    n1,
    gain,
    gain_sum,
    grads,
    keep,
    send,
    d_mix,
    total,
    bias,
    d_qkv,
    *loads,
    store,
):
    ready = load((qkv, lse, n1), loads[:-1], loads[-1])
    qkv, lse, n1 = loads[:-1]
    seq_len = a.shape[0]
    blocks = seq_len // BLOCK
    per = blocks // 2
    for block in range(per):
        w_out_t = w1[:, 3 * shard : 4 * shard]
        rows = slice(block * BLOCK, (block + 1) * BLOCK)
        d_mix[rows, :] = dot(low_own[rows, :], w_out_t, 1, 0).astype(bf16)
        after = slice((block + per) * BLOCK, (block + per + 1) * BLOCK)
        d_mix[after, :] = dot(low_other[rows, :], w_out_t, 1, 0).astype(bf16)
    ready()
    ready()
    total[...] = jnp.zeros(total.shape, f32)
    even = lax.broadcasted_iota(jnp.int32, (BLOCK, LANES), 1) < LANES // 2

    def attend(block, _):
        own = rows_at(exchanged(meta[0], block, blocks))
        low, count = window(meta, block, blocks)
        for size in range(1, blocks + 1):

            @pl.when(count == size)
            def _(size=size):
                span = size * BLOCK
                keys = pl.ds(pl.multiple_of(low * BLOCK, BLOCK), span)
                set_bias(bias, seg_col, seg_row, block, low, size)
                for pair in range(shard // LANES):
                    at = pair * LANES
                    query = qkv[rows_at(block), at : at + LANES] * jnp.bfloat16(scale)
                    key = qkv[keys, shard + at : shard + at + LANES]
                    value = qkv[keys, 2 * shard + at : 2 * shard + at + LANES]
                    grad = d_mix[own, at : at + LANES]
                    product = grad.astype(f32) * a[own, at : at + LANES].astype(f32)
                    d_query = []
                    d_key = d_value = 0.0
                    for e in range(2):
                        side = even == (e == 0)
                        picked = jnp.where(side, query, jnp.bfloat16(0))
                        picked_grad = jnp.where(side, grad, jnp.bfloat16(0))
                        delta = jnp.sum(jnp.where(side, product, 0.0), axis=1, keepdims=True)
                        head = 2 * pair + e
                        scores = dot(picked, key, 1, 1) + bias[:, :span]
                        probs = jnp.exp(scores - lse[rows_at(block), head : head + 1])
                        d_probs = dot(picked_grad, value, 1, 1)
                        d_scores = (probs * (d_probs - delta)).astype(bf16)
                        d_query.append(dot(d_scores, key, 1, 0))
                        d_key = d_key + dot(d_scores, picked, 0, 0)
                        d_value = d_value + dot(probs.astype(bf16), picked_grad, 0, 0)
                    total[keys, at : at + LANES] += d_key
                    total[keys, shard + at : shard + at + LANES] += d_value
                    d_qkv[own, at : at + LANES] = (
                        jnp.where(even, d_query[0], d_query[1]) * scale
                    ).astype(bf16)

        return 0

    lax.fori_loop(0, blocks, attend, 0)
    share = 1.0 / keep.shape[0]
    unit_sum = term_sum = jnp.zeros((1, n1.shape[1]), f32)
    ungain = 1.0 / gain[...]
    ready()
    for block in range(blocks):
        rows = slice(block * BLOCK, (block + 1) * BLOCK)
        d_qkv[rows, shard:] = total[rows_at(exchanged(meta[0], block, blocks)), :].astype(bf16)
        d_n1 = dot(d_qkv[rows, :], w1[:, : 3 * shard], 1, 1)
        unit = n1[rows, :].astype(f32) * ungain
        inv = lse[rows, LANES - 1 :]
        unit_sum = unit_sum + jnp.sum(d_n1 * unit, axis=0, keepdims=True)
        term = norm_back(unit, inv, gain[...], d_n1)
        if block < per:
            term = term + share * low_own[rows, :].astype(f32)
        term_sum = term_sum + jnp.sum(term, axis=0, keepdims=True)
        split_features(meta[0], term.astype(bf16), keep.at[:, rows, :], send.at[:, rows, :])
    row = lax.broadcasted_iota(jnp.int32, (LANES, n1.shape[1]), 0)
    table = jnp.where(row == meta[1] * seqs + seq, term_sum, 0.0)
    table = jnp.where(row == n_seqs, unit_sum, table)
    table = jnp.where(row == n_seqs + 1, gain_sum[...], table)
    grads[:, 4 * shard :] = table.T.astype(bf16)
    store(1)
    store(2)
    half = low_own.shape[0]
    for at in range(0, n1.shape[1], BLOCK):
        cols = slice(at, at + BLOCK)
        grads[cols, : 3 * shard] = dot(n1[:, cols], d_qkv[...], 0, 0).astype(bf16)
        proj = dot(low_own[:, cols], a[:half, :], 0, 0)
        proj = proj + dot(low_other[:, cols], a[half:, :], 0, 0)
        grads[cols, 3 * shard : 4 * shard] = proj.astype(bf16)
        store(0, cols)


def attended_back(
    meta, low, w1, kept, seg_col, seg_row, n1, gain, gain_sum, scale, groups, place, after
):
    qkv, a, lse = kept
    seq_len, shard = a.shape
    width = w1.shape[0]
    split = like((groups, seq_len, width // (2 * groups)), bf16)
    return call(
        functools.partial(attend_back_kernel, shard, scale, *place),
        "attend_back",
        36,
        16 * seq_len * width * shard + 20 * seq_len * seq_len * shard,
        (like((width, 4 * shard + LANES), bf16), split, split),
        (meta, *low, w1, qkv, a, lse, seg_col, seg_row, n1, gain, gain_sum),
        [
            pltpu.VMEM((seq_len, shard), bf16),
            pltpu.VMEM((seq_len, 2 * shard), f32),
            pltpu.VMEM((BLOCK, seq_len), f32),
            pltpu.VMEM((seq_len, 3 * shard), bf16),
            *held_like((qkv, lse, n1)),
        ],
        after,
        (0, 1, 2),
        (4, 6, 9),
    )


def assemble_kernel(spots, *refs):
    come, full, sems = refs[:-2], refs[-2], refs[-1]
    copies = []
    for k, ref in enumerate(come):
        rows = ref.shape[0]
        at = pl.ds(pl.multiple_of(spots[k], rows), rows)
        copies.append(pltpu.make_async_copy(ref, full.at[at, :], sems.at[k]))
    for copy in copies:
        copy.start()
    for copy in copies:
        copy.wait()


def assembled(spots, come):
    rows, cols = sum(c.shape[0] for c in come), come[0].shape[1]
    return pl.pallas_call(
        assemble_kernel,
        out_shape=like((rows, cols), come[0].dtype),
        in_specs=[SMEM] + [HBM] * len(come),
        out_specs=ANY,
        scratch_shapes=[pltpu.SemaphoreType.DMA((len(come),))],
        compiler_params=params(2),
        cost_estimate=pl.CostEstimate(
            flops=0, bytes_accessed=rows * cols // 16, transcendentals=0
        ),
        name="assemble",
    )(spots, *(pltpu.with_memory_space_constraint(c, pltpu.HBM) for c in come))


def pack_kernel(seqs, times, *refs):
    given, first, second, held, sems = refs[:6], refs[6], refs[7], refs[8:-1], refs[-1]
    copies = [
        pltpu.make_async_copy(ref, mine, sems.at[k])
        for k, (ref, mine) in enumerate(zip(given, held, strict=True))
    ]
    for copy in copies:
        copy.start()
    for copy in copies:
        copy.wait()
    w_qkv, w_out, w_time, w_up, w_down, gains = held
    shard = w_qkv.shape[2]
    rows = first.shape[0]
    for c in range(3):
        first[:, c * shard : (c + 1) * shard] = w_qkv[c]
    at = 3 * shard
    for block in (w_out, w_time):
        first[:, at : at + block.shape[0]] = block[...].astype(f32).T.astype(bf16)
        at += block.shape[0]
    row = lax.broadcasted_iota(jnp.int32, (LANES, rows), 0)
    marks = jnp.zeros((LANES, rows), f32)
    for k in range(2):
        marks = jnp.where(row == k, gains[k : k + 1, :].astype(f32), marks)
    for i in range(seqs):
        for k, part in enumerate((times[i] // 32, lax.rem(times[i], 32))):
            marks = jnp.where(row == 2 + 2 * i + k, part.astype(f32), marks)
    first[:, at:] = marks.T.astype(bf16)
    hid = w_up.shape[1]
    second[:, :hid] = w_up[...]
    second[:, hid:] = w_down[...].astype(f32).T.astype(bf16)


def packed(times, *given):
    w_qkv, w_out, w_time, w_up, _, _ = given
    rows = w_up.shape[0]
    cols = 3 * w_qkv.shape[2] + w_out.shape[0] + w_time.shape[0] + LANES
    return call(
        functools.partial(pack_kernel, times.shape[0]),
        "pack",
        8,
        0,
        (like((rows, cols), bf16), like((rows, 2 * w_up.shape[1]), bf16)),
        (times, *given),
        [*(pltpu.VMEM(g.shape, g.dtype) for g in given), pltpu.SemaphoreType.DMA((len(given),))],
        direct=tuple(range(1, 1 + len(given))),
    )


class Ring:
    def __init__(self, n):
        self.n = n
        me = lax.axis_index("dp")
        spot = jnp.where(me & 1 == 0, me >> 1, n - 1 - (me >> 1))
        order = list(range(0, n, 2)) + list(range(n - 1, 0, -2))
        self.right = [(order[p], order[(p + 1) % n]) for p in range(n)]
        self.left = [(b, a) for a, b in self.right]

        def at(offset):
            there = spot + offset
            there = jnp.where(there >= n, there - n, jnp.where(there < 0, there + n, there))
            return jnp.where(there < n // 2, 2 * there, 2 * (n - 1 - there) + 1)

        self.near = tuple(at(k) for k in range(1 - n // 2, n // 2 + 1))

    def at(self, offset):
        return self.near[offset + self.n // 2 - 1]

    def gather(self, block):
        n, rows = self.n, block.shape[0]
        come, spots = [block], [self.at(0) * rows]
        from_left = from_right = block
        waited = yield ()
        for hop in range(1, n // 2):
            from_left = lax.ppermute(from_left, "dp", self.right)
            from_right = lax.ppermute(from_right, "dp", self.left)
            waited = yield (from_left, from_right), waited
            (from_left, from_right), waited = gate((from_left, from_right), waited)
            come += [from_left, from_right]
            spots += [self.at(-hop) * rows, self.at(hop) * rows]
        come.append(lax.ppermute(from_left[: rows // 2], "dp", self.right))
        come.append(lax.ppermute(from_right[rows // 2 :], "dp", self.left))
        farthest = self.at(n // 2) * rows
        spots += [farthest, farthest + rows // 2]
        yield tuple(come[-2:]), waited
        yield assembled(jnp.stack(spots).astype(jnp.int32), come)

    def scatter(self, terms):
        n, rows = self.n, terms[0].shape[0] // self.n

        def whole(offset, at, size):
            parts = [
                lax.dynamic_slice_in_dim(t, self.at(offset) * rows + at, size, 0) for t in terms
            ]
            return sum(p.astype(f32) for p in parts)

        def part(offset, at=0, size=rows):
            return whole(offset, at, size).astype(bf16)

        def plus(run, offset, at=0, size=rows):
            return (run.astype(f32) + whole(offset, at, size)).astype(bf16)

        half = rows // 2
        right, left = part(n // 2, 0, half), part(n // 2, half, half)
        for hop in range(1, n // 2 + 1):
            right = lax.ppermute(right, "dp", self.right)
            left = lax.ppermute(left, "dp", self.left)
            waited = yield (right, left)
            (right, left), _ = gate((right, left), waited)
            if hop == 1:
                rest = n // 2 - 1
                right = jnp.concatenate([plus(right, rest, 0, half), part(rest, half, half)])
                left = jnp.concatenate([part(-rest, 0, half), plus(left, -rest, half, half)])
            elif hop < n // 2:
                right = plus(right, n // 2 - hop)
                left = plus(left, hop - n // 2)
        yield whole(0, 0, rows) + right.astype(f32) + left.astype(f32)


def butterfly(value, axis, bit, n):
    return lax.ppermute(value, axis, [(i, i ^ bit) for i in range(n)])


def gate(values, waited):
    return lax.optimization_barrier((values, tuple(waited)))


def swap(value, bit, n):
    return lax.ppermute(value, "tensor", [(i, i ^ bit) for i in range(n)])


def to_features(keep, got, n, waited, pieces=1):
    chip = lax.axis_index("tensor") // 2
    half = keep.shape[1] // 2
    (keep, got), _ = gate((keep, got), waited)
    got = jnp.concatenate([got[:, half:], got[:, :half]], axis=1)
    kept, came = keep, [got]
    bit = 1
    while 2 * bit < n:
        value = kept.astype(f32) + jnp.concatenate(came, axis=1).astype(f32)
        value = value.reshape((-1, 2) + keep.shape[1:])
        mine = (chip // bit) % 2
        kept = lax.dynamic_index_in_dim(value, mine, 1, keepdims=False)
        sent = lax.dynamic_index_in_dim(value, 1 - mine, 1, keepdims=False).astype(bf16)
        bit *= 2
        parts = pieces if 2 * bit >= n else 1
        came = [swap(p, bit, n) for p in jnp.split(sent, parts, axis=1)]
    return kept, came


def shards(
    inputs,
    segment_ids,
    doc_offsets,
    time_index,
    w_qkv,
    w_out,
    w_up,
    w_down,
    w_time,
    gain_attn,
    gain_mlp,
    cotangent,
):
    n_dp = lax.axis_size("dp")
    n_tensor = lax.axis_size("tensor")
    me_dp = lax.axis_index("dp")
    core = lax.axis_index("tensor") % 2
    chips = n_tensor // 2
    seqs_dev, seq_len, width = inputs.shape
    half = seq_len // 2
    blocks = seq_len // BLOCK
    shard = width // n_tensor
    scale = (width // HEADS) ** (-0.5)
    hidden_dev = w_up.shape[1]
    rows = width // n_dp
    n_seqs = n_dp * seqs_dev
    ring = Ring(n_dp)
    seqs = range(seqs_dev)

    metas, seg_cols, seg_rows, places = [], [], [], []
    for i in seqs:
        ids = segment_ids[i]
        metas.append(
            jnp.concatenate(
                [
                    jnp.stack([core, me_dp]).astype(jnp.int32),
                    ids[::BLOCK],
                    ids[BLOCK - 1 :: BLOCK],
                ]
            )
        )
        seg_cols.append(ids[:, None])
        seg_rows.append(ids.reshape(blocks, BLOCK))
        places.append(positions(ids, doc_offsets[i]))
    w1_part, w2_part, _ = packed(
        time_index, w_qkv, w_out, w_time, w_up, w_down, jnp.stack([gain_attn, gain_mlp])
    )
    *entered, _ = embedded(metas[0], inputs, jnp.stack(places))
    cot = [cotangent[i] for i in seqs]
    gather1 = ring.gather(w1_part)
    next(gather1)
    brought, passed = [gather1.send(())[0]], []
    beside = [(*seg_cols, *seg_rows, *cot, *ring.near, *metas), tuple(entered)]
    while not isinstance(w1 := gather1.send(beside.pop(0) if beside else ()), jax.Array):
        brought.append(w1[0])
        passed.append(w1[1])
    early, entered = passed[:2]
    seg_cols, seg_rows, cot = (early[k * seqs_dev : (k + 1) * seqs_dev] for k in range(3))
    ring.near = early[3 * seqs_dev : -seqs_dev]
    metas = early[-seqs_dev:]
    w2_part, _ = gate(w2_part, brought[-2][:1])
    gather2 = ring.gather(w2_part)
    next(gather2)
    brought2 = [gather2.send(())[0]]
    small = w1[:, 4 * shard :]
    temb = sinusoid(time_index.astype(f32), TEMB)
    cond = jnp.sum(temb[:, None, :] * small[None, :, :TEMB].astype(f32), axis=2)
    attn_g = small[:, TEMB].astype(f32)[None]
    mlp_g = small[:, TEMB + 1].astype(f32)[None]
    def exchange_core(value):
        return swap(value, 1, n_tensor)

    def gather_chips(value):
        values = [value]
        bit = 2
        while bit < n_tensor:
            values = values + [swap(v, bit, n_tensor) for v in values]
            bit *= 2
        return values

    def sum_chips(value):
        bit = 2
        low, got = value.astype(bf16), jnp.zeros_like(value, bf16)
        while bit < n_tensor:
            low = (low.astype(f32) + got.astype(f32)).astype(bf16)
            got = swap(low, bit, n_tensor)
            bit *= 2
        return low, got

    h0, n1, kept, h1, inv1, n2 = [], [], [], [], [], []
    w_outs = gather_chips(w1[:, 3 * shard : 4 * shard])
    while not isinstance(w2 := gather2.send(()), jax.Array):
        brought2.append(w2[0])
    brought2 = brought2[-4:]
    after = ()
    for i in seqs:
        h, n, qkv, inv, token = projected(
            metas[i], entered[i], cond[i : i + 1], attn_g, w1, shard, after
        )
        a, lse, token = attended(
            metas[i],
            qkv,
            inv,
            seg_cols[i],
            seg_rows[i],
            shard,
            scale,
            (token, *(brought2[i] if i < 2 else ())),
        )
        after = (token, *w_outs[1:])
        h0.append(h)
        n1.append(n)
        kept.append((qkv, a, lse))
    mixes = [gather_chips(k[1]) for k in kept]
    outs, terms, d_n2, grad2, downs = [], [], [], [], []
    share = 1.0 / chips
    final = seqs_dev - 1

    def out_of(i, after):
        keep, send, token = projected_out(metas[i], mixes[i], w_outs, after)
        outs.append((keep, exchange_core(send)))
        return token

    def middle_of(i, after):
        h, own, inv, token = middle(metas[i], h0[i], *outs[i], mlp_g, after)
        inv1.append(inv)
        h1.append(h)
        n2.append((own, exchange_core(own)))
        return token

    def hidden_of(i, after):
        given = (metas[i], n2[i], cot[i], w2, h1[i], chips)
        if i < final:
            d_keep, d_send, *rest, token = hidden_layer(*given, after, ())
        else:
            d_keep, d_send, *rest, token = hidden_layer(*given, after)
        terms.append((d_keep, exchange_core(d_send)))
        return token, rest

    def rest_of(i, rest, after):
        token = after[0]
        if i < final:
            *rest, token = hidden_layer(
                metas[i], n2[i], cot[i], w2, h1[i], chips, after, tuple(rest)
            )
        grad, keep, send = rest
        grad2.append(grad)
        downs.append((keep, exchange_core(send)))
        return token

    def sum_of(i, after):
        (keep, got), _ = gate(terms[i], after)
        d_n2.append(sum_chips(keep.astype(f32) + got.astype(f32)))
        return d_n2[i][0]

    for i in seqs:
        token = out_of(i, (token, *(brought2[2] if i == 0 else ())))
    for i in seqs:
        token = middle_of(i, (token, *(brought2[3] if i == 0 else ())))
    for i in seqs:
        token, rest = hidden_of(i, (token,))
        if i < final:
            token = sum_of(i, (token,))
        token = rest_of(i, rest, (token,))
    grad2, _ = gate(grad2, (got for _, got in d_n2))
    sum2 = ring.scatter(grad2)
    hops2 = next(sum2)
    gain_sums, to_inputs, lows = [], [], []

    def middle_back_of(i, after):
        low, gain_sum, token = middle_back(
            metas[i], *d_n2[i], n2[i][0], inv1[i], cot[i], mlp_g, after
        )
        lows.append((low, exchange_core(low)))
        gain_sums.append(gain_sum * share)
        return token

    token = middle_back_of(0, (token,))
    if final:
        token = sum_of(final, (token,))
    grad1 = []
    for i in seqs:
        grad, keep, send, token = attended_back(
            metas[i],
            lows[i],
            w1,
            kept[i],
            seg_cols[i],
            seg_rows[i],
            n1[i],
            attn_g,
            gain_sums[i],
            scale,
            chips,
            (i, seqs_dev, n_seqs),
            (token,),
        )
        grad1.append(grad)
        to_inputs.append((keep, exchange_core(send)))
        hops2 = sum2.send((token,))
        if i < final:
            token = middle_back_of(i + 1, (token,))
            block_out = [to_features(*pair, n_tensor, (token,)) for pair in downs]
    side = [to_features(*pair, n_tensor, (token,), 2) for pair in to_inputs]
    grad1, _ = gate(grad1, (got for _, came in block_out for got in came))
    sum1 = ring.scatter(grad1)
    hops1 = next(sum1)
    came = side[final][1]
    sent = [got for _, came in side for got in came]
    window = 0
    while not isinstance(hops1, jax.Array):
        latest = hops1
        hops1 = sum1.send((sent.pop(0),) if len(sent) > len(came) else ())
        window += 1
        if window == 1:
            block_out, _ = gate(block_out, latest)
        if window in (2, 3) and not isinstance(hops2, jax.Array):
            hops2 = sum2.send(latest)
        if window == 3:
            side[0], _ = gate(side[0], latest)
    while not isinstance(hops2, jax.Array):
        hops2 = sum2.send(())
    share1, share2 = hops1, hops2
    sums = share1[:, 4 * shard :]
    bit = 1
    while bit < n_tensor:
        sums = sums + butterfly(sums, "tensor", bit, n_tensor)
        bit *= 2
    small, _ = gate(small, (token,))
    marks = small[::rows, TEMB + 2 : TEMB + 2 + 2 * seqs_dev].astype(f32)
    times = (marks[:, 0::2] * 32 + marks[:, 1::2]).reshape(n_seqs)
    block_out, input_grad = (
        [kept + jnp.concatenate(came, axis=1).astype(f32) for kept, came in pairs]
        for pairs in (block_out, side)
    )
    block_out = jnp.concatenate(block_out).astype(bf16)
    input_grad = jnp.concatenate(input_grad)
    factor = float(n_seqs * seq_len) ** (-0.5)
    temb_all = sinusoid(times, TEMB)
    grad_time = (
        jnp.einsum("st,ds->td", temb_all, sums[:, :n_seqs], precision=lax.Precision.HIGHEST)
        * factor
    )

    def natural(value):
        return jnp.roll(value, core * half, axis=1)

    cols = 3 * shard
    return (
        natural(block_out),
        natural(input_grad),
        jnp.stack([share1[:, c * shard : (c + 1) * shard] for c in range(3)]) * factor,
        share1[:, cols : cols + shard].T * factor,
        share2[:, :hidden_dev] * factor,
        share2[:, hidden_dev:].T * factor,
        grad_time,
        sums[:, n_seqs] * factor,
        sums[:, n_seqs + 1] * factor,
    )


def solution(mesh):
    in_specs = (
        P("dp", None, None),
        P("dp", None),
        P("dp", None),
        P("dp"),
        P(None, "dp", "tensor"),
        P("tensor", "dp"),
        P("dp", "tensor"),
        P("tensor", "dp"),
        P(None, "dp"),
        P("dp"),
        P("dp"),
        P("dp", None, None),
    )
    out_specs = (
        P("dp", None, "tensor"),
        P("dp", None, "tensor"),
        P(None, "dp", "tensor"),
        P("tensor", "dp"),
        P("dp", "tensor"),
        P("tensor", "dp"),
        P(None, "dp"),
        P("dp"),
        P("dp"),
    )
    return jax.shard_map(shards, mesh=mesh, in_specs=in_specs, out_specs=out_specs, check_vma=False)
```
